32 devices in a mesh: pre: 2 (over x), mdl: 4 (over y, core), dec: 4 (over z).
Axes of the slice: x: 2, y: 2, z: 4, core: 2. Of those that a mesh axis runs over, the one named last changes fastest.
Arguments:
- tokens: bfloat16 [2, 4, 256, 3072], P('pre', 'dec', None, 'mdl'), may hold values from -6 to 6
- norm_gain: bfloat16 [3072], replicated, may hold values from 0.099609375 to 1.8984375
- w_qkv: bfloat16 [3072, 3, 3072], P(('pre', 'dec'), None, 'mdl'), may hold values from -0.109375 to 0.109375
- w_out: bfloat16 [3072, 3072], P(('pre', 'dec'), 'mdl'), may hold values from -0.109375 to 0.109375
- sink_cache: bfloat16 [2, 4, 6144], P(None, None, 'mdl'), may hold values from -10 to 10
- cache_a: bfloat16 [2, 4, 1024, 6144], P(None, 'dec', 'pre', 'mdl'), may hold values from -110 to 110, as said below
- cache_b: bfloat16 [2, 4, 1024, 6144], P(None, 'dec', 'pre', 'mdl'), may hold values from -6 to 6
- lengths: int32 [2, 4], replicated, may hold values from 4 to 2047, as said below
- groups: int32 [2, 4], replicated, may hold values from 0 to 1
Outputs:
- attn_out: bfloat16 [2, 4, 256, 3072], P('pre', 'dec', None, 'mdl')
- decode_a: bfloat16 [2, 4, 1024, 6144], P('pre', 'dec', None, 'mdl')
- decode_b: bfloat16 [2, 4, 1024, 6144], P('pre', 'dec', None, 'mdl')
The draws below stay inside these ranges and needn't reach their ends.
Inputs may be any that keep to these rules, and one draw needn't show every extreme that they name: `lengths`: each request's prior length is 4 or more; some request has exactly the largest and some exactly the smallest allowed length. `cache_a`: keys and values of this layer's window.
All inputs are finite; a program needn't handle non-finite values.
Results may differ from the reference program's by a relative error of at most 0.006.
The reference program's roundings to bfloat16 on the way (of `normed`, `probability` and `attended`) count: a program that leaves them out, or rounds other values in their place, can miss the bound.
Values may be sent and summed in bfloat16 or wider, within the bound.
No kernel may reach another device: no remote copies, remote signals or barrier semaphores. Data moves between devices by JAX's collectives and lax.ppermute only.
A program may use at most 128 MiB of HBM per device.

```python
import jax
import jax.numpy as jnp
from jax import lax

D = 3072
H = 32
HD = 96
FRESH = 256
WINDOW = 1024
SINKS = 4
GROUPS = 2
RPRE = 2
RDEC = 4
HHD = 3072


def draw_cache_a(key, part):
    full_shape = (RPRE, RDEC, WINDOW, H, 2, HD)
    values_drawn = jnp.clip(jax.random.normal(key, full_shape, jnp.float32), -6.0, 6.0)
    return values_drawn.reshape(RPRE, RDEC, WINDOW, 2 * H * HD).astype(jnp.bfloat16)


def draw_lengths(key, part):
    count = RPRE * RDEC
    first_key, second_key = jax.random.split(jax.random.fold_in(key, 7))
    drawn = jax.random.randint(first_key, (count,), SINKS, 2 * WINDOW)
    chosen = jax.random.randint(second_key, (), 0, count)
    places = jnp.arange(count)
    drawn = jnp.where(places == chosen, 2 * WINDOW - 1, drawn)
    drawn = jnp.where(places == (chosen + 1) % count, SINKS, drawn)
    return drawn.reshape(RPRE, RDEC).astype(jnp.int32)


def touch_ends(values, stream_key, smallest, largest):
    longest = values.shape.index(max(values.shape))
    spots = []
    for shift in (0, 1):
        where = [jax.random.randint(jax.random.fold_in(stream_key, axis), (), 0, length) for axis, length in enumerate(values.shape)]
        where[longest] = (where[longest] + shift) % values.shape[longest]
        spots.append(tuple(where))
    return values.at[spots[0]].set(smallest).at[spots[1]].set(largest)


def shard_levels(own_key, dims, cuts, least, top_value):
    level, own = 1.0, jax.random.fold_in(own_key, 6)
    for position, shards_of in cuts:
        heights = jnp.exp(jax.random.uniform(jax.random.fold_in(own, position), (shards_of,), jnp.float32, least / len(cuts), top_value / len(cuts)))
        level = level * jnp.repeat(heights, dims[position] // shards_of).reshape([-1 if axis == position else 1 for axis in range(len(dims))])
    return level


def centred(own_key, extent, deviation, limit, cuts=(), kind=jnp.bfloat16):
    result = jax.random.normal(own_key, extent, jnp.float32) * deviation
    if len(cuts) > 0:
        result = shard_levels(own_key, extent, cuts, -0.22, 0.18) * result
    return jnp.clip(result, min=-limit, max=limit).astype(kind)


def setup_inputs(seed: int = 0) -> dict:
    arg_keys = jax.random.split(jax.random.key(seed), 10)
    tokens = centred(arg_keys[0], (RPRE, RDEC, FRESH, D), 1.0, 6.0, ((0, 2), (1, 4), (3, 4)))
    norm_gain = jnp.clip(1.0 + 0.18 * jax.random.normal(arg_keys[1], (D,), jnp.float32), 0.099609375, 1.8984375).astype(jnp.bfloat16)
    w_qkv = centred(arg_keys[2], (D, 3, HHD), D ** -0.5, 0.109375, ((0, 8), (2, 4)))
    w_out = centred(arg_keys[3], (HHD, D), HHD ** -0.5, 0.109375, ((0, 8), (1, 4)))
    sink_cache = centred(arg_keys[4], (GROUPS, SINKS, 2 * HHD), 2.5, 10.0, ((2, 4),))
    cache_a = draw_cache_a(jax.random.fold_in(arg_keys[9], 71), 0)
    cache_b = centred(arg_keys[6], (RPRE, RDEC, WINDOW, 2 * HHD), 1.0, 6.0, ((1, 4), (2, 2), (3, 4)))
    lengths = draw_lengths(jax.random.fold_in(arg_keys[9], 71), 0)
    groups = touch_ends(jax.random.randint(arg_keys[8], (RPRE, RDEC), 0, GROUPS), jax.random.fold_in(arg_keys[8], 1), 0, GROUPS - 1).astype(jnp.int32)
    return dict(tokens=tokens, norm_gain=norm_gain, w_qkv=w_qkv, w_out=w_out, sink_cache=sink_cache, cache_a=cache_a, cache_b=cache_b, lengths=lengths, groups=groups)


MASKED_SCORE = -1e+30

def rotate(vector, cosines, sines):
    halfway = vector.shape[-1] // 2
    first_half = vector[..., :halfway]
    second_half = vector[..., halfway:]
    return jnp.concatenate([first_half * cosines - second_half * sines, second_half * cosines + first_half * sines], axis=-1)

def angles(offset, count):
    halfway = HD // 2
    frequency = 10000.0 ** (-(jnp.arange(halfway).astype(jnp.float32) * 2.0) / HD)
    places = offset.astype(jnp.float32) + jnp.arange(count).astype(jnp.float32)
    phases = places[:, None] * frequency[None, :]
    return (jnp.cos(phases)[:, None, :], jnp.sin(phases)[:, None, :])

def reference(tokens, norm_gain, w_qkv, w_out, sink_cache, cache_a, cache_b, lengths, groups):
    row_count = RPRE * RDEC
    flat_tok = tokens.reshape(row_count, FRESH, D)
    flat_cache = cache_a.reshape(row_count, WINDOW, 2 * H * HD)
    flat_len = lengths.reshape(row_count)
    flat_grp = groups.reshape(row_count)
    w_flat = w_qkv.reshape(D, 3 * H * HD)
    score_scale = HD ** (-0.5)

    def per_request(items):
        tok_rows, window_kv, length, group_id = items
        as_float = tok_rows.astype(jnp.float32)
        normed = (as_float * lax.rsqrt(lax.optimization_barrier(jnp.mean(as_float * as_float, axis=-1, keepdims=True)) + 1e-05) * norm_gain.astype(jnp.float32)).astype(jnp.bfloat16)
        projected = jnp.dot(normed, w_flat, preferred_element_type=jnp.float32).reshape(FRESH, 3, H, HD)
        cosines, sines = angles(length, FRESH)
        query = rotate(projected[:, 0], cosines, sines).astype(jnp.bfloat16)
        key_new = rotate(projected[:, 1], cosines, sines).astype(jnp.bfloat16)
        value_new = projected[:, 2].astype(jnp.bfloat16)
        sink_rows = sink_cache[group_id].reshape(SINKS, H, 2, HD)
        window_rows = window_kv.reshape(WINDOW, H, 2, HD)
        all_keys = jnp.concatenate([sink_rows[:, :, 0], window_rows[:, :, 0], key_new], axis=0)
        all_values = jnp.concatenate([sink_rows[:, :, 1], window_rows[:, :, 1], value_new], axis=0)
        query_pos = jnp.arange(FRESH)[:, None]
        slot_pos = jnp.arange(WINDOW)[None, :]
        window_ok = (slot_pos >= query_pos + 1) & (slot_pos >= SINKS + WINDOW - length)
        sink_ok = jnp.ones((FRESH, SINKS), dtype=bool)
        recent_ok = jnp.arange(FRESH)[None, :] <= query_pos
        key_mask = jnp.concatenate([sink_ok, window_ok, recent_ok], axis=1)[None]
        scores = jnp.einsum('qhd,khd->hqk', query.astype(jnp.float32), all_keys.astype(jnp.float32)) * score_scale
        scores = jnp.where(key_mask, scores, MASKED_SCORE)
        row_top = lax.optimization_barrier(jnp.max(scores, axis=-1, keepdims=True))
        probability = jnp.where(key_mask, jnp.exp(scores - row_top), 0.0)
        row_total = lax.optimization_barrier(jnp.sum(probability, axis=-1))
        rounded = lax.optimization_barrier(probability.astype(jnp.bfloat16)).astype(jnp.float32)
        mixed = jnp.einsum('hqk,khd->qhd', rounded, all_values.astype(jnp.float32))
        attended = (mixed / jnp.transpose(row_total)[:, :, None]).astype(jnp.bfloat16).reshape(FRESH, H * HD)
        output_rows = jnp.dot(attended, w_out, preferred_element_type=jnp.float32).astype(jnp.bfloat16)
        fresh_kv = jnp.stack([key_new, value_new], axis=2).reshape(FRESH, 2 * H * HD)
        new_window = jnp.concatenate([window_kv[FRESH:], fresh_kv], axis=0)
        return (output_rows, new_window)
    outputs, windows = lax.map(per_request, (flat_tok, flat_cache, flat_len, flat_grp))
    attn_out = outputs.reshape(RPRE, RDEC, FRESH, D)
    decode_a = windows.reshape(RPRE, RDEC, WINDOW, 2 * H * HD)
    return (attn_out, decode_a, cache_b)
```

```python
import functools

import jax
import jax.numpy as jnp
from jax import lax
from jax.experimental import pallas as pl
from jax.experimental.pallas import tpu as pltpu
from jax.sharding import PartitionSpec as P

HD = 96
WINDOW = 1024
SINKS = 4


MASKED_SCORE = -1e30


def rotate(vector, cosines, sines):
    halfway = vector.shape[-1] // 2
    first_half = vector[..., :halfway]
    second_half = vector[..., halfway:]
    return jnp.concatenate(
        [first_half * cosines - second_half * sines, second_half * cosines + first_half * sines],
        axis=-1,
    )


def angles(offsets, count):
    halfway = HD // 2
    frequency = 10000.0 ** (-(jnp.arange(halfway).astype(jnp.float32) * 2.0) / HD)
    places = offsets.astype(jnp.float32)[:, None] + jnp.arange(count).astype(jnp.float32)[None, :]
    phases = places[:, :, None] * frequency[None, None, :]
    return (jnp.cos(phases)[:, :, None, :], jnp.sin(phases)[:, :, None, :])


def window_mask(slot_count, fresh_len, prior):
    slot_pos = jnp.arange(slot_count)[None, None, :]
    query_pos = jnp.arange(fresh_len)[None, :, None]
    return (slot_pos >= query_pos + 1) & (slot_pos >= SINKS + WINDOW - prior[:, None, None])


def masked_scores(query, all_keys, key_mask):
    scores = jnp.einsum(
        "rqhd,rkhd->rhqk", query, all_keys, preferred_element_type=jnp.float32
    ) * HD ** (-0.5)
    return jnp.where(key_mask[:, None], scores, MASKED_SCORE)


def partial_terms(scores, key_mask, all_values, row_top):
    probability = jnp.where(key_mask[:, None], jnp.exp(scores - row_top[..., None]), 0.0)
    denominator = jnp.sum(probability, axis=-1)
    numerator = jnp.einsum(
        "rhqk,rkhd->rqhd",
        probability.astype(jnp.bfloat16),
        all_values,
        preferred_element_type=jnp.float32,
    )
    return (numerator, denominator)


def general_body(tokens, norm_gain, w_qkv, w_out, sink_cache, cache_a, cache_b, lengths, groups):
    req_count = tokens.shape[0]
    fresh_len = tokens.shape[2]
    col_width = cache_a.shape[-1] // 2
    heads_dev = col_width // HD
    row_count = req_count * fresh_len
    pre_at = lax.axis_index("pre") * req_count
    dec_at = lax.axis_index("dec")
    gathered = lax.all_gather(tokens, "mdl", axis=3, tiled=True)
    as_float = gathered.reshape(row_count, -1).astype(jnp.float32)
    normed = (
        as_float
        * lax.rsqrt(jnp.mean(as_float * as_float, axis=-1, keepdims=True) + 1e-05)
        * norm_gain.astype(jnp.float32)
    ).astype(jnp.bfloat16)
    shard_rows = lax.all_gather(w_qkv, ("pre", "dec"), axis=0, tiled=True)
    columns = normed
    projected = jnp.dot(
        columns, shard_rows.reshape(shard_rows.shape[0], -1), preferred_element_type=jnp.float32
    )
    projected = projected.reshape(req_count, fresh_len, 3, heads_dev, HD)
    my_len = lax.dynamic_slice(lengths, (pre_at, dec_at), (req_count, 1))[:, 0]
    my_group = lax.dynamic_slice(groups, (pre_at, dec_at), (req_count, 1))[:, 0]
    cosines, sines = angles(my_len, fresh_len)
    query = rotate(projected[:, :, 0], cosines, sines).astype(jnp.bfloat16)
    key_new = rotate(projected[:, :, 1], cosines, sines).astype(jnp.bfloat16)
    value_new = projected[:, :, 2].astype(jnp.bfloat16)
    onehot = (my_group[:, None] == jnp.arange(sink_cache.shape[0])[None, :]).astype(jnp.float32)
    sink_rows = jnp.einsum("rg,gsc->rsc", onehot, sink_cache.astype(jnp.float32)).astype(
        jnp.bfloat16
    )
    sink_rows = sink_rows.reshape(req_count, SINKS, heads_dev, 2, HD)
    sink_keys = sink_rows[:, :, :, 0]
    sink_values = sink_rows[:, :, :, 1]
    sink_ok = jnp.ones((req_count, fresh_len, SINKS), dtype=bool)
    recent_ok = jnp.arange(fresh_len)[None, None, :] <= jnp.arange(fresh_len)[None, :, None]
    moved_a, moved_b = (
        lax.all_to_all(cache_a, "pre", split_axis=0, concat_axis=2, tiled=True),
        lax.all_to_all(cache_b, "pre", split_axis=0, concat_axis=2, tiled=True),
    )
    full_window = moved_a[:, 0].reshape(req_count, -1, heads_dev, 2, HD)
    window_keys = full_window[:, :, :, 0]
    window_values = full_window[:, :, :, 1]
    all_keys = jnp.concatenate([sink_keys, window_keys, key_new], axis=1)
    all_values = jnp.concatenate([sink_values, window_values, value_new], axis=1)
    far_mask = window_mask(WINDOW, fresh_len, my_len)
    key_mask = jnp.concatenate([sink_ok, far_mask, recent_ok], axis=2)
    scores = masked_scores(query, all_keys, key_mask)
    row_top = jnp.max(scores, axis=-1)
    numerator, denominator = partial_terms(scores, key_mask, all_values, row_top)
    attended = (
        (numerator / jnp.transpose(denominator, (0, 2, 1))[..., None])
        .astype(jnp.bfloat16)
        .reshape(row_count, col_width)
    )
    every_head = lax.all_gather(attended, "mdl", axis=1, tiled=True)
    columns = every_head
    output_rows = jnp.dot(
        columns,
        lax.all_gather(w_out, ("pre", "dec"), axis=0, tiled=True),
        preferred_element_type=jnp.float32,
    )
    attn_out = output_rows.astype(jnp.bfloat16).reshape(req_count, 1, fresh_len, -1)
    fresh_kv = jnp.stack([key_new, value_new], axis=3).reshape(req_count, fresh_len, 2 * col_width)[
        :, None
    ]
    decode_a = jnp.concatenate([moved_a[:, :, fresh_len:], fresh_kv], axis=2)
    return (attn_out, decode_a, moved_b)


VMEM_BYTES = 56 * 1024 * 1024
NT = (((1,), (1,)), ((), ()))


def project_kernel(width, *refs):
    pieces, (own_w, far_w, gain, cosines, sines) = refs[:16], refs[16:21]
    outs, (held, sems) = refs[21:25], refs[25:]
    mdl_at = lax.axis_index("mdl")
    row_at, core_at = mdl_at // 2, mdl_at % 2
    near = jnp.where(row_at == lax.axis_index("pre"), 0, 1)
    first = pltpu.make_async_copy(own_w, held.at[near], sems.at[0])
    second = pltpu.make_async_copy(far_w, held.at[1 - near], sems.at[1])
    first.start()
    second.start()
    first.wait()
    second.wait()
    depth = own_w.shape[2]
    rotated = 2 * width
    lane = lax.broadcasted_iota(jnp.int32, (1, rotated), 1)
    in_first = lane % HD < HD // 2
    for slot in range(4):
        group = pieces[4 * slot : 4 * slot + 4]
        squares = jnp.zeros((group[0].shape[0], 1), jnp.float32)
        for piece in group:
            part = piece[...].astype(jnp.float32)
            squares = squares + jnp.sum(part * part, axis=1, keepdims=True)
        scale = lax.rsqrt(squares / (4 * group[0].shape[1]) + 1e-05)
        total = None
        for which, piece in enumerate(group):
            core = core_at if which < 2 else 1 - core_at
            row = row_at if which in (0, 2) else 1 - row_at
            at = row * 2 + core
            normed = (piece[...].astype(jnp.float32) * scale * gain[at]).astype(jnp.bfloat16)
            for part in range(2):
                term = lax.dot_general(
                    normed[:, part * depth : (part + 1) * depth],
                    held[which % 2, core * 2 + part],
                    NT,
                    preferred_element_type=jnp.float32,
                )
                total = term if total is None else total + term
        turned = total[:, :rotated]
        ahead = pltpu.roll(turned, rotated - HD // 2, 1)
        behind = pltpu.roll(turned, HD // 2, 1)
        turned = turned * cosines[slot] + jnp.where(in_first, ahead, behind) * sines[slot]
        outs[slot][:, :rotated] = turned.astype(jnp.bfloat16)
        outs[slot][:, rotated:] = total[:, rotated:].astype(jnp.bfloat16)


def project(pieces, own_w, far_w, gain, cosines, sines):
    rows, depth = pieces[0].shape
    columns = own_w.shape[1]
    return pl.pallas_call(
        functools.partial(project_kernel, columns // 3),
        out_shape=[jax.ShapeDtypeStruct((rows, columns), jnp.bfloat16)] * 4,
        in_specs=[pl.BlockSpec(memory_space=pltpu.VMEM)] * 16
        + [pl.BlockSpec(memory_space=pl.ANY)] * 2
        + [pl.BlockSpec(memory_space=pltpu.VMEM)] * 3,
        out_specs=[pl.BlockSpec(memory_space=pltpu.VMEM)] * 4,
        scratch_shapes=[
            pltpu.VMEM((2,) + own_w.shape, jnp.bfloat16),
            pltpu.SemaphoreType.DMA((2,)),
        ],
        compiler_params=pltpu.CompilerParams(vmem_limit_bytes=VMEM_BYTES),
        cost_estimate=pl.CostEstimate(
            flops=8 * rows * 4 * depth * columns, bytes_accessed=16_000_000, transcendentals=0
        ),
        name="project",
    )(*pieces, own_w, far_w, gain, cosines, sines)


def attend_kernel(
    prior, y0, y1, y2, y3, own, far, sinks, attended, decode, held, fresh, sems, out_sems
):
    pre_at, dec_at = lax.axis_index("pre"), lax.axis_index("dec")
    copies = [
        pltpu.make_async_copy(source, held.at[lax.rem(dec_at + step, 4)], sems.at[step])
        for step, source in enumerate((y0, y1, y2, y3))
    ]
    for copy in copies:
        copy.start()
    for copy in copies:
        copy.wait()
    rows, half = held.shape[1], own.shape[0]
    span = 2 * HD
    heads = own.shape[1] // span
    local = heads // 4
    for head in range(heads):
        block, at = head // local, (head % local) * HD
        for kind in (1, 2):
            fresh[:, head * span + (kind - 1) * HD : head * span + kind * HD] = held[
                block, :, kind * local * HD + at : kind * local * HD + at + HD
            ]
    tail = pltpu.make_async_copy(fresh, decode.at[pl.ds(2 * half - rows, rows)], out_sems.at[0])
    tail.start()

    def keep(early, late):
        first = pltpu.make_async_copy(
            early.at[pl.ds(rows, half - rows)], decode.at[pl.ds(0, half - rows)], out_sems.at[1]
        )
        second = pltpu.make_async_copy(late, decode.at[pl.ds(half - rows, half)], out_sems.at[2])
        return first, second

    @pl.when(pre_at == 0)
    def _():
        for copy in keep(own, far):
            copy.start()

    @pl.when(pre_at != 0)
    def _():
        for copy in keep(far, own):
            copy.start()

    token = lax.broadcasted_iota(jnp.int32, (rows, 1), 0)
    lowest = jnp.maximum(token + 1, SINKS + 2 * half - prior[0])
    slot = lax.broadcasted_iota(jnp.int32, (1, half), 1)
    own_ok = slot >= lowest - pre_at * half
    far_ok = slot >= lowest - (1 - pre_at) * half
    new_ok = lax.broadcasted_iota(jnp.int32, (1, rows), 1) <= token
    sink_ok = lax.broadcasted_iota(jnp.int32, (1, sinks.shape[0]), 1) < SINKS
    scale = HD ** (-0.5)
    for head in range(heads):
        block, at = head // local, (head % local) * HD
        left = head * span
        query = held[block, :, at : at + HD]
        groups = []
        for keys, values, ok in (
            (own[:, left : left + HD], own[:, left + HD : left + span], own_ok),
            (far[:, left : left + HD], far[:, left + HD : left + span], far_ok),
            (fresh[:, left : left + HD], fresh[:, left + HD : left + span], new_ok),
            (sinks[:, left : left + HD], sinks[:, left + HD : left + span], sink_ok),
        ):
            scores = lax.dot_general(query, keys, NT, preferred_element_type=jnp.float32) * scale
            groups.append((jnp.where(ok, scores, MASKED_SCORE), values))
        top = functools.reduce(
            jnp.maximum, [jnp.max(scores, axis=1, keepdims=True) for scores, _ in groups]
        )
        below, mixed = None, None
        for scores, values in groups:
            probability = jnp.exp(scores - top)
            part = jnp.sum(probability, axis=1, keepdims=True)
            term = jnp.dot(
                probability.astype(jnp.bfloat16), values, preferred_element_type=jnp.float32
            )
            below = part if below is None else below + part
            mixed = term if mixed is None else mixed + term
        attended[:, head * HD : (head + 1) * HD] = (mixed / below).astype(jnp.bfloat16)
    tail.wait()

    @pl.when(pre_at == 0)
    def _():
        for copy in keep(own, far):
            copy.wait()

    @pl.when(pre_at != 0)
    def _():
        for copy in keep(far, own):
            copy.wait()


def attend(prior, parts, own, far, sinks):
    rows, columns = parts[0].shape
    half, width = own.shape
    return pl.pallas_call(
        attend_kernel,
        out_shape=[
            jax.ShapeDtypeStruct((rows, width // 2), jnp.bfloat16),
            jax.ShapeDtypeStruct((2 * half, width), jnp.bfloat16),
        ],
        in_specs=[pl.BlockSpec(memory_space=pltpu.SMEM)]
        + [pl.BlockSpec(memory_space=pl.ANY)] * 4
        + [pl.BlockSpec(memory_space=pltpu.VMEM)] * 3,
        out_specs=[
            pl.BlockSpec(memory_space=pltpu.VMEM),
            pl.BlockSpec(memory_space=pl.ANY),
        ],
        scratch_shapes=[
            pltpu.VMEM((4, rows, columns), jnp.bfloat16),
            pltpu.VMEM((rows, width), jnp.bfloat16),
            pltpu.SemaphoreType.DMA((4,)),
            pltpu.SemaphoreType.DMA((3,)),
        ],
        compiler_params=pltpu.CompilerParams(vmem_limit_bytes=VMEM_BYTES),
        cost_estimate=pl.CostEstimate(
            flops=2 * rows * (2 * half + rows) * width,
            bytes_accessed=10_000_000,
            transcendentals=rows * (2 * half + rows) * width // (2 * HD),
        ),
        name="attend",
    )(prior, *parts, own, far, sinks)


def finish_kernel(a0, a1, a2, a3, weights, out):
    mdl_at = lax.axis_index("mdl")
    row_at, core_at = mdl_at // 2, mdl_at % 2
    depth = a0.shape[1]
    total = None
    for which, piece in enumerate((a0, a1, a2, a3)):
        core = core_at if which < 2 else 1 - core_at
        row = row_at if which in (0, 2) else 1 - row_at
        start = pl.multiple_of((row * 2 + core) * depth, depth)
        term = jnp.dot(
            piece[...], weights[pl.ds(start, depth), :], preferred_element_type=jnp.float32
        )
        total = term if total is None else total + term
    out[...] = total.astype(jnp.bfloat16)


def finish(pieces, weights):
    rows, depth = pieces[0].shape
    return pl.pallas_call(
        finish_kernel,
        out_shape=jax.ShapeDtypeStruct((rows, weights.shape[1]), jnp.bfloat16),
        in_specs=[pl.BlockSpec(memory_space=pltpu.VMEM)] * 5,
        out_specs=pl.BlockSpec(memory_space=pltpu.VMEM),
        compiler_params=pltpu.CompilerParams(vmem_limit_bytes=VMEM_BYTES),
        cost_estimate=pl.CostEstimate(
            flops=8 * rows * depth * weights.shape[1], bytes_accessed=7_000_000, transcendentals=0
        ),
        name="finish",
    )(*pieces, weights)


def join_kernel(own, far, out, sems):
    half = own.shape[0]
    at = lax.axis_index("pre") * half
    first = pltpu.make_async_copy(own, out.at[pl.ds(pl.multiple_of(at, half), half)], sems.at[0])
    second = pltpu.make_async_copy(
        far, out.at[pl.ds(pl.multiple_of(half - at, half), half)], sems.at[1]
    )
    first.start()
    second.start()
    first.wait()
    second.wait()


def join(own, far):
    half, width = own.shape
    return pl.pallas_call(
        join_kernel,
        out_shape=jax.ShapeDtypeStruct((2 * half, width), jnp.bfloat16),
        in_specs=[pl.BlockSpec(memory_space=pl.ANY)] * 2,
        out_specs=pl.BlockSpec(memory_space=pl.ANY),
        scratch_shapes=[pltpu.SemaphoreType.DMA((2,))],
        cost_estimate=pl.CostEstimate(
            flops=0, bytes_accessed=8 * half * width, transcendentals=0
        ),
        name="join",
    )(own, far)


def split_body(sizes, tokens, norm_gain, w_qkv, w_out, sink_cache, cache_a, cache_b, lengths, groups):
    dec = sizes["dec"]
    rows = tokens.shape[2]
    heads_dev = cache_a.shape[-1] // (2 * HD)
    width = heads_dev // dec * HD
    pre_at, dec_at, mdl_at = (lax.axis_index(name) for name in ("pre", "dec", "mdl"))
    swap = [(0, 1), (1, 0)]
    over_y = [(0, 2), (1, 3), (2, 0), (3, 1)]
    over_core = [(0, 1), (1, 0), (2, 3), (3, 2)]

    def along(step):
        return [(at, (at + step) % dec) for at in range(dec)]

    own_tokens = tokens.reshape(rows, -1)
    turned = jnp.transpose(w_qkv, (1, 2, 0)).reshape(3, dec, width, -1)
    turned = jnp.transpose(turned, (1, 0, 2, 3)).reshape(dec, 3 * width, -1)
    own_w = lax.all_to_all(turned, "dec", 0, 0, tiled=True)
    far_w = lax.ppermute(own_w, "pre", swap)

    near = [own_tokens] + [lax.ppermute(own_tokens, "dec", along(step)) for step in (1, 2, 3)]
    across = [lax.ppermute(piece, "mdl", over_y) for piece in near]
    pieces = []
    for one, two in zip(near, across):
        pieces += [one, two, lax.ppermute(one, "mdl", over_core), lax.ppermute(two, "mdl", over_core)]

    own_a, own_b = (
        lax.dynamic_index_in_dim(cache[:, 0], pre_at, 0, keepdims=False) for cache in (cache_a, cache_b)
    )
    far_a, far_b = (
        lax.ppermute(lax.dynamic_index_in_dim(cache[:, 0], 1 - pre_at, 0, keepdims=False), "pre", swap)
        for cache in (cache_a, cache_b)
    )

    slots = (dec_at - jnp.arange(4)) % dec
    lens = lengths[pre_at][slots]
    cosines, sines = angles(lens, rows)
    cosines, sines = cosines[:, :, 0], sines[:, :, 0]
    repeat = 2 * width // HD
    cosines = jnp.tile(jnp.concatenate([cosines, cosines], axis=-1), (1, 1, repeat))
    sines = jnp.tile(jnp.concatenate([-sines, sines], axis=-1), (1, 1, repeat))
    gain = norm_gain.astype(jnp.float32).reshape(sizes["mdl"], 1, -1)
    sinks = jnp.pad(
        lax.dynamic_index_in_dim(sink_cache, groups[pre_at, dec_at], 0, keepdims=False),
        ((0, 16 - SINKS), (0, 0)),
    )
    prior = lengths[pre_at, dec_at].reshape(1)

    found = project(pieces, own_w, far_w, gain, cosines, sines)
    parts = [found[0]] + [
        lax.ppermute(found[step], "dec", along(-step)) for step in (1, 2, 3)
    ]
    attended, decode_a = attend(prior, parts, own_a, far_a, sinks)
    second = lax.ppermute(attended, "mdl", over_y)
    shares = [
        attended,
        second,
        lax.ppermute(attended, "mdl", over_core),
        lax.ppermute(second, "mdl", over_core),
    ]
    every_row = lax.all_gather(w_out, ("pre", "dec"), axis=0, tiled=True)
    attn_out = finish(shares, every_row)
    decode_b = join(own_b, far_b)
    return (attn_out[None, None], decode_a[None, None], decode_b[None, None])


def body(sizes, tokens, norm_gain, w_qkv, w_out, sink_cache, cache_a, cache_b, lengths, groups):
    heads_dev = cache_a.shape[-1] // (2 * HD)
    shapes = (sizes["pre"], sizes["mdl"], sizes["dec"], heads_dev)
    split = shapes == (2, 4, 4, 8) and tokens.shape[0] == 1 and tokens.shape[1] == 1
    args = (tokens, norm_gain, w_qkv, w_out, sink_cache, cache_a, cache_b, lengths, groups)
    return split_body(sizes, *args) if split else general_body(*args)


def solution(mesh):
    placed = (
        P("pre", "dec", None, "mdl"),
        P(),
        P(("pre", "dec"), None, "mdl"),
        P(("pre", "dec"), "mdl"),
        P(None, None, "mdl"),
        P(None, "dec", "pre", "mdl"),
        P(None, "dec", "pre", "mdl"),
        P(),
        P(),
    )
    return jax.shard_map(
        functools.partial(body, dict(mesh.shape)),
        mesh=mesh,
        in_specs=placed,
        out_specs=(
            P("pre", "dec", None, "mdl"),
            P("pre", "dec", None, "mdl"),
            P("pre", "dec", None, "mdl"),
        ),
        check_vma=False,
    )
```

```python
import functools

import jax
import jax.numpy as jnp
from jax import lax
from jax.experimental import pallas as pl
from jax.experimental.pallas import tpu as pltpu
from jax.sharding import PartitionSpec as P

HD = 96
WINDOW = 1024
SINKS = 4


MASKED_SCORE = -1e30


def rotate(vector, cosines, sines):
    halfway = vector.shape[-1] // 2
    first_half = vector[..., :halfway]
    second_half = vector[..., halfway:]
    return jnp.concatenate(
        [first_half * cosines - second_half * sines, second_half * cosines + first_half * sines],
        axis=-1,
    )


def angles(offsets, count):
    halfway = HD // 2
    frequency = 10000.0 ** (-(jnp.arange(halfway).astype(jnp.float32) * 2.0) / HD)
    places = offsets.astype(jnp.float32)[:, None] + jnp.arange(count).astype(jnp.float32)[None, :]
    phases = places[:, :, None] * frequency[None, None, :]
    return (jnp.cos(phases)[:, :, None, :], jnp.sin(phases)[:, :, None, :])


def window_mask(slot_count, fresh_len, prior):
    slot_pos = jnp.arange(slot_count)[None, None, :]
    query_pos = jnp.arange(fresh_len)[None, :, None]
    return (slot_pos >= query_pos + 1) & (slot_pos >= SINKS + WINDOW - prior[:, None, None])


def masked_scores(query, all_keys, key_mask):
    scores = jnp.einsum(
        "rqhd,rkhd->rhqk", query, all_keys, preferred_element_type=jnp.float32
    ) * HD ** (-0.5)
    return jnp.where(key_mask[:, None], scores, MASKED_SCORE)


def partial_terms(scores, key_mask, all_values, row_top):
    probability = jnp.where(key_mask[:, None], jnp.exp(scores - row_top[..., None]), 0.0)
    denominator = jnp.sum(probability, axis=-1)
    numerator = jnp.einsum(
        "rhqk,rkhd->rqhd",
        probability.astype(jnp.bfloat16),
        all_values,
        preferred_element_type=jnp.float32,
    )
    return (numerator, denominator)


def general_body(tokens, norm_gain, w_qkv, w_out, sink_cache, cache_a, cache_b, lengths, groups):
    req_count = tokens.shape[0]
    fresh_len = tokens.shape[2]
    col_width = cache_a.shape[-1] // 2
    heads_dev = col_width // HD
    row_count = req_count * fresh_len
    pre_at = lax.axis_index("pre") * req_count
    dec_at = lax.axis_index("dec")
    gathered = lax.all_gather(tokens, "mdl", axis=3, tiled=True)
    as_float = gathered.reshape(row_count, -1).astype(jnp.float32)
    normed = (
        as_float
        * lax.rsqrt(jnp.mean(as_float * as_float, axis=-1, keepdims=True) + 1e-05)
        * norm_gain.astype(jnp.float32)
    ).astype(jnp.bfloat16)
    shard_rows = lax.all_gather(w_qkv, ("pre", "dec"), axis=0, tiled=True)
    columns = normed
    projected = jnp.dot(
        columns, shard_rows.reshape(shard_rows.shape[0], -1), preferred_element_type=jnp.float32
    )
    projected = projected.reshape(req_count, fresh_len, 3, heads_dev, HD)
    my_len = lax.dynamic_slice(lengths, (pre_at, dec_at), (req_count, 1))[:, 0]
    my_group = lax.dynamic_slice(groups, (pre_at, dec_at), (req_count, 1))[:, 0]
    cosines, sines = angles(my_len, fresh_len)
    query = rotate(projected[:, :, 0], cosines, sines).astype(jnp.bfloat16)
    key_new = rotate(projected[:, :, 1], cosines, sines).astype(jnp.bfloat16)
    value_new = projected[:, :, 2].astype(jnp.bfloat16)
    onehot = (my_group[:, None] == jnp.arange(sink_cache.shape[0])[None, :]).astype(jnp.float32)
    sink_rows = jnp.einsum("rg,gsc->rsc", onehot, sink_cache.astype(jnp.float32)).astype(
        jnp.bfloat16
    )
    sink_rows = sink_rows.reshape(req_count, SINKS, heads_dev, 2, HD)
    sink_keys = sink_rows[:, :, :, 0]
    sink_values = sink_rows[:, :, :, 1]
    sink_ok = jnp.ones((req_count, fresh_len, SINKS), dtype=bool)
    recent_ok = jnp.arange(fresh_len)[None, None, :] <= jnp.arange(fresh_len)[None, :, None]
    moved_a, moved_b = (
        lax.all_to_all(cache_a, "pre", split_axis=0, concat_axis=2, tiled=True),
        lax.all_to_all(cache_b, "pre", split_axis=0, concat_axis=2, tiled=True),
    )
    full_window = moved_a[:, 0].reshape(req_count, -1, heads_dev, 2, HD)
    window_keys = full_window[:, :, :, 0]
    window_values = full_window[:, :, :, 1]
    all_keys = jnp.concatenate([sink_keys, window_keys, key_new], axis=1)
    all_values = jnp.concatenate([sink_values, window_values, value_new], axis=1)
    far_mask = window_mask(WINDOW, fresh_len, my_len)
    key_mask = jnp.concatenate([sink_ok, far_mask, recent_ok], axis=2)
    scores = masked_scores(query, all_keys, key_mask)
    row_top = jnp.max(scores, axis=-1)
    numerator, denominator = partial_terms(scores, key_mask, all_values, row_top)
    attended = (
        (numerator / jnp.transpose(denominator, (0, 2, 1))[..., None])
        .astype(jnp.bfloat16)
        .reshape(row_count, col_width)
    )
    every_head = lax.all_gather(attended, "mdl", axis=1, tiled=True)
    columns = every_head
    output_rows = jnp.dot(
        columns,
        lax.all_gather(w_out, ("pre", "dec"), axis=0, tiled=True),
        preferred_element_type=jnp.float32,
    )
    attn_out = output_rows.astype(jnp.bfloat16).reshape(req_count, 1, fresh_len, -1)
    fresh_kv = jnp.stack([key_new, value_new], axis=3).reshape(req_count, fresh_len, 2 * col_width)[
        :, None
    ]
    decode_a = jnp.concatenate([moved_a[:, :, fresh_len:], fresh_kv], axis=2)
    return (attn_out, decode_a, moved_b)


VMEM_BYTES = 56 * 1024 * 1024
NT = (((1,), (1,)), ((), ()))


class Link:
    def __init__(self, window):
        self.window, self.done = window, []

    def send(self, value, axis, pairs):
        at = len(self.done) - self.window
        if at >= 0:
            value, self.done[at] = lax.optimization_barrier((value, self.done[at]))
        got = lax.ppermute(value, axis, pairs)
        self.done.append(got)
        return got


def load_rows(own, far, held, sems):
    dec_at = lax.axis_index("dec")
    near = jnp.where(lax.axis_index("mdl") // 2 == lax.axis_index("pre"), 0, 1)
    copies = []
    for step, (one, two) in enumerate(zip(own, far)):
        place = lax.rem(dec_at + 4 - step, 4)
        copies.append(pltpu.make_async_copy(one, held.at[near, place], sems.at[2 * step]))
        copies.append(pltpu.make_async_copy(two, held.at[1 - near, place], sems.at[2 * step + 1]))
    for copy in copies:
        copy.start()
    for copy in copies:
        copy.wait()


def project_kernel(width, *refs):
    pieces, own_w, far_w, (cosines, sines) = refs[:16], refs[16:20], refs[20:24], refs[24:26]
    outs, (held, sems) = refs[26:30], refs[30:]
    core_at = lax.axis_index("mdl") % 2
    load_rows(own_w, far_w, held, sems)
    depth = held.shape[3]
    rotated = 2 * width
    lane = lax.broadcasted_iota(jnp.int32, (1, rotated), 1)
    in_first = lane % HD < HD // 2
    for slot in range(4):
        total = None
        for which in range(4):
            core = core_at if which < 2 else 1 - core_at
            for part in range(2):
                term = lax.dot_general(
                    pieces[4 * slot + which][:, part * depth : (part + 1) * depth],
                    held[which % 2, core * 2 + part],
                    NT,
                    preferred_element_type=jnp.float32,
                )
                total = term if total is None else total + term
        turned = total[:, :rotated]
        ahead = pltpu.roll(turned, rotated - HD // 2, 1)
        behind = pltpu.roll(turned, HD // 2, 1)
        turned = turned * cosines[slot] + jnp.where(in_first, ahead, behind) * sines[slot]
        outs[slot][:, :rotated] = turned.astype(jnp.bfloat16)
        outs[slot][:, rotated:] = total[:, rotated:].astype(jnp.bfloat16)


def project(pieces, own_w, far_w, cosines, sines):
    rows, depth = pieces[0].shape
    columns = own_w[0].shape[0]
    return pl.pallas_call(
        functools.partial(project_kernel, columns // 3),
        out_shape=[jax.ShapeDtypeStruct((rows, columns), jnp.bfloat16)] * 4,
        in_specs=[pl.BlockSpec(memory_space=pltpu.VMEM)] * 16
        + [pl.BlockSpec(memory_space=pl.ANY)] * 8
        + [pl.BlockSpec(memory_space=pltpu.VMEM)] * 2,
        out_specs=[pl.BlockSpec(memory_space=pltpu.VMEM)] * 4,
        scratch_shapes=[
            pltpu.VMEM((2, 4) + own_w[0].shape, jnp.bfloat16),
            pltpu.SemaphoreType.DMA((8,)),
        ],
        compiler_params=pltpu.CompilerParams(vmem_limit_bytes=VMEM_BYTES),
        cost_estimate=pl.CostEstimate(
            flops=8 * rows * 4 * depth * columns, bytes_accessed=16_000_000, transcendentals=0
        ),
        name="project",
    )(*pieces, *own_w, *far_w, cosines, sines)


def attend_kernel(
    prior, y0, y1, y2, y3, own, far, sinks, attended, decode, held, fresh, sems, out_sems
):
    pre_at, dec_at = lax.axis_index("pre"), lax.axis_index("dec")
    copies = [
        pltpu.make_async_copy(source, held.at[lax.rem(dec_at + step, 4)], sems.at[step])
        for step, source in enumerate((y0, y1, y2, y3))
    ]
    for copy in copies:
        copy.start()
    for copy in copies:
        copy.wait()
    rows, half = held.shape[1], own.shape[0]
    span = 2 * HD
    heads = own.shape[1] // span
    local = heads // 4
    for head in range(heads):
        block, at = head // local, (head % local) * HD
        for kind in (1, 2):
            fresh[:, head * span + (kind - 1) * HD : head * span + kind * HD] = held[
                block, :, kind * local * HD + at : kind * local * HD + at + HD
            ]
    tail = pltpu.make_async_copy(fresh, decode.at[pl.ds(2 * half - rows, rows)], out_sems.at[0])
    tail.start()

    def keep(early, late):
        first = pltpu.make_async_copy(
            early.at[pl.ds(rows, half - rows)], decode.at[pl.ds(0, half - rows)], out_sems.at[1]
        )
        second = pltpu.make_async_copy(late, decode.at[pl.ds(half - rows, half)], out_sems.at[2])
        return first, second

    @pl.when(pre_at == 0)
    def _():
        for copy in keep(own, far):
            copy.start()

    @pl.when(pre_at != 0)
    def _():
        for copy in keep(far, own):
            copy.start()

    token = lax.broadcasted_iota(jnp.int32, (rows, 1), 0)
    lowest = jnp.maximum(token + 1, SINKS + 2 * half - prior[0])
    slot = lax.broadcasted_iota(jnp.int32, (1, half), 1)
    own_ok = slot >= lowest - pre_at * half
    far_ok = slot >= lowest - (1 - pre_at) * half
    new_ok = lax.broadcasted_iota(jnp.int32, (1, rows), 1) <= token
    sink_ok = lax.broadcasted_iota(jnp.int32, (1, sinks.shape[0]), 1) < SINKS
    scale = HD ** (-0.5)
    for head in range(heads):
        block, at = head // local, (head % local) * HD
        left = head * span
        query = held[block, :, at : at + HD]
        groups = []
        for keys, values, ok in (
            (own[:, left : left + HD], own[:, left + HD : left + span], own_ok),
            (far[:, left : left + HD], far[:, left + HD : left + span], far_ok),
            (fresh[:, left : left + HD], fresh[:, left + HD : left + span], new_ok),
            (sinks[:, left : left + HD], sinks[:, left + HD : left + span], sink_ok),
        ):
            scores = lax.dot_general(query, keys, NT, preferred_element_type=jnp.float32) * scale
            groups.append((jnp.where(ok, scores, MASKED_SCORE), values))
        top = functools.reduce(
            jnp.maximum, [jnp.max(scores, axis=1, keepdims=True) for scores, _ in groups]
        )
        below, mixed = None, None
        for scores, values in groups:
            probability = jnp.exp(scores - top)
            part = jnp.sum(probability, axis=1, keepdims=True)
            term = jnp.dot(
                probability.astype(jnp.bfloat16), values, preferred_element_type=jnp.float32
            )
            below = part if below is None else below + part
            mixed = term if mixed is None else mixed + term
        attended[:, head * HD : (head + 1) * HD] = (mixed / below).astype(jnp.bfloat16)
    tail.wait()

    @pl.when(pre_at == 0)
    def _():
        for copy in keep(own, far):
            copy.wait()

    @pl.when(pre_at != 0)
    def _():
        for copy in keep(far, own):
            copy.wait()


def attend(prior, parts, own, far, sinks):
    rows, columns = parts[0].shape
    half, width = own.shape
    return pl.pallas_call(
        attend_kernel,
        out_shape=[
            jax.ShapeDtypeStruct((rows, width // 2), jnp.bfloat16),
            jax.ShapeDtypeStruct((2 * half, width), jnp.bfloat16),
        ],
        in_specs=[pl.BlockSpec(memory_space=pltpu.SMEM)]
        + [pl.BlockSpec(memory_space=pl.ANY)] * 4
        + [pl.BlockSpec(memory_space=pltpu.VMEM)] * 3,
        out_specs=[
            pl.BlockSpec(memory_space=pltpu.VMEM),
            pl.BlockSpec(memory_space=pl.ANY),
        ],
        scratch_shapes=[
            pltpu.VMEM((4, rows, columns), jnp.bfloat16),
            pltpu.VMEM((rows, width), jnp.bfloat16),
            pltpu.SemaphoreType.DMA((4,)),
            pltpu.SemaphoreType.DMA((3,)),
        ],
        compiler_params=pltpu.CompilerParams(vmem_limit_bytes=VMEM_BYTES),
        cost_estimate=pl.CostEstimate(
            flops=2 * rows * (2 * half + rows) * width,
            bytes_accessed=10_000_000,
            transcendentals=rows * (2 * half + rows) * width // (2 * HD),
        ),
        name="attend",
    )(prior, *parts, own, far, sinks)


def finish_kernel(*refs):
    pieces, own, far, (out, held, sems) = refs[:4], refs[4:8], refs[8:12], refs[12:]
    core_at = lax.axis_index("mdl") % 2
    load_rows(own, far, held, sems)
    depth = held.shape[2]
    total = None
    for which, piece in enumerate(pieces):
        core = core_at if which < 2 else 1 - core_at
        for part in range(2):
            term = jnp.dot(
                piece[:, part * depth : (part + 1) * depth],
                held[which % 2, core * 2 + part],
                preferred_element_type=jnp.float32,
            )
            total = term if total is None else total + term
    out[...] = total.astype(jnp.bfloat16)


def finish(pieces, own, far):
    rows, depth = pieces[0].shape
    columns = own[0].shape[1]
    return pl.pallas_call(
        finish_kernel,
        out_shape=jax.ShapeDtypeStruct((rows, columns), jnp.bfloat16),
        in_specs=[pl.BlockSpec(memory_space=pltpu.VMEM)] * 4
        + [pl.BlockSpec(memory_space=pl.ANY)] * 8,
        out_specs=pl.BlockSpec(memory_space=pltpu.VMEM),
        scratch_shapes=[
            pltpu.VMEM((2, 4) + own[0].shape, jnp.bfloat16),
            pltpu.SemaphoreType.DMA((8,)),
        ],
        compiler_params=pltpu.CompilerParams(vmem_limit_bytes=VMEM_BYTES),
        cost_estimate=pl.CostEstimate(
            flops=8 * rows * depth * columns, bytes_accessed=7_000_000, transcendentals=0
        ),
        name="finish",
    )(*pieces, *own, *far)


def join_kernel(own, far, out):
    half = own.shape[0]
    pre_at = lax.axis_index("pre")

    @pl.when(pre_at == 0)
    def _():
        out[:half] = own[...]
        out[half:] = far[...]

    @pl.when(pre_at != 0)
    def _():
        out[:half] = far[...]
        out[half:] = own[...]


def join(own, far):
    half, width = own.shape
    block = pl.BlockSpec((half, 256), lambda at: (0, at))
    return pl.pallas_call(
        join_kernel,
        out_shape=jax.ShapeDtypeStruct((2 * half, width), jnp.bfloat16),
        grid=(width // 256,),
        in_specs=[block, block],
        out_specs=pl.BlockSpec((2 * half, 256), lambda at: (0, at)),
        cost_estimate=pl.CostEstimate(
            flops=0, bytes_accessed=8 * half * width, transcendentals=0
        ),
        name="join",
    )(own, far)


def split_body(sizes, tokens, norm_gain, w_qkv, w_out, sink_cache, cache_a, cache_b, lengths, groups):
    dec = sizes["dec"]
    rows = tokens.shape[2]
    heads_dev = cache_a.shape[-1] // (2 * HD)
    width = heads_dev // dec * HD
    pre_at, dec_at, mdl_at = (lax.axis_index(name) for name in ("pre", "dec", "mdl"))
    swap = [(0, 1), (1, 0)]
    over_y = [(0, 2), (1, 3), (2, 0), (3, 1)]
    over_core = [(0, 1), (1, 0), (2, 3), (3, 2)]

    def along(step):
        return [(at, (at + step) % dec) for at in range(dec)]

    own_a, own_b = (
        lax.dynamic_index_in_dim(cache[:, 0], pre_at, 0, keepdims=False) for cache in (cache_a, cache_b)
    )
    sent_a, sent_b = (
        lax.dynamic_index_in_dim(cache[:, 0], 1 - pre_at, 0, keepdims=False)
        for cache in (cache_a, cache_b)
    )
    x_link, y_link, z_link = Link(2), Link(2), Link(3)

    raw = tokens.reshape(rows, -1).astype(jnp.float32)
    squares = jnp.sum(raw * raw, axis=-1).reshape(2, -1)
    squares = squares + lax.ppermute(squares, "mdl", over_y)
    squares = squares + lax.ppermute(squares, "mdl", over_core)
    mean = squares.reshape(rows, 1) / (sizes["mdl"] * raw.shape[1])
    gain = lax.dynamic_index_in_dim(
        norm_gain.astype(jnp.float32).reshape(sizes["mdl"], -1), mdl_at, 0, keepdims=True
    )
    normed = (raw * lax.rsqrt(mean + 1e-05) * gain).astype(jnp.bfloat16)

    turned = jnp.transpose(w_qkv, (1, 2, 0)).reshape(3, dec, width, -1)
    turned = jnp.transpose(turned, (1, 0, 2, 3)).reshape(dec, 3 * width, -1)
    share = [
        lax.dynamic_index_in_dim(turned, (dec_at + step) % dec, 0, keepdims=False) for step in range(dec)
    ]
    x_link.send(w_out, "pre", swap)
    x_link.send(sent_a, "pre", swap)
    near, own_w, across = [normed], [share[0]], []
    for step in (1, 2, 3):
        own_w.append(z_link.send(share[step], "dec", along(step)))
        near.append(z_link.send(normed, "dec", along(step)))
    for step in range(4):
        x_link.send(own_w[step], "pre", swap)
        across.append(y_link.send(near[step], "mdl", over_y))
    own_o = [w_out]
    for step in (1, 2, 3):
        own_o.append(z_link.send(w_out, "dec", along(step)))
    for step in (1, 2, 3):
        x_link.send(own_o[step], "pre", swap)
    x_link.send(sent_b, "pre", swap)
    far_w = x_link.done[2:6]
    far_o = [x_link.done[0]] + x_link.done[6:9]
    far_a, far_b = x_link.done[1], x_link.done[9]
    own_w = [share[0]] + [z_link.done[at] for at in (0, 2, 4)]
    near = [normed] + [z_link.done[at] for at in (1, 3, 5)]
    own_o = [w_out] + z_link.done[6:]
    across = y_link.done
    pieces = []
    for one, two in zip(near, across):
        pieces += [one, two, lax.ppermute(one, "mdl", over_core), lax.ppermute(two, "mdl", over_core)]

    slots = (dec_at - jnp.arange(4)) % dec
    lens = lengths[pre_at][slots]
    cosines, sines = angles(lens, rows)
    cosines, sines = cosines[:, :, 0], sines[:, :, 0]
    repeat = 2 * width // HD
    cosines = jnp.tile(jnp.concatenate([cosines, cosines], axis=-1), (1, 1, repeat))
    sines = jnp.tile(jnp.concatenate([-sines, sines], axis=-1), (1, 1, repeat))
    sinks = jnp.pad(
        lax.dynamic_index_in_dim(sink_cache, groups[pre_at, dec_at], 0, keepdims=False),
        ((0, 16 - SINKS), (0, 0)),
    )
    prior = lengths[pre_at, dec_at].reshape(1)

    found = project(pieces, own_w, far_w, cosines, sines)
    parts = [found[0]] + [
        lax.ppermute(found[step], "dec", along(-step)) for step in (1, 2, 3)
    ]
    attended, decode_a = attend(prior, parts, own_a, far_a, sinks)
    second = lax.ppermute(attended, "mdl", over_y)
    shares = [
        attended,
        second,
        lax.ppermute(attended, "mdl", over_core),
        lax.ppermute(second, "mdl", over_core),
    ]
    attn_out = finish(shares, own_o, far_o)
    decode_b = join(own_b, far_b)
    return (attn_out[None, None], decode_a[None, None], decode_b[None, None])


def body(sizes, tokens, norm_gain, w_qkv, w_out, sink_cache, cache_a, cache_b, lengths, groups):
    heads_dev = cache_a.shape[-1] // (2 * HD)
    shapes = (sizes["pre"], sizes["mdl"], sizes["dec"], heads_dev)
    split = shapes == (2, 4, 4, 8) and tokens.shape[0] == 1 and tokens.shape[1] == 1
    args = (tokens, norm_gain, w_qkv, w_out, sink_cache, cache_a, cache_b, lengths, groups)
    return split_body(sizes, *args) if split else general_body(*args)


def solution(mesh):
    placed = (
        P("pre", "dec", None, "mdl"),
        P(),
        P(("pre", "dec"), None, "mdl"),
        P(("pre", "dec"), "mdl"),
        P(None, None, "mdl"),
        P(None, "dec", "pre", "mdl"),
        P(None, "dec", "pre", "mdl"),
        P(),
        P(),
    )
    return jax.shard_map(
        functools.partial(body, dict(mesh.shape)),
        mesh=mesh,
        in_specs=placed,
        out_specs=(
            P("pre", "dec", None, "mdl"),
            P("pre", "dec", None, "mdl"),
            P("pre", "dec", None, "mdl"),
        ),
        check_vma=False,
    )
```

```python
import functools

import jax
import jax.numpy as jnp
from jax import lax
from jax.experimental import pallas as pl
from jax.experimental.pallas import tpu as pltpu
from jax.sharding import PartitionSpec as P

HD = 96
WINDOW = 1024
SINKS = 4


MASKED_SCORE = -1e30


def rotate(vector, cosines, sines):
    halfway = vector.shape[-1] // 2
    first_half = vector[..., :halfway]
    second_half = vector[..., halfway:]
    return jnp.concatenate(
        [first_half * cosines - second_half * sines, second_half * cosines + first_half * sines],
        axis=-1,
    )


def angles(offsets, count):
    halfway = HD // 2
    frequency = 10000.0 ** (-(jnp.arange(halfway).astype(jnp.float32) * 2.0) / HD)
    places = offsets.astype(jnp.float32)[:, None] + jnp.arange(count).astype(jnp.float32)[None, :]
    phases = places[:, :, None] * frequency[None, None, :]
    return (jnp.cos(phases)[:, :, None, :], jnp.sin(phases)[:, :, None, :])


def window_mask(slot_count, fresh_len, prior):
    slot_pos = jnp.arange(slot_count)[None, None, :]
    query_pos = jnp.arange(fresh_len)[None, :, None]
    return (slot_pos >= query_pos + 1) & (slot_pos >= SINKS + WINDOW - prior[:, None, None])


def masked_scores(query, all_keys, key_mask):
    scores = jnp.einsum(
        "rqhd,rkhd->rhqk", query, all_keys, preferred_element_type=jnp.float32
    ) * HD ** (-0.5)
    return jnp.where(key_mask[:, None], scores, MASKED_SCORE)


def partial_terms(scores, key_mask, all_values, row_top):
    probability = jnp.where(key_mask[:, None], jnp.exp(scores - row_top[..., None]), 0.0)
    denominator = jnp.sum(probability, axis=-1)
    numerator = jnp.einsum(
        "rhqk,rkhd->rqhd",
        probability.astype(jnp.bfloat16),
        all_values,
        preferred_element_type=jnp.float32,
    )
    return (numerator, denominator)


def general_body(tokens, norm_gain, w_qkv, w_out, sink_cache, cache_a, cache_b, lengths, groups):
    req_count = tokens.shape[0]
    fresh_len = tokens.shape[2]
    col_width = cache_a.shape[-1] // 2
    heads_dev = col_width // HD
    row_count = req_count * fresh_len
    pre_at = lax.axis_index("pre") * req_count
    dec_at = lax.axis_index("dec")
    gathered = lax.all_gather(tokens, "mdl", axis=3, tiled=True)
    as_float = gathered.reshape(row_count, -1).astype(jnp.float32)
    normed = (
        as_float
        * lax.rsqrt(jnp.mean(as_float * as_float, axis=-1, keepdims=True) + 1e-05)
        * norm_gain.astype(jnp.float32)
    ).astype(jnp.bfloat16)
    shard_rows = lax.all_gather(w_qkv, ("pre", "dec"), axis=0, tiled=True)
    columns = normed
    projected = jnp.dot(
        columns, shard_rows.reshape(shard_rows.shape[0], -1), preferred_element_type=jnp.float32
    )
    projected = projected.reshape(req_count, fresh_len, 3, heads_dev, HD)
    my_len = lax.dynamic_slice(lengths, (pre_at, dec_at), (req_count, 1))[:, 0]
    my_group = lax.dynamic_slice(groups, (pre_at, dec_at), (req_count, 1))[:, 0]
    cosines, sines = angles(my_len, fresh_len)
    query = rotate(projected[:, :, 0], cosines, sines).astype(jnp.bfloat16)
    key_new = rotate(projected[:, :, 1], cosines, sines).astype(jnp.bfloat16)
    value_new = projected[:, :, 2].astype(jnp.bfloat16)
    onehot = (my_group[:, None] == jnp.arange(sink_cache.shape[0])[None, :]).astype(jnp.float32)
    sink_rows = jnp.einsum("rg,gsc->rsc", onehot, sink_cache.astype(jnp.float32)).astype(
        jnp.bfloat16
    )
    sink_rows = sink_rows.reshape(req_count, SINKS, heads_dev, 2, HD)
    sink_keys = sink_rows[:, :, :, 0]
    sink_values = sink_rows[:, :, :, 1]
    sink_ok = jnp.ones((req_count, fresh_len, SINKS), dtype=bool)
    recent_ok = jnp.arange(fresh_len)[None, None, :] <= jnp.arange(fresh_len)[None, :, None]
    moved_a, moved_b = (
        lax.all_to_all(cache_a, "pre", split_axis=0, concat_axis=2, tiled=True),
        lax.all_to_all(cache_b, "pre", split_axis=0, concat_axis=2, tiled=True),
    )
    full_window = moved_a[:, 0].reshape(req_count, -1, heads_dev, 2, HD)
    window_keys = full_window[:, :, :, 0]
    window_values = full_window[:, :, :, 1]
    all_keys = jnp.concatenate([sink_keys, window_keys, key_new], axis=1)
    all_values = jnp.concatenate([sink_values, window_values, value_new], axis=1)
    far_mask = window_mask(WINDOW, fresh_len, my_len)
    key_mask = jnp.concatenate([sink_ok, far_mask, recent_ok], axis=2)
    scores = masked_scores(query, all_keys, key_mask)
    row_top = jnp.max(scores, axis=-1)
    numerator, denominator = partial_terms(scores, key_mask, all_values, row_top)
    attended = (
        (numerator / jnp.transpose(denominator, (0, 2, 1))[..., None])
        .astype(jnp.bfloat16)
        .reshape(row_count, col_width)
    )
    every_head = lax.all_gather(attended, "mdl", axis=1, tiled=True)
    columns = every_head
    output_rows = jnp.dot(
        columns,
        lax.all_gather(w_out, ("pre", "dec"), axis=0, tiled=True),
        preferred_element_type=jnp.float32,
    )
    attn_out = output_rows.astype(jnp.bfloat16).reshape(req_count, 1, fresh_len, -1)
    fresh_kv = jnp.stack([key_new, value_new], axis=3).reshape(req_count, fresh_len, 2 * col_width)[
        :, None
    ]
    decode_a = jnp.concatenate([moved_a[:, :, fresh_len:], fresh_kv], axis=2)
    return (attn_out, decode_a, moved_b)


VMEM_BYTES = 56 * 1024 * 1024
NT = (((1,), (1,)), ((), ()))


def mates(at):
    return [at, at + 1 - 2 * lax.rem(at, 2), 2 - at // 2, 3 - 3 * (at // 2)]


def near_half():
    return jnp.where(lax.axis_index("mdl") // 2 == lax.axis_index("pre"), 0, 1)


def run_all(copies):
    for copy in copies:
        copy.start()
    for copy in copies:
        copy.wait()


def project_kernel(width, *refs):
    where, normed, mate, third, fourth, y_own, y_mate, y_third, y_fourth, core_near, core_far = refs[:11]
    weights, (cosines, sines, out, held, sems) = refs[11:16], refs[16:]
    core_at = lax.axis_index("mdl") % 2
    half, depth = weights[0].shape[1:]
    copies = []
    for which, source in enumerate(weights):
        row = near_half() if which < 2 else 1 - near_half()
        head = (0, 1, 0, 1, 1)[which]
        for block in range(source.shape[0]):
            place = block + (2 if which == 4 else 0)
            target = held.at[row, place // 2, head, :, place % 2 * depth : (place % 2 + 1) * depth]
            copies.append(pltpu.make_async_copy(source.at[block], target, sems.at[len(copies)]))
    run_all(copies)
    rows = normed.shape[0]
    lane = lax.broadcasted_iota(jnp.int32, (1, width), 1)
    in_first = lane % HD < HD // 2
    blocks = (
        (normed, mate, y_own, y_mate, core_near),
        (third, fourth, y_third, y_fourth, core_far),
    )
    for pair, (one, two, y_one, y_two, others) in enumerate(blocks):
        pieces = (
            jnp.concatenate([one[...], two[...]], axis=0),
            jnp.concatenate([y_one[...], y_two[...]], axis=0),
            others[: 2 * rows],
            others[2 * rows :],
        )
        for head in range(2):
            total = None
            for which, piece in enumerate(pieces):
                core = core_at if which < 2 else 1 - core_at
                term = lax.dot_general(
                    piece, held[which % 2, core, head], NT, preferred_element_type=jnp.float32
                )
                total = term if total is None else total + term
            for slot in range(2):
                part = total[slot * rows : (slot + 1) * rows]
                turned = part[:, :width]
                ahead = pltpu.roll(turned, width - HD // 2, 1)
                behind = pltpu.roll(turned, HD // 2, 1)
                at = where[2 * pair + slot]
                cosine, sine = (
                    jnp.concatenate([table[at]] * 2, axis=1) for table in (cosines, sines)
                )
                turned = turned * cosine + jnp.where(in_first, ahead, behind) * sine
                out[at, :rows, head * width : (head + 1) * width] = turned.astype(jnp.bfloat16)
                value = part[:, width:].astype(jnp.bfloat16)
                for row in range(2):
                    left = row * width + head * HD
                    out[at, rows:, left : left + HD] = value[row * rows // 2 : (row + 1) * rows // 2]


def project(where, pieces, weights, cosines, sines):
    rows, depth = cosines.shape[1], pieces[0].shape[1]
    half = weights[0].shape[1]
    return pl.pallas_call(
        functools.partial(project_kernel, half // 3 * 2),
        out_shape=jax.ShapeDtypeStruct((4, rows + rows // 2, 4 * half // 3), jnp.bfloat16),
        in_specs=[pl.BlockSpec(memory_space=pltpu.SMEM)]
        + [pl.BlockSpec(memory_space=pltpu.VMEM)] * 10
        + [pl.BlockSpec(memory_space=pl.ANY)] * 5
        + [pl.BlockSpec(memory_space=pltpu.VMEM)] * 2,
        out_specs=pl.BlockSpec(memory_space=pltpu.VMEM),
        scratch_shapes=[
            pltpu.VMEM((2, 2, 2, half, 2 * weights[0].shape[2]), jnp.bfloat16),
            pltpu.SemaphoreType.DMA((16,)),
        ],
        compiler_params=pltpu.CompilerParams(vmem_limit_bytes=VMEM_BYTES),
        cost_estimate=pl.CostEstimate(
            flops=8 * rows * 8 * depth * half, bytes_accessed=16_000_000, transcendentals=0
        ),
        name="project",
    )(where, *pieces, *weights, cosines, sines)


def attend_kernel(
    prior, held, cache, far0, far1, sinks, attended, decode, window, bias, sems, out_sems
):
    pre_at = lax.axis_index("pre")
    rows, half = attended.shape[0], cache.shape[1]
    fresh, last = 2 * half, 2 * half + rows
    loads = [
        pltpu.make_async_copy(cache.at[pre_at], window.at[pl.ds(0, half)], sems.at[0]),
        pltpu.make_async_copy(far0, window.at[pl.ds(half, half // 2)], sems.at[1]),
        pltpu.make_async_copy(far1, window.at[pl.ds(half + half // 2, half // 2)], sems.at[2]),
    ]
    for load in loads:
        load.start()
    span = 2 * HD
    heads = cache.shape[2] // span
    local = heads // 4
    for head in range(heads):
        block, at = head // local, head % local
        left = head * span
        window[fresh:last, left : left + HD] = held[block, :rows, at * span + HD : (at + 1) * span]
        for row in range(2):
            start = row * local * HD + at * HD
            window[
                fresh + row * rows // 2 : fresh + (row + 1) * rows // 2, left + HD : left + span
            ] = held[block, rows:, start : start + HD]
    window[last:] = jnp.zeros((window.shape[0] - last, window.shape[1]), window.dtype)
    window[last : last + sinks.shape[0]] = sinks[...]
    tail = pltpu.make_async_copy(
        window.at[pl.ds(fresh, rows)], decode.at[pl.ds(2 * half - rows, rows)], out_sems.at[0]
    )
    tail.start()
    token = lax.broadcasted_iota(jnp.int32, (rows, 1), 0)
    lowest = jnp.maximum(token + 1, SINKS + 2 * half - prior[0])
    slot = lax.broadcasted_iota(jnp.int32, (1, half), 1)
    new = lax.broadcasted_iota(jnp.int32, (1, rows), 1)
    sink = lax.broadcasted_iota(jnp.int32, (1, window.shape[0] - last), 1)

    def shown(ok):
        return jnp.where(ok, 0.0, MASKED_SCORE)

    bias[:, :half] = shown(slot >= lowest - pre_at * half)
    bias[:, half:fresh] = shown(slot >= lowest - (1 - pre_at) * half)
    bias[:, fresh:last] = shown(new <= token)
    bias[:, last:] = jnp.broadcast_to(shown(sink < SINKS), (rows, window.shape[0] - last))
    for load in loads:
        load.wait()

    def keep(early, late):
        first = pltpu.make_async_copy(
            window.at[pl.ds(early + rows, half - rows)],
            decode.at[pl.ds(0, half - rows)],
            out_sems.at[1],
        )
        second = pltpu.make_async_copy(
            window.at[pl.ds(late, half)], decode.at[pl.ds(half - rows, half)], out_sems.at[2]
        )
        return first, second

    @pl.when(pre_at == 0)
    def _():
        for copy in keep(0, half):
            copy.start()

    @pl.when(pre_at != 0)
    def _():
        for copy in keep(half, 0):
            copy.start()

    scale = HD ** (-0.5)
    for head in range(heads):
        block, at = head // local, head % local * span
        left = head * span
        scores = lax.dot_general(
            held[block, :rows, at : at + HD],
            window[:, left : left + HD],
            NT,
            preferred_element_type=jnp.float32,
        )
        scores = scores * scale + bias[...]
        top = jnp.max(scores, axis=1, keepdims=True)
        probability = jnp.exp(scores - top)
        below = jnp.sum(probability, axis=1, keepdims=True)
        mixed = jnp.dot(
            probability.astype(jnp.bfloat16),
            window[:, left + HD : left + span],
            preferred_element_type=jnp.float32,
        )
        attended[:, head * HD : (head + 1) * HD] = (mixed / below).astype(jnp.bfloat16)
    tail.wait()

    @pl.when(pre_at == 0)
    def _():
        for copy in keep(0, half):
            copy.wait()

    @pl.when(pre_at != 0)
    def _():
        for copy in keep(half, 0):
            copy.wait()


def attend(prior, parts, cache, fars, sinks):
    rows = 2 * parts.shape[1] // 3
    half, width = cache.shape[1:]
    keys = 2 * half + rows + 128
    return pl.pallas_call(
        attend_kernel,
        out_shape=[
            jax.ShapeDtypeStruct((rows, width // 2), jnp.bfloat16),
            jax.ShapeDtypeStruct((2 * half, width), jnp.bfloat16),
        ],
        in_specs=[
            pl.BlockSpec(memory_space=pltpu.SMEM),
            pl.BlockSpec(memory_space=pltpu.VMEM),
            pl.BlockSpec(memory_space=pl.ANY),
            pl.BlockSpec(memory_space=pl.ANY),
            pl.BlockSpec(memory_space=pl.ANY),
            pl.BlockSpec(memory_space=pltpu.VMEM),
        ],
        out_specs=[
            pl.BlockSpec(memory_space=pltpu.VMEM),
            pl.BlockSpec(memory_space=pl.ANY),
        ],
        scratch_shapes=[
            pltpu.VMEM((keys, width), jnp.bfloat16),
            pltpu.VMEM((rows, keys), jnp.float32),
            pltpu.SemaphoreType.DMA((3,)),
            pltpu.SemaphoreType.DMA((3,)),
        ],
        compiler_params=pltpu.CompilerParams(vmem_limit_bytes=VMEM_BYTES),
        cost_estimate=pl.CostEstimate(
            flops=2 * rows * keys * width,
            bytes_accessed=10_000_000,
            transcendentals=rows * keys * width // (2 * HD),
        ),
        name="attend",
    )(prior, parts, cache, *fars, sinks)


def finish_kernel(*refs):
    pieces, own, far, (out, held, sems) = refs[:4], refs[4:8], refs[8:12], refs[12:]
    core_at = lax.axis_index("mdl") % 2
    depth = own[0].shape[0]
    copies = []
    for step, place in enumerate(mates(lax.axis_index("dec"))):
        rows = pl.ds(pl.multiple_of(lax.rem(place, 2) * depth, depth), depth)
        for row, source in ((near_half(), own[step]), (1 - near_half(), far[step])):
            target = held.at[row, place // 2, rows]
            copies.append(pltpu.make_async_copy(source, target, sems.at[len(copies)]))
    run_all(copies)
    total = None
    for which, piece in enumerate(pieces):
        core = core_at if which < 2 else 1 - core_at
        term = jnp.dot(piece[...], held[which % 2, core], preferred_element_type=jnp.float32)
        total = term if total is None else total + term
    out[...] = total.astype(jnp.bfloat16)


def finish(pieces, own, far):
    rows, depth = pieces[0].shape
    columns = own[0].shape[1]
    return pl.pallas_call(
        finish_kernel,
        out_shape=jax.ShapeDtypeStruct((rows, columns), jnp.bfloat16),
        in_specs=[pl.BlockSpec(memory_space=pltpu.VMEM)] * 4
        + [pl.BlockSpec(memory_space=pl.ANY)] * 8,
        out_specs=pl.BlockSpec(memory_space=pltpu.VMEM),
        scratch_shapes=[
            pltpu.VMEM((2, 2, 2 * own[0].shape[0], columns), jnp.bfloat16),
            pltpu.SemaphoreType.DMA((8,)),
        ],
        compiler_params=pltpu.CompilerParams(vmem_limit_bytes=VMEM_BYTES),
        cost_estimate=pl.CostEstimate(
            flops=8 * rows * depth * columns, bytes_accessed=7_000_000, transcendentals=0
        ),
        name="finish",
    )(*pieces, *own, *far)


def join_kernel(cache, far, out, held, sems):
    half = far.shape[0]
    pre_at = lax.axis_index("pre")
    loads = [
        pltpu.make_async_copy(cache.at[pre_at], held.at[0], sems.at[0]),
        pltpu.make_async_copy(far, held.at[1], sems.at[1]),
    ]
    stores = [
        pltpu.make_async_copy(
            held.at[which], out.at[pl.ds(pl.multiple_of(at * half, half), half)], sems.at[2 + which]
        )
        for which, at in enumerate((pre_at, 1 - pre_at))
    ]
    for load in loads:
        load.start()
    for load, store in zip(loads, stores):
        load.wait()
        store.start()
    for store in stores:
        store.wait()


def join(cache, far):
    half, width = far.shape
    return pl.pallas_call(
        join_kernel,
        out_shape=jax.ShapeDtypeStruct((2 * half, width), jnp.bfloat16),
        in_specs=[pl.BlockSpec(memory_space=pl.ANY)] * 2,
        out_specs=pl.BlockSpec(memory_space=pl.ANY),
        scratch_shapes=[pltpu.VMEM((2, half, width), jnp.bfloat16), pltpu.SemaphoreType.DMA((4,))],
        compiler_params=pltpu.CompilerParams(vmem_limit_bytes=VMEM_BYTES),
        cost_estimate=pl.CostEstimate(
            flops=0, bytes_accessed=8 * half * width, transcendentals=0
        ),
        name="join",
    )(cache, far)


def split_body(sizes, tokens, norm_gain, w_qkv, w_out, sink_cache, cache_a, cache_b, lengths, groups):
    dec = sizes["dec"]
    rows = tokens.shape[2]
    pre_at, dec_at, mdl_at = (lax.axis_index(name) for name in ("pre", "dec", "mdl"))
    swap = [(0, 1), (1, 0)]
    over_y = [(0, 2), (1, 3), (2, 0), (3, 1)]
    over_core = [(0, 1), (1, 0), (2, 3), (3, 2)]

    def along(step):
        return [(at, (at + step) % dec) for at in range(dec)]

    sent_a, sent_b = (
        lax.dynamic_index_in_dim(cache[:, 0], 1 - pre_at, 0, keepdims=False)
        for cache in (cache_a, cache_b)
    )
    raw = tokens.reshape(rows, -1).astype(jnp.float32)
    squares = jnp.sum(raw * raw, axis=-1).reshape(2, -1)
    across_both = [(0, 3), (1, 2), (2, 1), (3, 0)]
    squares = squares + sum(
        lax.ppermute(squares, "mdl", way) for way in (over_y, over_core, across_both)
    )
    mean = squares.reshape(rows, 1) / (sizes["mdl"] * raw.shape[1])
    gain = lax.dynamic_index_in_dim(
        norm_gain.astype(jnp.float32).reshape(sizes["mdl"], -1), mdl_at, 0, keepdims=True
    )
    normed = (raw * lax.rsqrt(mean + 1e-05) * gain).astype(jnp.bfloat16)

    turned = jnp.transpose(w_qkv, (1, 2, 0)).reshape(3, dec, 2, HD, -1)
    turned = jnp.transpose(turned, (2, 1, 0, 3, 4)).reshape(2, dec, 3 * HD, -1)
    pairs = [(0, 1), (1, 0), (2, 3), (3, 2)]
    middle = [(1, 2), (2, 1)]
    outward = [(1, 0), (2, 3)]
    in_middle = (dec_at == 1) | (dec_at == 2)

    def pick(middle_got, outer_got):
        return jnp.where(in_middle, middle_got, outer_got)

    edges = lax.optimization_barrier
    half = sent_a.shape[0] // 2
    first_w = lax.all_to_all(turned[0], "dec", 0, 0, tiled=True)
    mate = lax.ppermute(normed, "dec", pairs)
    inner = lax.ppermute(normed, "dec", middle)
    y_own = lax.ppermute(normed, "mdl", over_y)
    far_a0 = lax.ppermute(sent_a[:half], "pre", swap)
    o_far = lax.ppermute(w_out, "pre", swap)
    first_w, mate, inner, y_own, far_a0, o_far, second_w = edges(
        (first_w, mate, inner, y_own, far_a0, o_far, turned[1])
    )
    second_w = lax.all_to_all(second_w, "dec", 0, 0, tiled=True)
    inner_mate = lax.ppermute(mate, "dec", middle)
    outer = lax.ppermute(inner, "dec", outward)
    y_mate = lax.ppermute(mate, "mdl", over_y)
    far_first = lax.ppermute(first_w, "pre", swap)
    second_w, inner_mate, outer, y_mate, far_first, late_o, late_a = edges(
        (second_w, inner_mate, outer, y_mate, far_first, w_out, sent_a[half:])
    )
    third = pick(inner, outer)
    far_second = lax.ppermute(second_w[:2], "pre", swap)
    outer_mate = lax.ppermute(inner_mate, "dec", outward)
    o_inner = lax.ppermute(late_o, "dec", middle)
    y_third = lax.ppermute(third, "mdl", over_y)
    far_second, outer_mate, y_third, o_inner, rest_w, late_o = edges(
        (far_second, outer_mate, y_third, o_inner, second_w[2:], late_o)
    )
    far_rest = lax.ppermute(rest_w, "pre", swap)
    fourth = pick(inner_mate, outer_mate)
    y_fourth = lax.ppermute(fourth, "mdl", over_y)
    o_mate = lax.ppermute(late_o, "dec", pairs)
    core_near = lax.ppermute(
        jnp.concatenate([normed, mate, y_own, y_mate], axis=0), "mdl", over_core
    )
    far_rest, y_fourth, o_mate, late_a, o_far = edges((far_rest, y_fourth, o_mate, late_a, o_far))
    core_far = lax.ppermute(
        jnp.concatenate([third, fourth, y_third, y_fourth], axis=0), "mdl", over_core
    )
    far_a1 = lax.ppermute(late_a, "pre", swap)
    o_far_mate = lax.ppermute(o_far, "dec", pairs)
    o_inner_mate = lax.ppermute(o_mate, "dec", middle)
    weights = [first_w, second_w, far_first, far_second, far_rest]
    pieces = [normed, mate, third, fourth, y_own, y_mate, y_third, y_fourth, core_near, core_far]

    where = jnp.stack(mates(dec_at)).astype(jnp.int32)
    cosines, sines = angles(lengths[pre_at], rows)
    cosines, sines = cosines[:, :, 0], sines[:, :, 0]
    cosines = jnp.concatenate([cosines, cosines], axis=-1)
    sines = jnp.concatenate([-sines, sines], axis=-1)
    sinks = jnp.pad(
        lax.dynamic_index_in_dim(sink_cache, groups[pre_at, dec_at], 0, keepdims=False),
        ((0, 16 - SINKS), (0, 0)),
    )
    prior = lengths[pre_at, dec_at].reshape(1)

    found = project(where, pieces, weights, cosines, sines)
    found, far_a1, o_far_mate, o_inner_mate, late_b = edges(
        (found, far_a1, o_far_mate, o_inner_mate, sent_b)
    )
    parts = lax.all_to_all(found, "dec", 0, 0, tiled=True)
    far_b = lax.ppermute(late_b, "pre", swap)
    o_outer = lax.ppermute(o_inner, "dec", outward)
    parts, far_b, o_outer = edges((parts, far_b, o_outer))
    o_third = pick(o_inner, o_outer)
    o_far_third = lax.ppermute(o_third, "pre", swap)
    o_outer_mate = lax.ppermute(o_inner_mate, "dec", outward)
    attended, decode_a = attend(prior, parts, cache_a[:, 0], (far_a0, far_a1), sinks)
    attended, o_far_third, o_outer_mate = edges((attended, o_far_third, o_outer_mate))
    o_fourth = pick(o_inner_mate, o_outer_mate)
    o_far_fourth = lax.ppermute(o_fourth, "pre", swap)
    second = lax.ppermute(attended, "mdl", over_y)
    shares = [
        attended,
        second,
        lax.ppermute(attended, "mdl", over_core),
        lax.ppermute(second, "mdl", over_core),
    ]
    attn_out = finish(
        shares,
        [w_out, o_mate, o_third, o_fourth],
        [o_far, o_far_mate, o_far_third, o_far_fourth],
    )
    decode_b = join(cache_b[:, 0], far_b)
    return (attn_out[None, None], decode_a[None, None], decode_b[None, None])


def body(sizes, tokens, norm_gain, w_qkv, w_out, sink_cache, cache_a, cache_b, lengths, groups):
    heads_dev = cache_a.shape[-1] // (2 * HD)
    shapes = (sizes["pre"], sizes["mdl"], sizes["dec"], heads_dev)
    split = shapes == (2, 4, 4, 8) and tokens.shape[0] == 1 and tokens.shape[1] == 1
    args = (tokens, norm_gain, w_qkv, w_out, sink_cache, cache_a, cache_b, lengths, groups)
    return split_body(sizes, *args) if split else general_body(*args)


def solution(mesh):
    placed = (
        P("pre", "dec", None, "mdl"),
        P(),
        P(("pre", "dec"), None, "mdl"),
        P(("pre", "dec"), "mdl"),
        P(None, None, "mdl"),
        P(None, "dec", "pre", "mdl"),
        P(None, "dec", "pre", "mdl"),
        P(),
        P(),
    )
    return jax.shard_map(
        functools.partial(body, dict(mesh.shape)),
        mesh=mesh,
        in_specs=placed,
        out_specs=(
            P("pre", "dec", None, "mdl"),
            P("pre", "dec", None, "mdl"),
            P("pre", "dec", None, "mdl"),
        ),
        check_vma=False,
    )
```

```python
import functools

import jax
import jax.numpy as jnp
from jax import lax
from jax.experimental import pallas as pl
from jax.experimental.pallas import tpu as pltpu
from jax.sharding import PartitionSpec as P

HD = 96
WINDOW = 1024
SINKS = 4


MASKED_SCORE = -1e30


def rotate(vector, cosines, sines):
    halfway = vector.shape[-1] // 2
    first_half = vector[..., :halfway]
    second_half = vector[..., halfway:]
    return jnp.concatenate(
        [first_half * cosines - second_half * sines, second_half * cosines + first_half * sines],
        axis=-1,
    )


def angles(offsets, count):
    halfway = HD // 2
    frequency = 10000.0 ** (-(jnp.arange(halfway).astype(jnp.float32) * 2.0) / HD)
    places = offsets.astype(jnp.float32)[:, None] + jnp.arange(count).astype(jnp.float32)[None, :]
    phases = places[:, :, None] * frequency[None, None, :]
    return (jnp.cos(phases)[:, :, None, :], jnp.sin(phases)[:, :, None, :])


def window_mask(slot_count, fresh_len, prior):
    slot_pos = jnp.arange(slot_count)[None, None, :]
    query_pos = jnp.arange(fresh_len)[None, :, None]
    return (slot_pos >= query_pos + 1) & (slot_pos >= SINKS + WINDOW - prior[:, None, None])


def masked_scores(query, all_keys, key_mask):
    scores = jnp.einsum(
        "rqhd,rkhd->rhqk", query, all_keys, preferred_element_type=jnp.float32
    ) * HD ** (-0.5)
    return jnp.where(key_mask[:, None], scores, MASKED_SCORE)


def partial_terms(scores, key_mask, all_values, row_top):
    probability = jnp.where(key_mask[:, None], jnp.exp(scores - row_top[..., None]), 0.0)
    denominator = jnp.sum(probability, axis=-1)
    numerator = jnp.einsum(
        "rhqk,rkhd->rqhd",
        probability.astype(jnp.bfloat16),
        all_values,
        preferred_element_type=jnp.float32,
    )
    return (numerator, denominator)


def general_body(tokens, norm_gain, w_qkv, w_out, sink_cache, cache_a, cache_b, lengths, groups):
    req_count = tokens.shape[0]
    fresh_len = tokens.shape[2]
    col_width = cache_a.shape[-1] // 2
    heads_dev = col_width // HD
    row_count = req_count * fresh_len
    pre_at = lax.axis_index("pre") * req_count
    dec_at = lax.axis_index("dec")
    gathered = lax.all_gather(tokens, "mdl", axis=3, tiled=True)
    as_float = gathered.reshape(row_count, -1).astype(jnp.float32)
    normed = (
        as_float
        * lax.rsqrt(jnp.mean(as_float * as_float, axis=-1, keepdims=True) + 1e-05)
        * norm_gain.astype(jnp.float32)
    ).astype(jnp.bfloat16)
    shard_rows = lax.all_gather(w_qkv, ("pre", "dec"), axis=0, tiled=True)
    columns = normed
    projected = jnp.dot(
        columns, shard_rows.reshape(shard_rows.shape[0], -1), preferred_element_type=jnp.float32
    )
    projected = projected.reshape(req_count, fresh_len, 3, heads_dev, HD)
    my_len = lax.dynamic_slice(lengths, (pre_at, dec_at), (req_count, 1))[:, 0]
    my_group = lax.dynamic_slice(groups, (pre_at, dec_at), (req_count, 1))[:, 0]
    cosines, sines = angles(my_len, fresh_len)
    query = rotate(projected[:, :, 0], cosines, sines).astype(jnp.bfloat16)
    key_new = rotate(projected[:, :, 1], cosines, sines).astype(jnp.bfloat16)
    value_new = projected[:, :, 2].astype(jnp.bfloat16)
    onehot = (my_group[:, None] == jnp.arange(sink_cache.shape[0])[None, :]).astype(jnp.float32)
    sink_rows = jnp.einsum("rg,gsc->rsc", onehot, sink_cache.astype(jnp.float32)).astype(
        jnp.bfloat16
    )
    sink_rows = sink_rows.reshape(req_count, SINKS, heads_dev, 2, HD)
    sink_keys = sink_rows[:, :, :, 0]
    sink_values = sink_rows[:, :, :, 1]
    sink_ok = jnp.ones((req_count, fresh_len, SINKS), dtype=bool)
    recent_ok = jnp.arange(fresh_len)[None, None, :] <= jnp.arange(fresh_len)[None, :, None]
    moved_a, moved_b = (
        lax.all_to_all(cache_a, "pre", split_axis=0, concat_axis=2, tiled=True),
        lax.all_to_all(cache_b, "pre", split_axis=0, concat_axis=2, tiled=True),
    )
    full_window = moved_a[:, 0].reshape(req_count, -1, heads_dev, 2, HD)
    window_keys = full_window[:, :, :, 0]
    window_values = full_window[:, :, :, 1]
    all_keys = jnp.concatenate([sink_keys, window_keys, key_new], axis=1)
    all_values = jnp.concatenate([sink_values, window_values, value_new], axis=1)
    far_mask = window_mask(WINDOW, fresh_len, my_len)
    key_mask = jnp.concatenate([sink_ok, far_mask, recent_ok], axis=2)
    scores = masked_scores(query, all_keys, key_mask)
    row_top = jnp.max(scores, axis=-1)
    numerator, denominator = partial_terms(scores, key_mask, all_values, row_top)
    attended = (
        (numerator / jnp.transpose(denominator, (0, 2, 1))[..., None])
        .astype(jnp.bfloat16)
        .reshape(row_count, col_width)
    )
    every_head = lax.all_gather(attended, "mdl", axis=1, tiled=True)
    columns = every_head
    output_rows = jnp.dot(
        columns,
        lax.all_gather(w_out, ("pre", "dec"), axis=0, tiled=True),
        preferred_element_type=jnp.float32,
    )
    attn_out = output_rows.astype(jnp.bfloat16).reshape(req_count, 1, fresh_len, -1)
    fresh_kv = jnp.stack([key_new, value_new], axis=3).reshape(req_count, fresh_len, 2 * col_width)[
        :, None
    ]
    decode_a = jnp.concatenate([moved_a[:, :, fresh_len:], fresh_kv], axis=2)
    return (attn_out, decode_a, moved_b)


VMEM_BYTES = 56 * 1024 * 1024
NT = (((1,), (1,)), ((), ()))


def mates(at):
    return [at, at + 1 - 2 * lax.rem(at, 2), 2 - at // 2, 3 - 3 * (at // 2)]


def near_half():
    return jnp.where(lax.axis_index("mdl") // 2 == lax.axis_index("pre"), 0, 1)


def run_all(copies):
    for copy in copies:
        copy.start()
    for copy in copies:
        copy.wait()


def feature_place(which):
    row, core = lax.axis_index("mdl") // 2, lax.axis_index("mdl") % 2
    row = row if which in (0, 2) else 1 - row
    core = core if which < 2 else 1 - core
    return row * 2 + core, core


def norm_kernel(count, *refs):
    pieces, (gain, *outs) = refs[:-5], refs[-5:]
    rows = pieces[0].shape[0]
    for slot in range(count):
        parts = [pieces[which * count + slot][...] for which in range(4)]
        parts = [part.astype(jnp.float32) for part in parts]
        squares = sum(jnp.sum(part * part, axis=1, keepdims=True) for part in parts)
        scale = lax.rsqrt(squares / (4 * parts[0].shape[1]) + 1e-05)
        for which, part in enumerate(parts):
            place, _ = feature_place(which)
            outs[which][slot * rows : (slot + 1) * rows] = (part * scale * gain[place]).astype(
                jnp.bfloat16
            )


def norm(count, pieces, gain):
    rows, depth = pieces[0].shape
    space = pl.BlockSpec(memory_space=pltpu.VMEM)
    return pl.pallas_call(
        functools.partial(norm_kernel, count),
        out_shape=[jax.ShapeDtypeStruct((count * rows, depth), jnp.bfloat16)] * 4,
        in_specs=[space] * (len(pieces) + 1),
        out_specs=[space] * 4,
        compiler_params=pltpu.CompilerParams(vmem_limit_bytes=VMEM_BYTES),
        cost_estimate=pl.CostEstimate(
            flops=24 * count * rows * depth, bytes_accessed=16 * count * rows * depth, transcendentals=0
        ),
        name="norm",
    )(*pieces, gain)


def project_kernel(*refs):
    where, groups, weights = refs[0], (refs[1:5], refs[5:9]), refs[9:13]
    cosines, sines, out, held_qk, held_v, sems = refs[13:]
    depth = weights[0].shape[2]
    copies = []
    for which, source in enumerate(weights):
        held = (held_qk, held_v)[which // 2]
        row = near_half() if which % 2 == 0 else 1 - near_half()
        for place in range(4):
            target = held.at[row, place // 2, :, place % 2 * depth : (place % 2 + 1) * depth]
            copies.append(pltpu.make_async_copy(source.at[place], target, sems.at[len(copies)]))
    run_all(copies)
    rows, columns = refs[5].shape[0], held_qk.shape[2]
    width = columns // 2
    lane = lax.broadcasted_iota(jnp.int32, (1, columns), 1)
    in_first = lane % HD < HD // 2
    first = 0
    for pieces in groups:
        count = pieces[0].shape[0] // rows
        turning, values = (
            sum(
                lax.dot_general(
                    piece[...],
                    held[which % 2, feature_place(which)[1]],
                    NT,
                    preferred_element_type=jnp.float32,
                )
                for which, piece in enumerate(pieces)
            )
            for held in (held_qk, held_v)
        )
        for slot in range(count):
            at = where[first + slot]
            turned = turning[slot * rows : (slot + 1) * rows]
            ahead = pltpu.roll(turned, columns - HD // 2, 1)
            behind = pltpu.roll(turned, HD // 2, 1)
            cosine, sine = (
                jnp.concatenate([table[at]] * (columns // HD), axis=1) for table in (cosines, sines)
            )
            turned = turned * cosine + jnp.where(in_first, ahead, behind) * sine
            out[at, :rows] = turned.astype(jnp.bfloat16)
            value = values[slot * rows : (slot + 1) * rows].astype(jnp.bfloat16)
            for row in range(2):
                out[at, rows:, row * width : (row + 1) * width] = value[
                    row * rows // 2 : (row + 1) * rows // 2
                ]
        first += count


def project(where, pieces, weights, cosines, sines):
    rows, depth = cosines.shape[1], weights[0].shape[2]
    columns, width = weights[0].shape[1], weights[2].shape[1]
    return pl.pallas_call(
        project_kernel,
        out_shape=jax.ShapeDtypeStruct((4, rows + rows // 2, columns), jnp.bfloat16),
        in_specs=[pl.BlockSpec(memory_space=pltpu.SMEM)]
        + [pl.BlockSpec(memory_space=pltpu.VMEM)] * 8
        + [pl.BlockSpec(memory_space=pl.ANY)] * 4
        + [pl.BlockSpec(memory_space=pltpu.VMEM)] * 2,
        out_specs=pl.BlockSpec(memory_space=pltpu.VMEM),
        scratch_shapes=[
            pltpu.VMEM((2, 2, columns, 2 * depth), jnp.bfloat16),
            pltpu.VMEM((2, 2, width, 2 * depth), jnp.bfloat16),
            pltpu.SemaphoreType.DMA((16,)),
        ],
        compiler_params=pltpu.CompilerParams(vmem_limit_bytes=VMEM_BYTES),
        cost_estimate=pl.CostEstimate(
            flops=8 * rows * 8 * depth * (columns + width),
            bytes_accessed=16_000_000,
            transcendentals=0,
        ),
        name="project",
    )(where, *pieces, *weights, cosines, sines)


def attend_kernel(
    prior, held, cache, far0, far1, sinks, attended, decode, window, bias, sems, out_sems
):
    pre_at = lax.axis_index("pre")
    rows, half = attended.shape[0], cache.shape[1]
    fresh, last = 2 * half, 2 * half + rows
    loads = [
        pltpu.make_async_copy(cache.at[pre_at], window.at[pl.ds(0, half)], sems.at[0]),
        pltpu.make_async_copy(far0, window.at[pl.ds(half, far0.shape[0])], sems.at[1]),
        pltpu.make_async_copy(
            far1.at[pl.ds(0, half - far0.shape[0])],
            window.at[pl.ds(half + far0.shape[0], half - far0.shape[0])],
            sems.at[2],
        ),
    ]
    for load in loads:
        load.start()
    span = 2 * HD
    heads = cache.shape[2] // span
    local = heads // 4
    for head in range(heads):
        block, at = head // local, head % local
        left = head * span
        start = (local + at) * HD
        window[fresh:last, left : left + HD] = held[block, :rows, start : start + HD]
        for row in range(2):
            start = row * local * HD + at * HD
            window[
                fresh + row * rows // 2 : fresh + (row + 1) * rows // 2, left + HD : left + span
            ] = held[block, rows:, start : start + HD]
    window[last:] = jnp.zeros((window.shape[0] - last, window.shape[1]), window.dtype)
    window[last : last + sinks.shape[0]] = sinks[...]
    tail = pltpu.make_async_copy(
        window.at[pl.ds(fresh, rows)], decode.at[pl.ds(2 * half - rows, rows)], out_sems.at[0]
    )
    tail.start()
    token = lax.broadcasted_iota(jnp.int32, (rows, 1), 0)
    lowest = jnp.maximum(token + 1, SINKS + 2 * half - prior[0])
    slot = lax.broadcasted_iota(jnp.int32, (1, half), 1)
    new = lax.broadcasted_iota(jnp.int32, (1, rows), 1)
    sink = lax.broadcasted_iota(jnp.int32, (1, window.shape[0] - last), 1)

    def shown(ok):
        return jnp.where(ok, 0.0, MASKED_SCORE)

    bias[:, :half] = shown(slot >= lowest - pre_at * half)
    bias[:, half:fresh] = shown(slot >= lowest - (1 - pre_at) * half)
    bias[:, fresh:last] = shown(new <= token)
    bias[:, last:] = jnp.broadcast_to(shown(sink < SINKS), (rows, window.shape[0] - last))
    for load in loads:
        load.wait()

    def keep(early, late):
        first = pltpu.make_async_copy(
            window.at[pl.ds(early + rows, half - rows)],
            decode.at[pl.ds(0, half - rows)],
            out_sems.at[1],
        )
        second = pltpu.make_async_copy(
            window.at[pl.ds(late, half)], decode.at[pl.ds(half - rows, half)], out_sems.at[2]
        )
        return first, second

    @pl.when(pre_at == 0)
    def _():
        for copy in keep(0, half):
            copy.start()

    @pl.when(pre_at != 0)
    def _():
        for copy in keep(half, 0):
            copy.start()

    scale = HD ** (-0.5)
    for head in range(heads):
        block, at = head // local, head % local * HD
        left = head * span
        scores = lax.dot_general(
            held[block, :rows, at : at + HD],
            window[:, left : left + HD],
            NT,
            preferred_element_type=jnp.float32,
        )
        scores = scores * scale + bias[...]
        top = jnp.max(scores, axis=1, keepdims=True)
        probability = jnp.exp(scores - top)
        below = jnp.sum(probability, axis=1, keepdims=True)
        mixed = jnp.dot(
            probability.astype(jnp.bfloat16),
            window[:, left + HD : left + span],
            preferred_element_type=jnp.float32,
        )
        attended[:, head * HD : (head + 1) * HD] = (mixed / below).astype(jnp.bfloat16)
    tail.wait()

    @pl.when(pre_at == 0)
    def _():
        for copy in keep(0, half):
            copy.wait()

    @pl.when(pre_at != 0)
    def _():
        for copy in keep(half, 0):
            copy.wait()


def attend(prior, parts, cache, fars, sinks):
    rows = 2 * parts.shape[1] // 3
    half, width = cache.shape[1:]
    keys = 2 * half + rows + 128
    return pl.pallas_call(
        attend_kernel,
        out_shape=[
            jax.ShapeDtypeStruct((rows, width // 2), jnp.bfloat16),
            jax.ShapeDtypeStruct((2 * half, width), jnp.bfloat16),
        ],
        in_specs=[
            pl.BlockSpec(memory_space=pltpu.SMEM),
            pl.BlockSpec(memory_space=pltpu.VMEM),
            pl.BlockSpec(memory_space=pl.ANY),
            pl.BlockSpec(memory_space=pl.ANY),
            pl.BlockSpec(memory_space=pl.ANY),
            pl.BlockSpec(memory_space=pltpu.VMEM),
        ],
        out_specs=[
            pl.BlockSpec(memory_space=pltpu.VMEM),
            pl.BlockSpec(memory_space=pl.ANY),
        ],
        scratch_shapes=[
            pltpu.VMEM((keys, width), jnp.bfloat16),
            pltpu.VMEM((rows, keys), jnp.float32),
            pltpu.SemaphoreType.DMA((3,)),
            pltpu.SemaphoreType.DMA((3,)),
        ],
        compiler_params=pltpu.CompilerParams(vmem_limit_bytes=VMEM_BYTES),
        cost_estimate=pl.CostEstimate(
            flops=2 * rows * keys * width,
            bytes_accessed=10_000_000,
            transcendentals=rows * keys * width // (2 * HD),
        ),
        name="attend",
    )(prior, parts, cache, *fars, sinks)


def finish_kernel(*refs):
    pieces, own, far, (out, held, sems) = refs[:4], refs[4:8], refs[8:12], refs[12:]
    core_at = lax.axis_index("mdl") % 2
    depth = own[0].shape[0]
    copies = []
    for step, place in enumerate(mates(lax.axis_index("dec"))):
        rows = pl.ds(pl.multiple_of(lax.rem(place, 2) * depth, depth), depth)
        for row, source in ((near_half(), own[step]), (1 - near_half(), far[step])):
            target = held.at[row, place // 2, rows]
            copies.append(pltpu.make_async_copy(source, target, sems.at[len(copies)]))
    run_all(copies)
    total = None
    for which, piece in enumerate(pieces):
        core = core_at if which < 2 else 1 - core_at
        term = jnp.dot(piece[...], held[which % 2, core], preferred_element_type=jnp.float32)
        total = term if total is None else total + term
    out[...] = total.astype(jnp.bfloat16)


def finish(pieces, own, far):
    rows, depth = pieces[0].shape
    columns = own[0].shape[1]
    return pl.pallas_call(
        finish_kernel,
        out_shape=jax.ShapeDtypeStruct((rows, columns), jnp.bfloat16),
        in_specs=[pl.BlockSpec(memory_space=pltpu.VMEM)] * 4
        + [pl.BlockSpec(memory_space=pl.ANY)] * 8,
        out_specs=pl.BlockSpec(memory_space=pltpu.VMEM),
        scratch_shapes=[
            pltpu.VMEM((2, 2, 2 * own[0].shape[0], columns), jnp.bfloat16),
            pltpu.SemaphoreType.DMA((8,)),
        ],
        compiler_params=pltpu.CompilerParams(vmem_limit_bytes=VMEM_BYTES),
        cost_estimate=pl.CostEstimate(
            flops=8 * rows * depth * columns, bytes_accessed=7_000_000, transcendentals=0
        ),
        name="finish",
    )(*pieces, *own, *far)


def join_kernel(cache, far0, far1, out, held, sems):
    half = held.shape[1]
    part = half - far1.shape[0]
    pre_at = lax.axis_index("pre")
    loads = [
        pltpu.make_async_copy(cache.at[pre_at], held.at[0], sems.at[0]),
        pltpu.make_async_copy(
            far0.at[pl.ds(far0.shape[0] - part, part)], held.at[1, pl.ds(0, part)], sems.at[1]
        ),
        pltpu.make_async_copy(far1, held.at[1, pl.ds(part, half - part)], sems.at[4]),
    ]
    stores = [
        pltpu.make_async_copy(
            held.at[which], out.at[pl.ds(pl.multiple_of(at * half, half), half)], sems.at[2 + which]
        )
        for which, at in enumerate((pre_at, 1 - pre_at))
    ]
    for load in loads:
        load.start()
    loads[0].wait()
    stores[0].start()
    loads[1].wait()
    loads[2].wait()
    stores[1].start()
    for store in stores:
        store.wait()


def join(cache, far0, far1):
    half, width = cache.shape[1:]
    return pl.pallas_call(
        join_kernel,
        out_shape=jax.ShapeDtypeStruct((2 * half, width), jnp.bfloat16),
        in_specs=[pl.BlockSpec(memory_space=pl.ANY)] * 3,
        out_specs=pl.BlockSpec(memory_space=pl.ANY),
        scratch_shapes=[pltpu.VMEM((2, half, width), jnp.bfloat16), pltpu.SemaphoreType.DMA((5,))],
        compiler_params=pltpu.CompilerParams(vmem_limit_bytes=VMEM_BYTES),
        cost_estimate=pl.CostEstimate(
            flops=0, bytes_accessed=8 * half * width, transcendentals=0
        ),
        name="join",
    )(cache, far0, far1)


def split_body(sizes, tokens, norm_gain, w_qkv, w_out, sink_cache, cache_a, cache_b, lengths, groups):
    dec = sizes["dec"]
    rows = tokens.shape[2]
    pre_at, dec_at, mdl_at = (lax.axis_index(name) for name in ("pre", "dec", "mdl"))
    swap = [(0, 1), (1, 0)]
    over_y = [(0, 2), (1, 3), (2, 0), (3, 1)]
    over_core = [(0, 1), (1, 0), (2, 3), (3, 2)]

    def along(step):
        return [(at, (at + step) % dec) for at in range(dec)]

    sent_a, sent_b = (
        lax.dynamic_index_in_dim(cache[:, 0], 1 - pre_at, 0, keepdims=False)
        for cache in (cache_a, cache_b)
    )
    own = tokens.reshape(rows, -1)
    gain = norm_gain.astype(jnp.float32).reshape(sizes["mdl"], 1, -1)

    turned = jnp.transpose(w_qkv, (1, 2, 0)).reshape(3, dec, -1, w_qkv.shape[0])
    turned_qk = jnp.transpose(turned[:2], (1, 0, 2, 3)).reshape(dec, -1, w_qkv.shape[0])
    turned_v = turned[2]
    pairs = [(0, 1), (1, 0), (2, 3), (3, 2)]
    middle = [(1, 2), (2, 1)]
    outward = [(1, 0), (2, 3)]
    in_middle = (dec_at == 1) | (dec_at == 2)

    def over_cores(*values):
        return [lax.ppermute(value, "mdl", over_core) for value in values]

    def pick(middle_got, outer_got):
        return jnp.where(in_middle, middle_got, outer_got)

    where = jnp.stack(mates(dec_at)).astype(jnp.int32)
    cosines, sines = angles(lengths[pre_at], rows)
    cosines, sines = cosines[:, :, 0], sines[:, :, 0]
    cosines = jnp.concatenate([cosines, cosines], axis=-1)
    sines = jnp.concatenate([-sines, sines], axis=-1)
    sinks = jnp.pad(
        lax.dynamic_index_in_dim(sink_cache, groups[pre_at, dec_at], 0, keepdims=False),
        ((0, 16 - SINKS), (0, 0)),
    )
    prior = lengths[pre_at, dec_at].reshape(1)

    edges = lax.optimization_barrier
    half = sent_a.shape[0] // 4 * 3
    mate = lax.ppermute(own, "dec", pairs)
    inner = lax.ppermute(own, "dec", middle)
    y_own = lax.ppermute(own, "mdl", over_y)
    o_far = lax.ppermute(w_out, "pre", swap)
    mate, inner, y_own, o_far, first_w, early_a = edges(
        (mate, inner, y_own, o_far, turned_qk, sent_a[:half])
    )
    first_w = lax.all_to_all(first_w, "dec", 0, 0, tiled=True)
    inner_mate = lax.ppermute(mate, "dec", middle)
    outer = lax.ppermute(inner, "dec", outward)
    y_mate = lax.ppermute(mate, "mdl", over_y)
    far_a0 = lax.ppermute(early_a, "pre", swap)
    core_own = over_cores(own, y_own)
    first_w, inner_mate, outer, y_mate, far_a0, second_w, late_o, *tables = edges(
        (first_w, inner_mate, outer, y_mate, far_a0, turned_v, w_out, where, prior, cosines, sines, sinks)
    )
    where, prior, cosines, sines, sinks = tables
    second_w = lax.all_to_all(second_w, "dec", 0, 0, tiled=True)
    third = pick(inner, outer)
    outer_mate = lax.ppermute(inner_mate, "dec", outward)
    y_third = lax.ppermute(third, "mdl", over_y)
    far_first = lax.ppermute(first_w, "pre", swap)
    o_inner = lax.ppermute(late_o, "dec", middle)
    core_mate = over_cores(mate, y_mate)
    second_w, outer_mate, y_third, far_first, o_inner, late_o = edges(
        (second_w, outer_mate, y_third, far_first, o_inner, late_o)
    )
    far_second = lax.ppermute(second_w, "pre", swap)
    fourth = pick(inner_mate, outer_mate)
    y_fourth = lax.ppermute(fourth, "mdl", over_y)
    *core_third, late_o = edges((*over_cores(third, y_third), late_o))
    o_mate = lax.ppermute(late_o, "dec", pairs)
    near = list(zip(core_own, core_mate, core_third))
    pieces = norm(3, [own, mate, third, y_own, y_mate, y_third, *near[0], *near[1]], gain)
    quarter = sent_b.shape[0] // 4
    late_ab = jnp.concatenate([sent_a[half:], sent_b[:quarter]], axis=0)
    far_second, y_fourth, late_ab, *pieces = edges((far_second, y_fourth, late_ab, *pieces))
    pieces += norm(1, [fourth, y_fourth, *over_cores(fourth, y_fourth)], gain)
    far_ab = lax.ppermute(late_ab, "pre", swap)
    o_outer = lax.ppermute(o_inner, "dec", outward)
    o_inner_mate = lax.ppermute(o_mate, "dec", middle)
    weights = [first_w, far_first, second_w, far_second]

    found = project(where, pieces, weights, cosines, sines)
    found, far_ab, o_outer, o_inner_mate, late_b = edges(
        (found, far_ab, o_outer, o_inner_mate, sent_b[quarter:])
    )
    parts = lax.all_to_all(found, "dec", 0, 0, tiled=True)
    far_b1 = lax.ppermute(late_b, "pre", swap)
    parts, far_b1 = edges((parts, far_b1))
    o_third = pick(o_inner, o_outer)
    o_far_third = lax.ppermute(o_third, "pre", swap)
    o_outer_mate = lax.ppermute(o_inner_mate, "dec", outward)
    attended, decode_a = attend(prior, parts, cache_a[:, 0], (far_a0, far_ab), sinks)
    attended, o_far_third, o_outer_mate, o_far = edges((attended, o_far_third, o_outer_mate, o_far))
    o_fourth = pick(o_inner_mate, o_outer_mate)
    o_far_fourth = lax.ppermute(o_fourth, "pre", swap)
    o_far_mate = lax.ppermute(o_far, "dec", pairs)
    second = lax.ppermute(attended, "mdl", over_y)
    shares = [
        attended,
        second,
        lax.ppermute(attended, "mdl", over_core),
        lax.ppermute(second, "mdl", over_core),
    ]
    attn_out = finish(
        shares,
        [w_out, o_mate, o_third, o_fourth],
        [o_far, o_far_mate, o_far_third, o_far_fourth],
    )
    decode_b = join(cache_b[:, 0], far_ab, far_b1)
    return (attn_out[None, None], decode_a[None, None], decode_b[None, None])


def body(sizes, tokens, norm_gain, w_qkv, w_out, sink_cache, cache_a, cache_b, lengths, groups):
    heads_dev = cache_a.shape[-1] // (2 * HD)
    shapes = (sizes["pre"], sizes["mdl"], sizes["dec"], heads_dev)
    split = shapes == (2, 4, 4, 8) and tokens.shape[0] == 1 and tokens.shape[1] == 1
    args = (tokens, norm_gain, w_qkv, w_out, sink_cache, cache_a, cache_b, lengths, groups)
    return split_body(sizes, *args) if split else general_body(*args)


def solution(mesh):
    placed = (
        P("pre", "dec", None, "mdl"),
        P(),
        P(("pre", "dec"), None, "mdl"),
        P(("pre", "dec"), "mdl"),
        P(None, None, "mdl"),
        P(None, "dec", "pre", "mdl"),
        P(None, "dec", "pre", "mdl"),
        P(),
        P(),
    )
    return jax.shard_map(
        functools.partial(body, dict(mesh.shape)),
        mesh=mesh,
        in_specs=placed,
        out_specs=(
            P("pre", "dec", None, "mdl"),
            P("pre", "dec", None, "mdl"),
            P("pre", "dec", None, "mdl"),
        ),
        check_vma=False,
    )
```

```python
import functools

import jax
import jax.numpy as jnp
from jax import lax
from jax.experimental import pallas as pl
from jax.experimental.pallas import tpu as pltpu
from jax.sharding import PartitionSpec as P

HD = 96
WINDOW = 1024
SINKS = 4


MASKED_SCORE = -1e30


def rotate(vector, cosines, sines):
    halfway = vector.shape[-1] // 2
    first_half = vector[..., :halfway]
    second_half = vector[..., halfway:]
    return jnp.concatenate(
        [first_half * cosines - second_half * sines, second_half * cosines + first_half * sines],
        axis=-1,
    )


def angles(offsets, count):
    halfway = HD // 2
    frequency = 10000.0 ** (-(jnp.arange(halfway).astype(jnp.float32) * 2.0) / HD)
    places = offsets.astype(jnp.float32)[:, None] + jnp.arange(count).astype(jnp.float32)[None, :]
    phases = places[:, :, None] * frequency[None, None, :]
    return (jnp.cos(phases)[:, :, None, :], jnp.sin(phases)[:, :, None, :])


def window_mask(slot_count, fresh_len, prior):
    slot_pos = jnp.arange(slot_count)[None, None, :]
    query_pos = jnp.arange(fresh_len)[None, :, None]
    return (slot_pos >= query_pos + 1) & (slot_pos >= SINKS + WINDOW - prior[:, None, None])


def masked_scores(query, all_keys, key_mask):
    scores = jnp.einsum(
        "rqhd,rkhd->rhqk", query, all_keys, preferred_element_type=jnp.float32
    ) * HD ** (-0.5)
    return jnp.where(key_mask[:, None], scores, MASKED_SCORE)


def partial_terms(scores, key_mask, all_values, row_top):
    probability = jnp.where(key_mask[:, None], jnp.exp(scores - row_top[..., None]), 0.0)
    denominator = jnp.sum(probability, axis=-1)
    numerator = jnp.einsum(
        "rhqk,rkhd->rqhd",
        probability.astype(jnp.bfloat16),
        all_values,
        preferred_element_type=jnp.float32,
    )
    return (numerator, denominator)


def general_body(tokens, norm_gain, w_qkv, w_out, sink_cache, cache_a, cache_b, lengths, groups):
    req_count = tokens.shape[0]
    fresh_len = tokens.shape[2]
    col_width = cache_a.shape[-1] // 2
    heads_dev = col_width // HD
    row_count = req_count * fresh_len
    pre_at = lax.axis_index("pre") * req_count
    dec_at = lax.axis_index("dec")
    gathered = lax.all_gather(tokens, "mdl", axis=3, tiled=True)
    as_float = gathered.reshape(row_count, -1).astype(jnp.float32)
    normed = (
        as_float
        * lax.rsqrt(jnp.mean(as_float * as_float, axis=-1, keepdims=True) + 1e-05)
        * norm_gain.astype(jnp.float32)
    ).astype(jnp.bfloat16)
    shard_rows = lax.all_gather(w_qkv, ("pre", "dec"), axis=0, tiled=True)
    columns = normed
    projected = jnp.dot(
        columns, shard_rows.reshape(shard_rows.shape[0], -1), preferred_element_type=jnp.float32
    )
    projected = projected.reshape(req_count, fresh_len, 3, heads_dev, HD)
    my_len = lax.dynamic_slice(lengths, (pre_at, dec_at), (req_count, 1))[:, 0]
    my_group = lax.dynamic_slice(groups, (pre_at, dec_at), (req_count, 1))[:, 0]
    cosines, sines = angles(my_len, fresh_len)
    query = rotate(projected[:, :, 0], cosines, sines).astype(jnp.bfloat16)
    key_new = rotate(projected[:, :, 1], cosines, sines).astype(jnp.bfloat16)
    value_new = projected[:, :, 2].astype(jnp.bfloat16)
    onehot = (my_group[:, None] == jnp.arange(sink_cache.shape[0])[None, :]).astype(jnp.float32)
    sink_rows = jnp.einsum("rg,gsc->rsc", onehot, sink_cache.astype(jnp.float32)).astype(
        jnp.bfloat16
    )
    sink_rows = sink_rows.reshape(req_count, SINKS, heads_dev, 2, HD)
    sink_keys = sink_rows[:, :, :, 0]
    sink_values = sink_rows[:, :, :, 1]
    sink_ok = jnp.ones((req_count, fresh_len, SINKS), dtype=bool)
    recent_ok = jnp.arange(fresh_len)[None, None, :] <= jnp.arange(fresh_len)[None, :, None]
    moved_a, moved_b = (
        lax.all_to_all(cache_a, "pre", split_axis=0, concat_axis=2, tiled=True),
        lax.all_to_all(cache_b, "pre", split_axis=0, concat_axis=2, tiled=True),
    )
    full_window = moved_a[:, 0].reshape(req_count, -1, heads_dev, 2, HD)
    window_keys = full_window[:, :, :, 0]
    window_values = full_window[:, :, :, 1]
    all_keys = jnp.concatenate([sink_keys, window_keys, key_new], axis=1)
    all_values = jnp.concatenate([sink_values, window_values, value_new], axis=1)
    far_mask = window_mask(WINDOW, fresh_len, my_len)
    key_mask = jnp.concatenate([sink_ok, far_mask, recent_ok], axis=2)
    scores = masked_scores(query, all_keys, key_mask)
    row_top = jnp.max(scores, axis=-1)
    numerator, denominator = partial_terms(scores, key_mask, all_values, row_top)
    attended = (
        (numerator / jnp.transpose(denominator, (0, 2, 1))[..., None])
        .astype(jnp.bfloat16)
        .reshape(row_count, col_width)
    )
    every_head = lax.all_gather(attended, "mdl", axis=1, tiled=True)
    columns = every_head
    output_rows = jnp.dot(
        columns,
        lax.all_gather(w_out, ("pre", "dec"), axis=0, tiled=True),
        preferred_element_type=jnp.float32,
    )
    attn_out = output_rows.astype(jnp.bfloat16).reshape(req_count, 1, fresh_len, -1)
    fresh_kv = jnp.stack([key_new, value_new], axis=3).reshape(req_count, fresh_len, 2 * col_width)[
        :, None
    ]
    decode_a = jnp.concatenate([moved_a[:, :, fresh_len:], fresh_kv], axis=2)
    return (attn_out, decode_a, moved_b)


VMEM_BYTES = 56 * 1024 * 1024
NT = (((1,), (1,)), ((), ()))


def mates(at):
    return [at, at + 1 - 2 * lax.rem(at, 2), 2 - at // 2, 3 - 3 * (at // 2)]


def near_half():
    return jnp.where(lax.axis_index("mdl") // 2 == lax.axis_index("pre"), 0, 1)


def run_all(copies):
    for copy in copies:
        copy.start()
    for copy in copies:
        copy.wait()


def feature_place(which):
    row, core = lax.axis_index("mdl") // 2, lax.axis_index("mdl") % 2
    row = row if which in (0, 2) else 1 - row
    core = core if which < 2 else 1 - core
    return row * 2 + core, core


def normed_parts(parts, gain):
    parts = [part.astype(jnp.float32) for part in parts]
    squares = sum(jnp.sum(part * part, axis=1, keepdims=True) for part in parts)
    scale = lax.rsqrt(squares / (4 * parts[0].shape[1]) + 1e-05)
    return [
        (part * scale * gain[feature_place(which)[0]]).astype(jnp.bfloat16)
        for which, part in enumerate(parts)
    ]


def norm_kernel(count, *refs):
    pieces, (gain, *outs) = refs[:-5], refs[-5:]
    rows = pieces[0].shape[0]
    for slot in range(count):
        parts = normed_parts([pieces[which * count + slot][...] for which in range(4)], gain)
        for which, part in enumerate(parts):
            outs[which][slot * rows : (slot + 1) * rows] = part


def norm(count, pieces, gain):
    rows, depth = pieces[0].shape
    space = pl.BlockSpec(memory_space=pltpu.VMEM)
    return pl.pallas_call(
        functools.partial(norm_kernel, count),
        out_shape=[jax.ShapeDtypeStruct((count * rows, depth), jnp.bfloat16)] * 4,
        in_specs=[space] * (len(pieces) + 1),
        out_specs=[space] * 4,
        compiler_params=pltpu.CompilerParams(vmem_limit_bytes=VMEM_BYTES),
        cost_estimate=pl.CostEstimate(
            flops=24 * count * rows * depth, bytes_accessed=16 * count * rows * depth, transcendentals=0
        ),
        name="norm",
    )(*pieces, gain)


def project_kernel(*refs):
    where, weights, gain = refs[0], refs[9:13], refs[13]
    cosines, sines, out, held_qk, held_v, sems = refs[14:]
    early, depth = weights[0].shape[1:]
    late = held_qk.shape[2] - early
    copies = []
    for which, source in enumerate(weights):
        row = near_half() if which % 2 == 0 else 1 - near_half()
        for place in range(4):
            block = pl.ds(place % 2 * depth, depth)
            if which < 2:
                moves = [(source.at[place], held_qk.at[row, place // 2, pl.ds(0, early), block])]
            else:
                moves = [
                    (source.at[place, pl.ds(0, late)], held_qk.at[row, place // 2, pl.ds(early, late), block]),
                    (source.at[place, pl.ds(late, early - late)], held_v.at[row, place // 2, :, block]),
                ]
            for one, two in moves:
                copies.append(pltpu.make_async_copy(one, two, sems.at[len(copies)]))
    run_all(copies)
    rows, columns = refs[5].shape[0], held_qk.shape[2]
    width = columns // 2
    lane = lax.broadcasted_iota(jnp.int32, (1, columns), 1)
    in_first = lane % HD < HD // 2
    first = 0
    groups = (
        [piece[...] for piece in refs[1:5]],
        normed_parts([piece[...] for piece in refs[5:9]], gain),
    )
    for pieces in groups:
        count = pieces[0].shape[0] // rows
        turning, values = (
            sum(
                lax.dot_general(
                    piece,
                    held[which % 2, feature_place(which)[1]],
                    NT,
                    preferred_element_type=jnp.float32,
                )
                for which, piece in enumerate(pieces)
            )
            for held in (held_qk, held_v)
        )
        for slot in range(count):
            at = where[first + slot]
            turned = turning[slot * rows : (slot + 1) * rows]
            ahead = pltpu.roll(turned, columns - HD // 2, 1)
            behind = pltpu.roll(turned, HD // 2, 1)
            cosine, sine = (
                jnp.concatenate([table[at]] * (columns // HD), axis=1) for table in (cosines, sines)
            )
            turned = turned * cosine + jnp.where(in_first, ahead, behind) * sine
            out[at, :rows] = turned.astype(jnp.bfloat16)
            value = values[slot * rows : (slot + 1) * rows].astype(jnp.bfloat16)
            for row in range(2):
                out[at, rows:, row * width : (row + 1) * width] = value[
                    row * rows // 2 : (row + 1) * rows // 2
                ]
        first += count


def project(where, pieces, weights, gain, cosines, sines):
    rows, depth = cosines.shape[1], weights[0].shape[2]
    columns = 4 * weights[0].shape[1] // 3
    width = columns // 2
    return pl.pallas_call(
        project_kernel,
        out_shape=jax.ShapeDtypeStruct((4, rows + rows // 2, columns), jnp.bfloat16),
        in_specs=[pl.BlockSpec(memory_space=pltpu.SMEM)]
        + [pl.BlockSpec(memory_space=pltpu.VMEM)] * 8
        + [pl.BlockSpec(memory_space=pl.ANY)] * 4
        + [pl.BlockSpec(memory_space=pltpu.VMEM)] * 3,
        out_specs=pl.BlockSpec(memory_space=pltpu.VMEM),
        scratch_shapes=[
            pltpu.VMEM((2, 2, columns, 2 * depth), jnp.bfloat16),
            pltpu.VMEM((2, 2, width, 2 * depth), jnp.bfloat16),
            pltpu.SemaphoreType.DMA((24,)),
        ],
        compiler_params=pltpu.CompilerParams(vmem_limit_bytes=VMEM_BYTES),
        cost_estimate=pl.CostEstimate(
            flops=8 * rows * 8 * depth * (columns + width),
            bytes_accessed=16_000_000,
            transcendentals=0,
        ),
        name="project",
    )(where, *pieces, *weights, gain, cosines, sines)


def attend_kernel(
    prior, held, cache, far0, far1, sinks, attended, decode, window, bias, sems, out_sems
):
    pre_at = lax.axis_index("pre")
    rows, half = attended.shape[0], cache.shape[1]
    fresh, last = 2 * half, 2 * half + rows
    loads = [
        pltpu.make_async_copy(cache.at[pre_at], window.at[pl.ds(0, half)], sems.at[0]),
        pltpu.make_async_copy(far0, window.at[pl.ds(half, far0.shape[0])], sems.at[1]),
        pltpu.make_async_copy(
            far1.at[pl.ds(0, half - far0.shape[0])],
            window.at[pl.ds(half + far0.shape[0], half - far0.shape[0])],
            sems.at[2],
        ),
    ]
    for load in loads:
        load.start()
    span = 2 * HD
    heads = cache.shape[2] // span
    local = heads // 4
    for head in range(heads):
        block, at = head // local, head % local
        left = head * span
        start = (local + at) * HD
        window[fresh:last, left : left + HD] = held[block, :rows, start : start + HD]
        for row in range(2):
            start = row * local * HD + at * HD
            window[
                fresh + row * rows // 2 : fresh + (row + 1) * rows // 2, left + HD : left + span
            ] = held[block, rows:, start : start + HD]
    window[last:] = jnp.zeros((window.shape[0] - last, window.shape[1]), window.dtype)
    window[last : last + sinks.shape[0]] = sinks[...]
    tail = pltpu.make_async_copy(
        window.at[pl.ds(fresh, rows)], decode.at[pl.ds(2 * half - rows, rows)], out_sems.at[0]
    )
    tail.start()
    token = lax.broadcasted_iota(jnp.int32, (rows, 1), 0)
    lowest = jnp.maximum(token + 1, SINKS + 2 * half - prior[0])
    slot = lax.broadcasted_iota(jnp.int32, (1, half), 1)
    new = lax.broadcasted_iota(jnp.int32, (1, rows), 1)
    sink = lax.broadcasted_iota(jnp.int32, (1, window.shape[0] - last), 1)

    def shown(ok):
        return jnp.where(ok, 0.0, MASKED_SCORE)

    bias[:, :half] = shown(slot >= lowest - pre_at * half)
    bias[:, half:fresh] = shown(slot >= lowest - (1 - pre_at) * half)
    bias[:, fresh:last] = shown(new <= token)
    bias[:, last:] = jnp.broadcast_to(shown(sink < SINKS), (rows, window.shape[0] - last))
    for load in loads:
        load.wait()

    def keep(early, late):
        first = pltpu.make_async_copy(
            window.at[pl.ds(early + rows, half - rows)],
            decode.at[pl.ds(0, half - rows)],
            out_sems.at[1],
        )
        second = pltpu.make_async_copy(
            window.at[pl.ds(late, half)], decode.at[pl.ds(half - rows, half)], out_sems.at[2]
        )
        return first, second

    @pl.when(pre_at == 0)
    def _():
        for copy in keep(0, half):
            copy.start()

    @pl.when(pre_at != 0)
    def _():
        for copy in keep(half, 0):
            copy.start()

    scale = HD ** (-0.5)
    for head in range(heads):
        block, at = head // local, head % local * HD
        left = head * span
        scores = lax.dot_general(
            held[block, :rows, at : at + HD],
            window[:, left : left + HD],
            NT,
            preferred_element_type=jnp.float32,
        )
        scores = scores * scale + bias[...]
        top = jnp.max(scores, axis=1, keepdims=True)
        probability = jnp.exp(scores - top)
        below = jnp.sum(probability, axis=1, keepdims=True)
        mixed = jnp.dot(
            probability.astype(jnp.bfloat16),
            window[:, left + HD : left + span],
            preferred_element_type=jnp.float32,
        )
        attended[:, head * HD : (head + 1) * HD] = (mixed / below).astype(jnp.bfloat16)
    tail.wait()

    @pl.when(pre_at == 0)
    def _():
        for copy in keep(0, half):
            copy.wait()

    @pl.when(pre_at != 0)
    def _():
        for copy in keep(half, 0):
            copy.wait()


def attend(prior, parts, cache, fars, sinks):
    rows = 2 * parts.shape[1] // 3
    half, width = cache.shape[1:]
    keys = 2 * half + rows + 128
    return pl.pallas_call(
        attend_kernel,
        out_shape=[
            jax.ShapeDtypeStruct((rows, width // 2), jnp.bfloat16),
            jax.ShapeDtypeStruct((2 * half, width), jnp.bfloat16),
        ],
        in_specs=[
            pl.BlockSpec(memory_space=pltpu.SMEM),
            pl.BlockSpec(memory_space=pltpu.VMEM),
            pl.BlockSpec(memory_space=pl.ANY),
            pl.BlockSpec(memory_space=pl.ANY),
            pl.BlockSpec(memory_space=pl.ANY),
            pl.BlockSpec(memory_space=pltpu.VMEM),
        ],
        out_specs=[
            pl.BlockSpec(memory_space=pltpu.VMEM),
            pl.BlockSpec(memory_space=pl.ANY),
        ],
        scratch_shapes=[
            pltpu.VMEM((keys, width), jnp.bfloat16),
            pltpu.VMEM((rows, keys), jnp.float32),
            pltpu.SemaphoreType.DMA((3,)),
            pltpu.SemaphoreType.DMA((3,)),
        ],
        compiler_params=pltpu.CompilerParams(vmem_limit_bytes=VMEM_BYTES),
        cost_estimate=pl.CostEstimate(
            flops=2 * rows * keys * width,
            bytes_accessed=10_000_000,
            transcendentals=rows * keys * width // (2 * HD),
        ),
        name="attend",
    )(prior, parts, cache, *fars, sinks)


def finish_kernel(*refs):
    pieces, own, far, (out, held, sems) = refs[:4], refs[4:8], refs[8:12], refs[12:]
    core_at = lax.axis_index("mdl") % 2
    depth = own[0].shape[0]
    copies = []
    for step, place in enumerate(mates(lax.axis_index("dec"))):
        rows = pl.ds(pl.multiple_of(lax.rem(place, 2) * depth, depth), depth)
        for row, source in ((near_half(), own[step]), (1 - near_half(), far[step])):
            target = held.at[row, place // 2, rows]
            copies.append(pltpu.make_async_copy(source, target, sems.at[len(copies)]))
    run_all(copies)
    total = None
    for which, piece in enumerate(pieces):
        core = core_at if which < 2 else 1 - core_at
        term = jnp.dot(piece[...], held[which % 2, core], preferred_element_type=jnp.float32)
        total = term if total is None else total + term
    out[...] = total.astype(jnp.bfloat16)


def finish(pieces, own, far):
    rows, depth = pieces[0].shape
    columns = own[0].shape[1]
    return pl.pallas_call(
        finish_kernel,
        out_shape=jax.ShapeDtypeStruct((rows, columns), jnp.bfloat16),
        in_specs=[pl.BlockSpec(memory_space=pltpu.VMEM)] * 4
        + [pl.BlockSpec(memory_space=pl.ANY)] * 8,
        out_specs=pl.BlockSpec(memory_space=pltpu.VMEM),
        scratch_shapes=[
            pltpu.VMEM((2, 2, 2 * own[0].shape[0], columns), jnp.bfloat16),
            pltpu.SemaphoreType.DMA((8,)),
        ],
        compiler_params=pltpu.CompilerParams(vmem_limit_bytes=VMEM_BYTES),
        cost_estimate=pl.CostEstimate(
            flops=8 * rows * depth * columns, bytes_accessed=7_000_000, transcendentals=0
        ),
        name="finish",
    )(*pieces, *own, *far)


def join_kernel(cache, far0, far1, out, held, sems):
    half = held.shape[1]
    part = half - far1.shape[0]
    pre_at = lax.axis_index("pre")
    loads = [
        pltpu.make_async_copy(cache.at[pre_at], held.at[0], sems.at[0]),
        pltpu.make_async_copy(
            far0.at[pl.ds(far0.shape[0] - part, part)], held.at[1, pl.ds(0, part)], sems.at[1]
        ),
        pltpu.make_async_copy(far1, held.at[1, pl.ds(part, half - part)], sems.at[4]),
    ]
    stores = [
        pltpu.make_async_copy(
            held.at[which], out.at[pl.ds(pl.multiple_of(at * half, half), half)], sems.at[2 + which]
        )
        for which, at in enumerate((pre_at, 1 - pre_at))
    ]
    for load in loads:
        load.start()
    loads[0].wait()
    stores[0].start()
    loads[1].wait()
    loads[2].wait()
    stores[1].start()
    for store in stores:
        store.wait()


def join(cache, far0, far1):
    half, width = cache.shape[1:]
    return pl.pallas_call(
        join_kernel,
        out_shape=jax.ShapeDtypeStruct((2 * half, width), jnp.bfloat16),
        in_specs=[pl.BlockSpec(memory_space=pl.ANY)] * 3,
        out_specs=pl.BlockSpec(memory_space=pl.ANY),
        scratch_shapes=[pltpu.VMEM((2, half, width), jnp.bfloat16), pltpu.SemaphoreType.DMA((5,))],
        compiler_params=pltpu.CompilerParams(vmem_limit_bytes=VMEM_BYTES),
        cost_estimate=pl.CostEstimate(
            flops=0, bytes_accessed=8 * half * width, transcendentals=0
        ),
        name="join",
    )(cache, far0, far1)


def split_body(sizes, tokens, norm_gain, w_qkv, w_out, sink_cache, cache_a, cache_b, lengths, groups):
    dec = sizes["dec"]
    rows = tokens.shape[2]
    pre_at, dec_at, mdl_at = (lax.axis_index(name) for name in ("pre", "dec", "mdl"))
    swap = [(0, 1), (1, 0)]
    over_y = [(0, 2), (1, 3), (2, 0), (3, 1)]
    over_core = [(0, 1), (1, 0), (2, 3), (3, 2)]

    def along(step):
        return [(at, (at + step) % dec) for at in range(dec)]

    sent_a, sent_b = (
        lax.dynamic_index_in_dim(cache[:, 0], 1 - pre_at, 0, keepdims=False)
        for cache in (cache_a, cache_b)
    )
    own = tokens.reshape(rows, -1)
    gain = norm_gain.astype(jnp.float32).reshape(sizes["mdl"], 1, -1)

    turned = jnp.transpose(w_qkv, (1, 2, 0)).reshape(3, dec, -1, w_qkv.shape[0])
    turned = jnp.transpose(turned, (1, 0, 2, 3)).reshape(dec, -1, w_qkv.shape[0])
    split = turned.shape[1] // 2
    pairs = [(0, 1), (1, 0), (2, 3), (3, 2)]
    middle = [(1, 2), (2, 1)]
    outward = [(1, 0), (2, 3)]
    in_middle = (dec_at == 1) | (dec_at == 2)

    def over_cores(*values):
        return [lax.ppermute(value, "mdl", over_core) for value in values]

    def pick(middle_got, outer_got):
        return jnp.where(in_middle, middle_got, outer_got)

    where = jnp.stack(mates(dec_at)).astype(jnp.int32)
    cosines, sines = angles(lengths[pre_at], rows)
    cosines, sines = cosines[:, :, 0], sines[:, :, 0]
    cosines = jnp.concatenate([cosines, cosines], axis=-1)
    sines = jnp.concatenate([-sines, sines], axis=-1)
    sinks = jnp.pad(
        lax.dynamic_index_in_dim(sink_cache, groups[pre_at, dec_at], 0, keepdims=False),
        ((0, 16 - SINKS), (0, 0)),
    )
    prior = lengths[pre_at, dec_at].reshape(1)

    edges = lax.optimization_barrier
    half = sent_a.shape[0] // 4 * 3
    mate = lax.ppermute(own, "dec", pairs)
    inner = lax.ppermute(own, "dec", middle)
    y_own = lax.ppermute(own, "mdl", over_y)
    o_far = lax.ppermute(w_out, "pre", swap)
    mate, inner, y_own, o_far, first_w, early_a = edges(
        (mate, inner, y_own, o_far, turned[:, :split], sent_a[:half])
    )
    first_w = lax.all_to_all(first_w, "dec", 0, 0, tiled=True)
    inner_mate = lax.ppermute(mate, "dec", middle)
    outer = lax.ppermute(inner, "dec", outward)
    y_mate = lax.ppermute(mate, "mdl", over_y)
    far_a0 = lax.ppermute(early_a, "pre", swap)
    core_own = over_cores(own, y_own)
    first_w, inner_mate, outer, y_mate, far_a0, second_w, late_o, *tables = edges(
        (first_w, inner_mate, outer, y_mate, far_a0, turned[:, split:], w_out, where, prior, cosines, sines, sinks)
    )
    where, prior, cosines, sines, sinks = tables
    second_w = lax.all_to_all(second_w, "dec", 0, 0, tiled=True)
    third = pick(inner, outer)
    outer_mate = lax.ppermute(inner_mate, "dec", outward)
    y_third = lax.ppermute(third, "mdl", over_y)
    far_first = lax.ppermute(first_w, "pre", swap)
    core_mate = over_cores(mate, y_mate)
    second_w, outer_mate, y_third, far_first, late_o = edges(
        (second_w, outer_mate, y_third, far_first, late_o)
    )
    far_second = lax.ppermute(second_w, "pre", swap)
    fourth = pick(inner_mate, outer_mate)
    y_fourth = lax.ppermute(fourth, "mdl", over_y)
    *core_third, late_o = edges((*over_cores(third, y_third), late_o))
    o_mate = lax.ppermute(late_o, "dec", pairs)
    o_inner = lax.ppermute(late_o, "dec", middle)
    near = list(zip(core_own, core_mate, core_third))
    pieces = norm(3, [own, mate, third, y_own, y_mate, y_third, *near[0], *near[1]], gain)
    quarter = sent_b.shape[0] // 4
    late_ab = jnp.concatenate([sent_a[half:], sent_b[:quarter]], axis=0)
    far_second, y_fourth, late_ab, *pieces = edges((far_second, y_fourth, late_ab, *pieces))
    pieces += [fourth, y_fourth, *over_cores(fourth, y_fourth)]
    far_ab = lax.ppermute(late_ab, "pre", swap)
    o_outer = lax.ppermute(o_inner, "dec", outward)
    o_inner_mate = lax.ppermute(o_mate, "dec", middle)
    weights = [first_w, far_first, second_w, far_second]

    found = project(where, pieces, weights, gain, cosines, sines)
    found, far_ab, o_outer, o_inner_mate, late_b = edges(
        (found, far_ab, o_outer, o_inner_mate, sent_b[quarter:])
    )
    parts = lax.all_to_all(found, "dec", 0, 0, tiled=True)
    far_b1 = lax.ppermute(late_b, "pre", swap)
    parts, far_b1 = edges((parts, far_b1))
    o_third = pick(o_inner, o_outer)
    o_far_third = lax.ppermute(o_third, "pre", swap)
    o_outer_mate = lax.ppermute(o_inner_mate, "dec", outward)
    attended, decode_a = attend(prior, parts, cache_a[:, 0], (far_a0, far_ab), sinks)
    attended, o_far_third, o_outer_mate, o_far = edges((attended, o_far_third, o_outer_mate, o_far))
    o_fourth = pick(o_inner_mate, o_outer_mate)
    o_far_fourth = lax.ppermute(o_fourth, "pre", swap)
    o_far_mate = lax.ppermute(o_far, "dec", pairs)
    second = lax.ppermute(attended, "mdl", over_y)
    shares = [
        attended,
        second,
        lax.ppermute(attended, "mdl", over_core),
        lax.ppermute(second, "mdl", over_core),
    ]
    attn_out = finish(
        shares,
        [w_out, o_mate, o_third, o_fourth],
        [o_far, o_far_mate, o_far_third, o_far_fourth],
    )
    decode_b = join(cache_b[:, 0], far_ab, far_b1)
    return (attn_out[None, None], decode_a[None, None], decode_b[None, None])


def body(sizes, tokens, norm_gain, w_qkv, w_out, sink_cache, cache_a, cache_b, lengths, groups):
    heads_dev = cache_a.shape[-1] // (2 * HD)
    shapes = (sizes["pre"], sizes["mdl"], sizes["dec"], heads_dev)
    split = shapes == (2, 4, 4, 8) and tokens.shape[0] == 1 and tokens.shape[1] == 1
    args = (tokens, norm_gain, w_qkv, w_out, sink_cache, cache_a, cache_b, lengths, groups)
    return split_body(sizes, *args) if split else general_body(*args)


def solution(mesh):
    placed = (
        P("pre", "dec", None, "mdl"),
        P(),
        P(("pre", "dec"), None, "mdl"),
        P(("pre", "dec"), "mdl"),
        P(None, None, "mdl"),
        P(None, "dec", "pre", "mdl"),
        P(None, "dec", "pre", "mdl"),
        P(),
        P(),
    )
    return jax.shard_map(
        functools.partial(body, dict(mesh.shape)),
        mesh=mesh,
        in_specs=placed,
        out_specs=(
            P("pre", "dec", None, "mdl"),
            P("pre", "dec", None, "mdl"),
            P("pre", "dec", None, "mdl"),
        ),
        check_vma=False,
    )
```

```python
import functools

import jax
import jax.numpy as jnp
from jax import lax
from jax.experimental import pallas as pl
from jax.experimental.pallas import tpu as pltpu
from jax.sharding import PartitionSpec as P

HD = 96
WINDOW = 1024
SINKS = 4


MASKED_SCORE = -1e30


def rotate(vector, cosines, sines):
    halfway = vector.shape[-1] // 2
    first_half = vector[..., :halfway]
    second_half = vector[..., halfway:]
    return jnp.concatenate(
        [first_half * cosines - second_half * sines, second_half * cosines + first_half * sines],
        axis=-1,
    )


def angles(offsets, count):
    halfway = HD // 2
    frequency = 10000.0 ** (-(jnp.arange(halfway).astype(jnp.float32) * 2.0) / HD)
    places = offsets.astype(jnp.float32)[:, None] + jnp.arange(count).astype(jnp.float32)[None, :]
    phases = places[:, :, None] * frequency[None, None, :]
    return (jnp.cos(phases)[:, :, None, :], jnp.sin(phases)[:, :, None, :])


def window_mask(slot_count, fresh_len, prior):
    slot_pos = jnp.arange(slot_count)[None, None, :]
    query_pos = jnp.arange(fresh_len)[None, :, None]
    return (slot_pos >= query_pos + 1) & (slot_pos >= SINKS + WINDOW - prior[:, None, None])


def masked_scores(query, all_keys, key_mask):
    scores = jnp.einsum(
        "rqhd,rkhd->rhqk", query, all_keys, preferred_element_type=jnp.float32
    ) * HD ** (-0.5)
    return jnp.where(key_mask[:, None], scores, MASKED_SCORE)


def partial_terms(scores, key_mask, all_values, row_top):
    probability = jnp.where(key_mask[:, None], jnp.exp(scores - row_top[..., None]), 0.0)
    denominator = jnp.sum(probability, axis=-1)
    numerator = jnp.einsum(
        "rhqk,rkhd->rqhd",
        probability.astype(jnp.bfloat16),
        all_values,
        preferred_element_type=jnp.float32,
    )
    return (numerator, denominator)


def general_body(tokens, norm_gain, w_qkv, w_out, sink_cache, cache_a, cache_b, lengths, groups):
    req_count = tokens.shape[0]
    fresh_len = tokens.shape[2]
    col_width = cache_a.shape[-1] // 2
    heads_dev = col_width // HD
    row_count = req_count * fresh_len
    pre_at = lax.axis_index("pre") * req_count
    dec_at = lax.axis_index("dec")
    gathered = lax.all_gather(tokens, "mdl", axis=3, tiled=True)
    as_float = gathered.reshape(row_count, -1).astype(jnp.float32)
    normed = (
        as_float
        * lax.rsqrt(jnp.mean(as_float * as_float, axis=-1, keepdims=True) + 1e-05)
        * norm_gain.astype(jnp.float32)
    ).astype(jnp.bfloat16)
    shard_rows = lax.all_gather(w_qkv, ("pre", "dec"), axis=0, tiled=True)
    columns = normed
    projected = jnp.dot(
        columns, shard_rows.reshape(shard_rows.shape[0], -1), preferred_element_type=jnp.float32
    )
    projected = projected.reshape(req_count, fresh_len, 3, heads_dev, HD)
    my_len = lax.dynamic_slice(lengths, (pre_at, dec_at), (req_count, 1))[:, 0]
    my_group = lax.dynamic_slice(groups, (pre_at, dec_at), (req_count, 1))[:, 0]
    cosines, sines = angles(my_len, fresh_len)
    query = rotate(projected[:, :, 0], cosines, sines).astype(jnp.bfloat16)
    key_new = rotate(projected[:, :, 1], cosines, sines).astype(jnp.bfloat16)
    value_new = projected[:, :, 2].astype(jnp.bfloat16)
    onehot = (my_group[:, None] == jnp.arange(sink_cache.shape[0])[None, :]).astype(jnp.float32)
    sink_rows = jnp.einsum("rg,gsc->rsc", onehot, sink_cache.astype(jnp.float32)).astype(
        jnp.bfloat16
    )
    sink_rows = sink_rows.reshape(req_count, SINKS, heads_dev, 2, HD)
    sink_keys = sink_rows[:, :, :, 0]
    sink_values = sink_rows[:, :, :, 1]
    sink_ok = jnp.ones((req_count, fresh_len, SINKS), dtype=bool)
    recent_ok = jnp.arange(fresh_len)[None, None, :] <= jnp.arange(fresh_len)[None, :, None]
    moved_a, moved_b = (
        lax.all_to_all(cache_a, "pre", split_axis=0, concat_axis=2, tiled=True),
        lax.all_to_all(cache_b, "pre", split_axis=0, concat_axis=2, tiled=True),
    )
    full_window = moved_a[:, 0].reshape(req_count, -1, heads_dev, 2, HD)
    window_keys = full_window[:, :, :, 0]
    window_values = full_window[:, :, :, 1]
    all_keys = jnp.concatenate([sink_keys, window_keys, key_new], axis=1)
    all_values = jnp.concatenate([sink_values, window_values, value_new], axis=1)
    far_mask = window_mask(WINDOW, fresh_len, my_len)
    key_mask = jnp.concatenate([sink_ok, far_mask, recent_ok], axis=2)
    scores = masked_scores(query, all_keys, key_mask)
    row_top = jnp.max(scores, axis=-1)
    numerator, denominator = partial_terms(scores, key_mask, all_values, row_top)
    attended = (
        (numerator / jnp.transpose(denominator, (0, 2, 1))[..., None])
        .astype(jnp.bfloat16)
        .reshape(row_count, col_width)
    )
    every_head = lax.all_gather(attended, "mdl", axis=1, tiled=True)
    columns = every_head
    output_rows = jnp.dot(
        columns,
        lax.all_gather(w_out, ("pre", "dec"), axis=0, tiled=True),
        preferred_element_type=jnp.float32,
    )
    attn_out = output_rows.astype(jnp.bfloat16).reshape(req_count, 1, fresh_len, -1)
    fresh_kv = jnp.stack([key_new, value_new], axis=3).reshape(req_count, fresh_len, 2 * col_width)[
        :, None
    ]
    decode_a = jnp.concatenate([moved_a[:, :, fresh_len:], fresh_kv], axis=2)
    return (attn_out, decode_a, moved_b)


VMEM_BYTES = 56 * 1024 * 1024
NT = (((1,), (1,)), ((), ()))


def mates(at):
    return [at, at + 1 - 2 * lax.rem(at, 2), 2 - at // 2, 3 - 3 * (at // 2)]


def near_half():
    return jnp.where(lax.axis_index("mdl") // 2 == lax.axis_index("pre"), 0, 1)


def run_all(copies):
    for copy in copies:
        copy.start()
    for copy in copies:
        copy.wait()


def feature_place(which):
    row, core = lax.axis_index("mdl") // 2, lax.axis_index("mdl") % 2
    row = row if which in (0, 2) else 1 - row
    core = core if which < 2 else 1 - core
    return row * 2 + core, core


def normed_parts(parts, gain):
    parts = [part.astype(jnp.float32) for part in parts]
    squares = sum(jnp.sum(part * part, axis=1, keepdims=True) for part in parts)
    scale = lax.rsqrt(squares / (4 * parts[0].shape[1]) + 1e-05)
    return [
        (part * scale * gain[feature_place(which)[0]]).astype(jnp.bfloat16)
        for which, part in enumerate(parts)
    ]


def norm_kernel(count, *refs):
    pieces, (gain, *outs) = refs[:-5], refs[-5:]
    rows = pieces[0].shape[0]
    for slot in range(count):
        parts = normed_parts([pieces[which * count + slot][...] for which in range(4)], gain)
        for which, part in enumerate(parts):
            outs[which][slot * rows : (slot + 1) * rows] = part


def norm(count, pieces, gain):
    rows, depth = pieces[0].shape
    space = pl.BlockSpec(memory_space=pltpu.VMEM)
    return pl.pallas_call(
        functools.partial(norm_kernel, count),
        out_shape=[jax.ShapeDtypeStruct((count * rows, depth), jnp.bfloat16)] * 4,
        in_specs=[space] * (len(pieces) + 1),
        out_specs=[space] * 4,
        compiler_params=pltpu.CompilerParams(vmem_limit_bytes=VMEM_BYTES),
        cost_estimate=pl.CostEstimate(
            flops=24 * count * rows * depth, bytes_accessed=16 * count * rows * depth, transcendentals=0
        ),
        name="norm",
    )(*pieces, gain)


def project_kernel(*refs):
    where, weights, gain = refs[0], refs[9:13], refs[13]
    cosines, sines, out, held_qk, held_v, sems = refs[14:]
    early, depth = weights[0].shape[1:]
    late = held_qk.shape[2] - early
    copies = []
    for which, source in enumerate(weights):
        row = near_half() if which % 2 == 0 else 1 - near_half()
        for place in range(4):
            block = pl.ds(place % 2 * depth, depth)
            if which < 2:
                moves = [(source.at[place], held_qk.at[row, place // 2, pl.ds(0, early), block])]
            else:
                moves = [
                    (source.at[place, pl.ds(0, late)], held_qk.at[row, place // 2, pl.ds(early, late), block]),
                    (source.at[place, pl.ds(late, early - late)], held_v.at[row, place // 2, :, block]),
                ]
            for one, two in moves:
                copies.append(pltpu.make_async_copy(one, two, sems.at[len(copies)]))
    run_all(copies)
    rows, columns = refs[5].shape[0], held_qk.shape[2]
    width = columns // 2
    lane = lax.broadcasted_iota(jnp.int32, (1, columns), 1)
    in_first = lane % HD < HD // 2
    first = 0
    groups = (
        [piece[...] for piece in refs[1:5]],
        normed_parts([piece[...] for piece in refs[5:9]], gain),
    )
    for pieces in groups:
        count = pieces[0].shape[0] // rows
        turning, values = (
            sum(
                lax.dot_general(
                    piece,
                    held[which % 2, feature_place(which)[1]],
                    NT,
                    preferred_element_type=jnp.float32,
                )
                for which, piece in enumerate(pieces)
            )
            for held in (held_qk, held_v)
        )
        for slot in range(count):
            at = where[first + slot]
            turned = turning[slot * rows : (slot + 1) * rows]
            ahead = pltpu.roll(turned, columns - HD // 2, 1)
            behind = pltpu.roll(turned, HD // 2, 1)
            cosine, sine = (
                jnp.concatenate([table[at]] * (columns // HD), axis=1) for table in (cosines, sines)
            )
            turned = turned * cosine + jnp.where(in_first, ahead, behind) * sine
            out[at, :rows] = turned.astype(jnp.bfloat16)
            value = values[slot * rows : (slot + 1) * rows].astype(jnp.bfloat16)
            for row in range(2):
                out[at, rows:, row * width : (row + 1) * width] = value[
                    row * rows // 2 : (row + 1) * rows // 2
                ]
        first += count


def project(where, pieces, weights, gain, cosines, sines):
    rows, depth = cosines.shape[1], weights[0].shape[2]
    columns = 4 * weights[0].shape[1] // 3
    width = columns // 2
    return pl.pallas_call(
        project_kernel,
        out_shape=jax.ShapeDtypeStruct((4, rows + rows // 2, columns), jnp.bfloat16),
        in_specs=[pl.BlockSpec(memory_space=pltpu.SMEM)]
        + [pl.BlockSpec(memory_space=pltpu.VMEM)] * 8
        + [pl.BlockSpec(memory_space=pl.ANY)] * 4
        + [pl.BlockSpec(memory_space=pltpu.VMEM)] * 3,
        out_specs=pl.BlockSpec(memory_space=pltpu.VMEM),
        scratch_shapes=[
            pltpu.VMEM((2, 2, columns, 2 * depth), jnp.bfloat16),
            pltpu.VMEM((2, 2, width, 2 * depth), jnp.bfloat16),
            pltpu.SemaphoreType.DMA((24,)),
        ],
        compiler_params=pltpu.CompilerParams(vmem_limit_bytes=VMEM_BYTES),
        cost_estimate=pl.CostEstimate(
            flops=8 * rows * 8 * depth * (columns + width),
            bytes_accessed=16_000_000,
            transcendentals=0,
        ),
        name="project",
    )(where, *pieces, *weights, gain, cosines, sines)


def attend_kernel(
    prior, held, cache, far0, far1, sinks, attended, decode, window, bias, sems, out_sems
):
    pre_at = lax.axis_index("pre")
    rows, half = attended.shape[0], cache.shape[1]
    fresh, last = 2 * half, 2 * half + rows
    loads = [
        pltpu.make_async_copy(cache.at[pre_at], window.at[pl.ds(0, half)], sems.at[0]),
        pltpu.make_async_copy(far0, window.at[pl.ds(half, far0.shape[0])], sems.at[1]),
        pltpu.make_async_copy(
            far1.at[pl.ds(0, half - far0.shape[0])],
            window.at[pl.ds(half + far0.shape[0], half - far0.shape[0])],
            sems.at[2],
        ),
    ]
    for load in loads:
        load.start()
    span = 2 * HD
    heads = cache.shape[2] // span
    local = heads // 4
    for head in range(heads):
        block, at = head // local, head % local
        left = head * span
        start = (local + at) * HD
        window[fresh:last, left : left + HD] = held[block, :rows, start : start + HD]
        for row in range(2):
            start = row * local * HD + at * HD
            window[
                fresh + row * rows // 2 : fresh + (row + 1) * rows // 2, left + HD : left + span
            ] = held[block, rows:, start : start + HD]
    window[last:] = jnp.zeros((window.shape[0] - last, window.shape[1]), window.dtype)
    window[last : last + sinks.shape[0]] = sinks[...]
    tail = pltpu.make_async_copy(
        window.at[pl.ds(fresh, rows)], decode.at[pl.ds(2 * half - rows, rows)], out_sems.at[0]
    )
    tail.start()
    token = lax.broadcasted_iota(jnp.int32, (rows, 1), 0)
    lowest = jnp.maximum(token + 1, SINKS + 2 * half - prior[0])
    slot = lax.broadcasted_iota(jnp.int32, (1, half), 1)
    new = lax.broadcasted_iota(jnp.int32, (1, rows), 1)
    sink = lax.broadcasted_iota(jnp.int32, (1, window.shape[0] - last), 1)

    def shown(ok):
        return jnp.where(ok, 0.0, MASKED_SCORE)

    bias[:, :half] = shown(slot >= lowest - pre_at * half)
    bias[:, half:fresh] = shown(slot >= lowest - (1 - pre_at) * half)
    bias[:, fresh:last] = shown(new <= token)
    bias[:, last:] = jnp.broadcast_to(shown(sink < SINKS), (rows, window.shape[0] - last))
    for load in loads:
        load.wait()

    def keep(early, late):
        first = pltpu.make_async_copy(
            window.at[pl.ds(early + rows, half - rows)],
            decode.at[pl.ds(0, half - rows)],
            out_sems.at[1],
        )
        second = pltpu.make_async_copy(
            window.at[pl.ds(late, half)], decode.at[pl.ds(half - rows, half)], out_sems.at[2]
        )
        return first, second

    @pl.when(pre_at == 0)
    def _():
        for copy in keep(0, half):
            copy.start()

    @pl.when(pre_at != 0)
    def _():
        for copy in keep(half, 0):
            copy.start()

    scale = HD ** (-0.5)
    for head in range(heads):
        block, at = head // local, head % local * HD
        left = head * span
        scores = lax.dot_general(
            held[block, :rows, at : at + HD],
            window[:, left : left + HD],
            NT,
            preferred_element_type=jnp.float32,
        )
        scores = scores * scale + bias[...]
        top = jnp.max(scores, axis=1, keepdims=True)
        probability = jnp.exp(scores - top)
        below = jnp.sum(probability, axis=1, keepdims=True)
        mixed = jnp.dot(
            probability.astype(jnp.bfloat16),
            window[:, left + HD : left + span],
            preferred_element_type=jnp.float32,
        )
        attended[:, head * HD : (head + 1) * HD] = (mixed / below).astype(jnp.bfloat16)
    tail.wait()

    @pl.when(pre_at == 0)
    def _():
        for copy in keep(0, half):
            copy.wait()

    @pl.when(pre_at != 0)
    def _():
        for copy in keep(half, 0):
            copy.wait()


def attend(prior, parts, cache, fars, sinks):
    rows = 2 * parts.shape[1] // 3
    half, width = cache.shape[1:]
    keys = 2 * half + rows + 128
    return pl.pallas_call(
        attend_kernel,
        out_shape=[
            jax.ShapeDtypeStruct((rows, width // 2), jnp.bfloat16),
            jax.ShapeDtypeStruct((2 * half, width), jnp.bfloat16),
        ],
        in_specs=[
            pl.BlockSpec(memory_space=pltpu.SMEM),
            pl.BlockSpec(memory_space=pltpu.VMEM),
            pl.BlockSpec(memory_space=pl.ANY),
            pl.BlockSpec(memory_space=pl.ANY),
            pl.BlockSpec(memory_space=pl.ANY),
            pl.BlockSpec(memory_space=pltpu.VMEM),
        ],
        out_specs=[
            pl.BlockSpec(memory_space=pltpu.VMEM),
            pl.BlockSpec(memory_space=pl.ANY),
        ],
        scratch_shapes=[
            pltpu.VMEM((keys, width), jnp.bfloat16),
            pltpu.VMEM((rows, keys), jnp.float32),
            pltpu.SemaphoreType.DMA((3,)),
            pltpu.SemaphoreType.DMA((3,)),
        ],
        compiler_params=pltpu.CompilerParams(vmem_limit_bytes=VMEM_BYTES),
        cost_estimate=pl.CostEstimate(
            flops=2 * rows * keys * width,
            bytes_accessed=10_000_000,
            transcendentals=rows * keys * width // (2 * HD),
        ),
        name="attend",
    )(prior, parts, cache, *fars, sinks)


def finish_kernel(*refs):
    pieces, own, far, (out, held, sems) = refs[:4], refs[4:8], refs[8:12], refs[12:]
    core_at = lax.axis_index("mdl") % 2
    depth = own[0].shape[0]
    copies = []
    for step, place in enumerate(mates(lax.axis_index("dec"))):
        rows = pl.ds(pl.multiple_of(lax.rem(place, 2) * depth, depth), depth)
        for row, source in ((near_half(), own[step]), (1 - near_half(), far[step])):
            target = held.at[row, place // 2, rows]
            copies.append(pltpu.make_async_copy(source, target, sems.at[len(copies)]))
    run_all(copies)
    total = None
    for which, piece in enumerate(pieces):
        core = core_at if which < 2 else 1 - core_at
        term = jnp.dot(piece[...], held[which % 2, core], preferred_element_type=jnp.float32)
        total = term if total is None else total + term
    out[...] = total.astype(jnp.bfloat16)


def finish(pieces, own, far):
    rows, depth = pieces[0].shape
    columns = own[0].shape[1]
    return pl.pallas_call(
        finish_kernel,
        out_shape=jax.ShapeDtypeStruct((rows, columns), jnp.bfloat16),
        in_specs=[pl.BlockSpec(memory_space=pltpu.VMEM)] * 4
        + [pl.BlockSpec(memory_space=pl.ANY)] * 8,
        out_specs=pl.BlockSpec(memory_space=pltpu.VMEM),
        scratch_shapes=[
            pltpu.VMEM((2, 2, 2 * own[0].shape[0], columns), jnp.bfloat16),
            pltpu.SemaphoreType.DMA((8,)),
        ],
        compiler_params=pltpu.CompilerParams(vmem_limit_bytes=VMEM_BYTES),
        cost_estimate=pl.CostEstimate(
            flops=8 * rows * depth * columns, bytes_accessed=7_000_000, transcendentals=0
        ),
        name="finish",
    )(*pieces, *own, *far)


def join_kernel(cache, far0, far1, out, held, sems):
    half = held.shape[1]
    part = half - far1.shape[0]
    pre_at = lax.axis_index("pre")
    loads = [
        pltpu.make_async_copy(cache.at[pre_at], held.at[0], sems.at[0]),
        pltpu.make_async_copy(
            far0.at[pl.ds(far0.shape[0] - part, part)], held.at[1, pl.ds(0, part)], sems.at[1]
        ),
        pltpu.make_async_copy(far1, held.at[1, pl.ds(part, half - part)], sems.at[4]),
    ]
    stores = [
        pltpu.make_async_copy(
            held.at[which], out.at[pl.ds(pl.multiple_of(at * half, half), half)], sems.at[2 + which]
        )
        for which, at in enumerate((pre_at, 1 - pre_at))
    ]
    for load in loads:
        load.start()
    loads[0].wait()
    stores[0].start()
    loads[1].wait()
    loads[2].wait()
    stores[1].start()
    for store in stores:
        store.wait()


def join(cache, far0, far1):
    half, width = cache.shape[1:]
    return pl.pallas_call(
        join_kernel,
        out_shape=jax.ShapeDtypeStruct((2 * half, width), jnp.bfloat16),
        in_specs=[pl.BlockSpec(memory_space=pl.ANY)] * 3,
        out_specs=pl.BlockSpec(memory_space=pl.ANY),
        scratch_shapes=[pltpu.VMEM((2, half, width), jnp.bfloat16), pltpu.SemaphoreType.DMA((5,))],
        compiler_params=pltpu.CompilerParams(vmem_limit_bytes=VMEM_BYTES),
        cost_estimate=pl.CostEstimate(
            flops=0, bytes_accessed=8 * half * width, transcendentals=0
        ),
        name="join",
    )(cache, far0, far1)


def split_body(sizes, tokens, norm_gain, w_qkv, w_out, sink_cache, cache_a, cache_b, lengths, groups):
    dec = sizes["dec"]
    rows = tokens.shape[2]
    pre_at, dec_at, mdl_at = (lax.axis_index(name) for name in ("pre", "dec", "mdl"))
    swap = [(0, 1), (1, 0)]
    over_y = [(0, 2), (1, 3), (2, 0), (3, 1)]
    over_core = [(0, 1), (1, 0), (2, 3), (3, 2)]

    def along(step):
        return [(at, (at + step) % dec) for at in range(dec)]

    sent_a, sent_b = (
        lax.dynamic_index_in_dim(cache[:, 0], 1 - pre_at, 0, keepdims=False)
        for cache in (cache_a, cache_b)
    )
    own = tokens.reshape(rows, -1)
    gain = norm_gain.astype(jnp.float32).reshape(sizes["mdl"], 1, -1)

    turned = jnp.transpose(w_qkv, (1, 2, 0)).reshape(3, dec, -1, w_qkv.shape[0])
    turned = jnp.transpose(turned, (1, 0, 2, 3)).reshape(dec, -1, w_qkv.shape[0])
    split = turned.shape[1] // 2
    pairs = [(0, 1), (1, 0), (2, 3), (3, 2)]
    middle = [(1, 2), (2, 1)]
    outward = [(1, 0), (2, 3)]
    in_middle = (dec_at == 1) | (dec_at == 2)

    def over_cores(*values):
        return [lax.ppermute(value, "mdl", over_core) for value in values]

    def pick(middle_got, outer_got):
        return jnp.where(in_middle, middle_got, outer_got)

    where = jnp.stack(mates(dec_at)).astype(jnp.int32)
    cosines, sines = angles(lengths[pre_at], rows)
    cosines, sines = cosines[:, :, 0], sines[:, :, 0]
    cosines = jnp.concatenate([cosines, cosines], axis=-1)
    sines = jnp.concatenate([-sines, sines], axis=-1)
    sinks = jnp.pad(
        lax.dynamic_index_in_dim(sink_cache, groups[pre_at, dec_at], 0, keepdims=False),
        ((0, 16 - SINKS), (0, 0)),
    )
    prior = lengths[pre_at, dec_at].reshape(1)

    edges = lax.optimization_barrier
    half = sent_a.shape[0] // 4 * 3
    mate = lax.ppermute(own, "dec", pairs)
    inner = lax.ppermute(own, "dec", middle)
    y_own = lax.ppermute(own, "mdl", over_y)
    o_far = lax.ppermute(w_out, "pre", swap)
    mate, inner, y_own, o_far, first_w, early_a = edges(
        (mate, inner, y_own, o_far, turned[:, :split], sent_a[:half])
    )
    first_w = lax.all_to_all(first_w, "dec", 0, 0, tiled=True)
    inner_mate = lax.ppermute(mate, "dec", middle)
    outer = lax.ppermute(inner, "dec", outward)
    y_mate = lax.ppermute(mate, "mdl", over_y)
    far_a0 = lax.ppermute(early_a, "pre", swap)
    core_own = over_cores(own, y_own)
    first_w, inner_mate, outer, y_mate, far_a0, second_w, late_o, *tables = edges(
        (first_w, inner_mate, outer, y_mate, far_a0, turned[:, split:], w_out, where, prior, cosines, sines, sinks)
    )
    where, prior, cosines, sines, sinks = tables
    second_w = lax.all_to_all(second_w, "dec", 0, 0, tiled=True)
    third = pick(inner, outer)
    outer_mate = lax.ppermute(inner_mate, "dec", outward)
    y_third = lax.ppermute(third, "mdl", over_y)
    far_first = lax.ppermute(first_w, "pre", swap)
    core_mate = over_cores(mate, y_mate)
    second_w, outer_mate, y_third, far_first, late_o = edges(
        (second_w, outer_mate, y_third, far_first, late_o)
    )
    far_second = lax.ppermute(second_w, "pre", swap)
    fourth = pick(inner_mate, outer_mate)
    y_fourth = lax.ppermute(fourth, "mdl", over_y)
    *core_third, late_o = edges((*over_cores(third, y_third), late_o))
    o_mate = lax.ppermute(late_o, "dec", pairs)
    o_inner = lax.ppermute(late_o, "dec", middle)
    near = list(zip(core_own, core_mate, core_third))
    pieces = norm(3, [own, mate, third, y_own, y_mate, y_third, *near[0], *near[1]], gain)
    quarter = sent_b.shape[0] // 4
    late_ab = jnp.concatenate([sent_a[half:], sent_b[:quarter]], axis=0)
    pieces = [*pieces, fourth, y_fourth, *over_cores(fourth, y_fourth)]
    far_second, late_ab, late_b, *pieces = edges((far_second, late_ab, sent_b[quarter:], *pieces))
    far_ab = lax.ppermute(late_ab, "pre", swap)
    o_outer = lax.ppermute(o_inner, "dec", outward)
    o_inner_mate = lax.ppermute(o_mate, "dec", middle)
    weights = [first_w, far_first, second_w, far_second]

    found = project(where, pieces, weights, gain, cosines, sines)
    found, far_ab, o_outer, o_inner_mate, late_b = edges(
        (found, far_ab, o_outer, o_inner_mate, late_b)
    )
    parts = lax.all_to_all(found, "dec", 0, 0, tiled=True)
    far_b1 = lax.ppermute(late_b, "pre", swap)
    parts, far_b1 = edges((parts, far_b1))
    o_third = pick(o_inner, o_outer)
    o_far_third = lax.ppermute(o_third, "pre", swap)
    o_outer_mate = lax.ppermute(o_inner_mate, "dec", outward)
    attended, decode_a = attend(prior, parts, cache_a[:, 0], (far_a0, far_ab), sinks)
    attended, o_far_third, o_outer_mate, o_far = edges((attended, o_far_third, o_outer_mate, o_far))
    o_fourth = pick(o_inner_mate, o_outer_mate)
    o_far_fourth = lax.ppermute(o_fourth, "pre", swap)
    o_far_mate = lax.ppermute(o_far, "dec", pairs)
    second = lax.ppermute(attended, "mdl", over_y)
    shares = [
        attended,
        second,
        lax.ppermute(attended, "mdl", over_core),
        lax.ppermute(second, "mdl", over_core),
    ]
    attn_out = finish(
        shares,
        [w_out, o_mate, o_third, o_fourth],
        [o_far, o_far_mate, o_far_third, o_far_fourth],
    )
    decode_b = join(cache_b[:, 0], far_ab, far_b1)
    return (attn_out[None, None], decode_a[None, None], decode_b[None, None])


def body(sizes, tokens, norm_gain, w_qkv, w_out, sink_cache, cache_a, cache_b, lengths, groups):
    heads_dev = cache_a.shape[-1] // (2 * HD)
    shapes = (sizes["pre"], sizes["mdl"], sizes["dec"], heads_dev)
    split = shapes == (2, 4, 4, 8) and tokens.shape[0] == 1 and tokens.shape[1] == 1
    args = (tokens, norm_gain, w_qkv, w_out, sink_cache, cache_a, cache_b, lengths, groups)
    return split_body(sizes, *args) if split else general_body(*args)


def solution(mesh):
    placed = (
        P("pre", "dec", None, "mdl"),
        P(),
        P(("pre", "dec"), None, "mdl"),
        P(("pre", "dec"), "mdl"),
        P(None, None, "mdl"),
        P(None, "dec", "pre", "mdl"),
        P(None, "dec", "pre", "mdl"),
        P(),
        P(),
    )
    return jax.shard_map(
        functools.partial(body, dict(mesh.shape)),
        mesh=mesh,
        in_specs=placed,
        out_specs=(
            P("pre", "dec", None, "mdl"),
            P("pre", "dec", None, "mdl"),
            P("pre", "dec", None, "mdl"),
        ),
        check_vma=False,
    )
```

```python
import functools

import jax
import jax.numpy as jnp
from jax import lax
from jax.experimental import pallas as pl
from jax.experimental.pallas import tpu as pltpu
from jax.sharding import PartitionSpec as P

HD = 96
WINDOW = 1024
SINKS = 4


MASKED_SCORE = -1e30


def rotate(vector, cosines, sines):
    halfway = vector.shape[-1] // 2
    first_half = vector[..., :halfway]
    second_half = vector[..., halfway:]
    return jnp.concatenate(
        [first_half * cosines - second_half * sines, second_half * cosines + first_half * sines],
        axis=-1,
    )


def angles(offsets, count):
    halfway = HD // 2
    frequency = 10000.0 ** (-(jnp.arange(halfway).astype(jnp.float32) * 2.0) / HD)
    places = offsets.astype(jnp.float32)[:, None] + jnp.arange(count).astype(jnp.float32)[None, :]
    phases = places[:, :, None] * frequency[None, None, :]
    return (jnp.cos(phases)[:, :, None, :], jnp.sin(phases)[:, :, None, :])


def window_mask(slot_count, fresh_len, prior):
    slot_pos = jnp.arange(slot_count)[None, None, :]
    query_pos = jnp.arange(fresh_len)[None, :, None]
    return (slot_pos >= query_pos + 1) & (slot_pos >= SINKS + WINDOW - prior[:, None, None])


def masked_scores(query, all_keys, key_mask):
    scores = jnp.einsum(
        "rqhd,rkhd->rhqk", query, all_keys, preferred_element_type=jnp.float32
    ) * HD ** (-0.5)
    return jnp.where(key_mask[:, None], scores, MASKED_SCORE)


def partial_terms(scores, key_mask, all_values, row_top):
    probability = jnp.where(key_mask[:, None], jnp.exp(scores - row_top[..., None]), 0.0)
    denominator = jnp.sum(probability, axis=-1)
    numerator = jnp.einsum(
        "rhqk,rkhd->rqhd",
        probability.astype(jnp.bfloat16),
        all_values,
        preferred_element_type=jnp.float32,
    )
    return (numerator, denominator)


def general_body(tokens, norm_gain, w_qkv, w_out, sink_cache, cache_a, cache_b, lengths, groups):
    req_count = tokens.shape[0]
    fresh_len = tokens.shape[2]
    col_width = cache_a.shape[-1] // 2
    heads_dev = col_width // HD
    row_count = req_count * fresh_len
    pre_at = lax.axis_index("pre") * req_count
    dec_at = lax.axis_index("dec")
    gathered = lax.all_gather(tokens, "mdl", axis=3, tiled=True)
    as_float = gathered.reshape(row_count, -1).astype(jnp.float32)
    normed = (
        as_float
        * lax.rsqrt(jnp.mean(as_float * as_float, axis=-1, keepdims=True) + 1e-05)
        * norm_gain.astype(jnp.float32)
    ).astype(jnp.bfloat16)
    shard_rows = lax.all_gather(w_qkv, ("pre", "dec"), axis=0, tiled=True)
    columns = normed
    projected = jnp.dot(
        columns, shard_rows.reshape(shard_rows.shape[0], -1), preferred_element_type=jnp.float32
    )
    projected = projected.reshape(req_count, fresh_len, 3, heads_dev, HD)
    my_len = lax.dynamic_slice(lengths, (pre_at, dec_at), (req_count, 1))[:, 0]
    my_group = lax.dynamic_slice(groups, (pre_at, dec_at), (req_count, 1))[:, 0]
    cosines, sines = angles(my_len, fresh_len)
    query = rotate(projected[:, :, 0], cosines, sines).astype(jnp.bfloat16)
    key_new = rotate(projected[:, :, 1], cosines, sines).astype(jnp.bfloat16)
    value_new = projected[:, :, 2].astype(jnp.bfloat16)
    onehot = (my_group[:, None] == jnp.arange(sink_cache.shape[0])[None, :]).astype(jnp.float32)
    sink_rows = jnp.einsum("rg,gsc->rsc", onehot, sink_cache.astype(jnp.float32)).astype(
        jnp.bfloat16
    )
    sink_rows = sink_rows.reshape(req_count, SINKS, heads_dev, 2, HD)
    sink_keys = sink_rows[:, :, :, 0]
    sink_values = sink_rows[:, :, :, 1]
    sink_ok = jnp.ones((req_count, fresh_len, SINKS), dtype=bool)
    recent_ok = jnp.arange(fresh_len)[None, None, :] <= jnp.arange(fresh_len)[None, :, None]
    moved_a, moved_b = (
        lax.all_to_all(cache_a, "pre", split_axis=0, concat_axis=2, tiled=True),
        lax.all_to_all(cache_b, "pre", split_axis=0, concat_axis=2, tiled=True),
    )
    full_window = moved_a[:, 0].reshape(req_count, -1, heads_dev, 2, HD)
    window_keys = full_window[:, :, :, 0]
    window_values = full_window[:, :, :, 1]
    all_keys = jnp.concatenate([sink_keys, window_keys, key_new], axis=1)
    all_values = jnp.concatenate([sink_values, window_values, value_new], axis=1)
    far_mask = window_mask(WINDOW, fresh_len, my_len)
    key_mask = jnp.concatenate([sink_ok, far_mask, recent_ok], axis=2)
    scores = masked_scores(query, all_keys, key_mask)
    row_top = jnp.max(scores, axis=-1)
    numerator, denominator = partial_terms(scores, key_mask, all_values, row_top)
    attended = (
        (numerator / jnp.transpose(denominator, (0, 2, 1))[..., None])
        .astype(jnp.bfloat16)
        .reshape(row_count, col_width)
    )
    every_head = lax.all_gather(attended, "mdl", axis=1, tiled=True)
    columns = every_head
    output_rows = jnp.dot(
        columns,
        lax.all_gather(w_out, ("pre", "dec"), axis=0, tiled=True),
        preferred_element_type=jnp.float32,
    )
    attn_out = output_rows.astype(jnp.bfloat16).reshape(req_count, 1, fresh_len, -1)
    fresh_kv = jnp.stack([key_new, value_new], axis=3).reshape(req_count, fresh_len, 2 * col_width)[
        :, None
    ]
    decode_a = jnp.concatenate([moved_a[:, :, fresh_len:], fresh_kv], axis=2)
    return (attn_out, decode_a, moved_b)


VMEM_BYTES = 56 * 1024 * 1024
NT = (((1,), (1,)), ((), ()))


def mates(at):
    return [at, at + 1 - 2 * lax.rem(at, 2), 2 - at // 2, 3 - 3 * (at // 2)]


def near_half():
    return jnp.where(lax.axis_index("mdl") // 2 == lax.axis_index("pre"), 0, 1)


def feature_place(which):
    row, core = lax.axis_index("mdl") // 2, lax.axis_index("mdl") % 2
    row = row if which in (0, 2) else 1 - row
    core = core if which < 2 else 1 - core
    return row * 2 + core, core


def normed_parts(parts, gain):
    parts = [part.astype(jnp.float32) for part in parts]
    squares = sum(jnp.sum(part * part, axis=1, keepdims=True) for part in parts)
    scale = lax.rsqrt(squares / (4 * parts[0].shape[1]) + 1e-05)
    return [
        (part * scale * gain[feature_place(which)[0]]).astype(jnp.bfloat16)
        for which, part in enumerate(parts)
    ]


def norm_kernel(count, *refs):
    pieces, (gain, *outs) = refs[:-5], refs[-5:]
    rows = pieces[0].shape[0]
    for slot in range(count):
        parts = normed_parts([pieces[which * count + slot][...] for which in range(4)], gain)
        for which, part in enumerate(parts):
            outs[which][slot * rows : (slot + 1) * rows] = part


def norm(count, pieces, gain):
    rows, depth = pieces[0].shape
    space = pl.BlockSpec(memory_space=pltpu.VMEM)
    return pl.pallas_call(
        functools.partial(norm_kernel, count),
        out_shape=[jax.ShapeDtypeStruct((count * rows, depth), jnp.bfloat16)] * 4,
        in_specs=[space] * (len(pieces) + 1),
        out_specs=[space] * 4,
        compiler_params=pltpu.CompilerParams(vmem_limit_bytes=VMEM_BYTES),
        cost_estimate=pl.CostEstimate(
            flops=24 * count * rows * depth, bytes_accessed=16 * count * rows * depth, transcendentals=0
        ),
        name="norm",
    )(*pieces, gain)


def project_kernel(*refs):
    where, weights, gain = refs[0], refs[9:13], refs[13]
    cosines, sines, out, held_qk, held_v, sems = refs[14:]
    early, depth = weights[0].shape[1:]
    late = held_qk.shape[2] - early
    copies = []
    for which, source in enumerate(weights):
        row = near_half() if which % 2 == 0 else 1 - near_half()
        for place in range(4):
            block = pl.ds(place % 2 * depth, depth)
            if which < 2:
                moves = [(source.at[place], held_qk.at[row, place // 2, pl.ds(0, early), block])]
            else:
                moves = [
                    (source.at[place, pl.ds(0, late)], held_qk.at[row, place // 2, pl.ds(early, late), block]),
                    (source.at[place, pl.ds(late, early - late)], held_v.at[row, place // 2, :, block]),
                ]
            for one, two in moves:
                copies.append(pltpu.make_async_copy(one, two, sems.at[len(copies)]))
    for copy in copies:
        copy.start()
    rows, columns = refs[5].shape[0], held_qk.shape[2]
    width = columns // 2
    lane = lax.broadcasted_iota(jnp.int32, (1, columns), 1)
    in_first = lane % HD < HD // 2
    first = 0
    groups = (
        [piece[...] for piece in refs[1:5]],
        normed_parts([piece[...] for piece in refs[5:9]], gain),
    )
    for copy in copies:
        copy.wait()
    for pieces in groups:
        count = pieces[0].shape[0] // rows
        turning, values = (
            sum(
                lax.dot_general(
                    piece,
                    held[which % 2, feature_place(which)[1]],
                    NT,
                    preferred_element_type=jnp.float32,
                )
                for which, piece in enumerate(pieces)
            )
            for held in (held_qk, held_v)
        )
        for slot in range(count):
            at = where[first + slot]
            turned = turning[slot * rows : (slot + 1) * rows]
            ahead = pltpu.roll(turned, columns - HD // 2, 1)
            behind = pltpu.roll(turned, HD // 2, 1)
            cosine, sine = (
                jnp.concatenate([table[at]] * (columns // HD), axis=1) for table in (cosines, sines)
            )
            turned = turned * cosine + jnp.where(in_first, ahead, behind) * sine
            out[at, :rows] = turned.astype(jnp.bfloat16)
            value = values[slot * rows : (slot + 1) * rows].astype(jnp.bfloat16)
            for row in range(2):
                out[at, rows:, row * width : (row + 1) * width] = value[
                    row * rows // 2 : (row + 1) * rows // 2
                ]
        first += count


def project(where, pieces, weights, gain, cosines, sines):
    rows, depth = cosines.shape[1], weights[0].shape[2]
    columns = 4 * weights[0].shape[1] // 3
    width = columns // 2
    return pl.pallas_call(
        project_kernel,
        out_shape=jax.ShapeDtypeStruct((4, rows + rows // 2, columns), jnp.bfloat16),
        in_specs=[pl.BlockSpec(memory_space=pltpu.SMEM)]
        + [pl.BlockSpec(memory_space=pltpu.VMEM)] * 8
        + [pl.BlockSpec(memory_space=pl.ANY)] * 4
        + [pl.BlockSpec(memory_space=pltpu.VMEM)] * 3,
        out_specs=pl.BlockSpec(memory_space=pltpu.VMEM),
        scratch_shapes=[
            pltpu.VMEM((2, 2, columns, 2 * depth), jnp.bfloat16),
            pltpu.VMEM((2, 2, width, 2 * depth), jnp.bfloat16),
            pltpu.SemaphoreType.DMA((24,)),
        ],
        compiler_params=pltpu.CompilerParams(vmem_limit_bytes=VMEM_BYTES),
        cost_estimate=pl.CostEstimate(
            flops=8 * rows * 8 * depth * (columns + width),
            bytes_accessed=16_000_000,
            transcendentals=0,
        ),
        name="project",
    )(where, *pieces, *weights, gain, cosines, sines)


def attend_kernel(
    prior, held, cache, far0, far1, sinks, attended, decode, window, bias, sems, out_sems
):
    pre_at = lax.axis_index("pre")
    rows, half = attended.shape[0], cache.shape[1]
    fresh, last = 2 * half, 2 * half + rows
    loads = [
        pltpu.make_async_copy(cache.at[pre_at], window.at[pl.ds(0, half)], sems.at[0]),
        pltpu.make_async_copy(far0, window.at[pl.ds(half, far0.shape[0])], sems.at[1]),
        pltpu.make_async_copy(
            far1.at[pl.ds(0, half - far0.shape[0])],
            window.at[pl.ds(half + far0.shape[0], half - far0.shape[0])],
            sems.at[2],
        ),
    ]
    for load in loads:
        load.start()
    span = 2 * HD
    heads = cache.shape[2] // span
    local = heads // 4
    for head in range(heads):
        block, at = head // local, head % local
        left = head * span
        start = (local + at) * HD
        window[fresh:last, left : left + HD] = held[block, :rows, start : start + HD]
        for row in range(2):
            start = row * local * HD + at * HD
            window[
                fresh + row * rows // 2 : fresh + (row + 1) * rows // 2, left + HD : left + span
            ] = held[block, rows:, start : start + HD]
    window[last:] = jnp.zeros((window.shape[0] - last, window.shape[1]), window.dtype)
    window[last : last + sinks.shape[0]] = sinks[...]
    tail = pltpu.make_async_copy(
        window.at[pl.ds(fresh, rows)], decode.at[pl.ds(2 * half - rows, rows)], out_sems.at[0]
    )
    tail.start()
    token = lax.broadcasted_iota(jnp.int32, (rows, 1), 0)
    lowest = jnp.maximum(token + 1, SINKS + 2 * half - prior[0])
    slot = lax.broadcasted_iota(jnp.int32, (1, half), 1)
    new = lax.broadcasted_iota(jnp.int32, (1, rows), 1)
    sink = lax.broadcasted_iota(jnp.int32, (1, window.shape[0] - last), 1)

    def shown(ok):
        return jnp.where(ok, 0.0, MASKED_SCORE)

    bias[:, :half] = shown(slot >= lowest - pre_at * half)
    bias[:, half:fresh] = shown(slot >= lowest - (1 - pre_at) * half)
    bias[:, fresh:last] = shown(new <= token)
    bias[:, last:] = jnp.broadcast_to(shown(sink < SINKS), (rows, window.shape[0] - last))
    for load in loads:
        load.wait()

    def keep(early, late):
        first = pltpu.make_async_copy(
            window.at[pl.ds(early + rows, half - rows)],
            decode.at[pl.ds(0, half - rows)],
            out_sems.at[1],
        )
        second = pltpu.make_async_copy(
            window.at[pl.ds(late, half)], decode.at[pl.ds(half - rows, half)], out_sems.at[2]
        )
        return first, second

    @pl.when(pre_at == 0)
    def _():
        for copy in keep(0, half):
            copy.start()

    @pl.when(pre_at != 0)
    def _():
        for copy in keep(half, 0):
            copy.start()

    scale = HD ** (-0.5)
    for head in range(heads):
        block, at = head // local, head % local * HD
        left = head * span
        scores = lax.dot_general(
            held[block, :rows, at : at + HD],
            window[:, left : left + HD],
            NT,
            preferred_element_type=jnp.float32,
        )
        scores = scores * scale + bias[...]
        top = jnp.max(scores, axis=1, keepdims=True)
        probability = jnp.exp(scores - top)
        below = jnp.sum(probability, axis=1, keepdims=True)
        mixed = jnp.dot(
            probability.astype(jnp.bfloat16),
            window[:, left + HD : left + span],
            preferred_element_type=jnp.float32,
        )
        attended[:, head * HD : (head + 1) * HD] = (mixed / below).astype(jnp.bfloat16)
    tail.wait()

    @pl.when(pre_at == 0)
    def _():
        for copy in keep(0, half):
            copy.wait()

    @pl.when(pre_at != 0)
    def _():
        for copy in keep(half, 0):
            copy.wait()


def attend(prior, parts, cache, fars, sinks):
    rows = 2 * parts.shape[1] // 3
    half, width = cache.shape[1:]
    keys = 2 * half + rows + 128
    return pl.pallas_call(
        attend_kernel,
        out_shape=[
            jax.ShapeDtypeStruct((rows, width // 2), jnp.bfloat16),
            jax.ShapeDtypeStruct((2 * half, width), jnp.bfloat16),
        ],
        in_specs=[
            pl.BlockSpec(memory_space=pltpu.SMEM),
            pl.BlockSpec(memory_space=pltpu.VMEM),
            pl.BlockSpec(memory_space=pl.ANY),
            pl.BlockSpec(memory_space=pl.ANY),
            pl.BlockSpec(memory_space=pl.ANY),
            pl.BlockSpec(memory_space=pltpu.VMEM),
        ],
        out_specs=[
            pl.BlockSpec(memory_space=pltpu.VMEM),
            pl.BlockSpec(memory_space=pl.ANY),
        ],
        scratch_shapes=[
            pltpu.VMEM((keys, width), jnp.bfloat16),
            pltpu.VMEM((rows, keys), jnp.float32),
            pltpu.SemaphoreType.DMA((3,)),
            pltpu.SemaphoreType.DMA((3,)),
        ],
        compiler_params=pltpu.CompilerParams(vmem_limit_bytes=VMEM_BYTES),
        cost_estimate=pl.CostEstimate(
            flops=2 * rows * keys * width,
            bytes_accessed=10_000_000,
            transcendentals=rows * keys * width // (2 * HD),
        ),
        name="attend",
    )(prior, parts, cache, *fars, sinks)


def finish_kernel(*refs):
    pieces, own, far, out = refs[:4], refs[4:8], refs[8:12], refs[12]
    core_at, match = lax.axis_index("mdl") % 2, near_half() == 0
    depth = own[0].shape[0]
    total = None
    for step, place in enumerate(mates(lax.axis_index("dec"))):
        columns = pl.ds(pl.multiple_of(lax.rem(place, 2) * depth, depth), depth)
        same = place // 2 == core_at
        own_row, far_row = (
            jnp.where(same, pieces[which][:, columns], pieces[which + 2][:, columns])
            for which in range(2)
        )
        for heads, weights in (
            (jnp.where(match, own_row, far_row), own[step]),
            (jnp.where(match, far_row, own_row), far[step]),
        ):
            term = jnp.dot(heads, weights[...], preferred_element_type=jnp.float32)
            total = term if total is None else total + term
    out[...] = total.astype(jnp.bfloat16)


def finish(pieces, own, far):
    rows, depth = pieces[0].shape
    columns = own[0].shape[1]
    return pl.pallas_call(
        finish_kernel,
        out_shape=jax.ShapeDtypeStruct((rows, columns), jnp.bfloat16),
        in_specs=[pl.BlockSpec(memory_space=pltpu.VMEM)] * 12,
        out_specs=pl.BlockSpec(memory_space=pltpu.VMEM),
        compiler_params=pltpu.CompilerParams(vmem_limit_bytes=VMEM_BYTES),
        cost_estimate=pl.CostEstimate(
            flops=8 * rows * depth * columns, bytes_accessed=7_000_000, transcendentals=0
        ),
        name="finish",
    )(*pieces, *own, *far)


def join_kernel(cache, far0, far1, out, held, sems):
    half = held.shape[1]
    part = half - far1.shape[0]
    pre_at = lax.axis_index("pre")
    loads = [
        pltpu.make_async_copy(cache.at[pre_at], held.at[0], sems.at[0]),
        pltpu.make_async_copy(
            far0.at[pl.ds(far0.shape[0] - part, part)], held.at[1, pl.ds(0, part)], sems.at[1]
        ),
        pltpu.make_async_copy(far1, held.at[1, pl.ds(part, half - part)], sems.at[4]),
    ]
    stores = [
        pltpu.make_async_copy(
            held.at[which], out.at[pl.ds(pl.multiple_of(at * half, half), half)], sems.at[2 + which]
        )
        for which, at in enumerate((pre_at, 1 - pre_at))
    ]
    for load in loads:
        load.start()
    loads[0].wait()
    stores[0].start()
    loads[1].wait()
    loads[2].wait()
    stores[1].start()
    for store in stores:
        store.wait()


def join(cache, far0, far1):
    half, width = cache.shape[1:]
    return pl.pallas_call(
        join_kernel,
        out_shape=jax.ShapeDtypeStruct((2 * half, width), jnp.bfloat16),
        in_specs=[pl.BlockSpec(memory_space=pl.ANY)] * 3,
        out_specs=pl.BlockSpec(memory_space=pl.ANY),
        scratch_shapes=[pltpu.VMEM((2, half, width), jnp.bfloat16), pltpu.SemaphoreType.DMA((5,))],
        compiler_params=pltpu.CompilerParams(vmem_limit_bytes=VMEM_BYTES),
        cost_estimate=pl.CostEstimate(
            flops=0, bytes_accessed=8 * half * width, transcendentals=0
        ),
        name="join",
    )(cache, far0, far1)


def split_body(sizes, tokens, norm_gain, w_qkv, w_out, sink_cache, cache_a, cache_b, lengths, groups):
    dec = sizes["dec"]
    rows = tokens.shape[2]
    pre_at, dec_at, mdl_at = (lax.axis_index(name) for name in ("pre", "dec", "mdl"))
    swap = [(0, 1), (1, 0)]
    over_y = [(0, 2), (1, 3), (2, 0), (3, 1)]
    over_core = [(0, 1), (1, 0), (2, 3), (3, 2)]

    def along(step):
        return [(at, (at + step) % dec) for at in range(dec)]

    sent_a, sent_b = (
        lax.dynamic_index_in_dim(cache[:, 0], 1 - pre_at, 0, keepdims=False)
        for cache in (cache_a, cache_b)
    )
    own = tokens.reshape(rows, -1)
    gain = norm_gain.astype(jnp.float32).reshape(sizes["mdl"], 1, -1)

    turned = jnp.transpose(w_qkv, (1, 2, 0)).reshape(3, dec, -1, w_qkv.shape[0])
    turned = jnp.transpose(turned, (1, 0, 2, 3)).reshape(dec, -1, w_qkv.shape[0])
    split = turned.shape[1] // 2
    pairs = [(0, 1), (1, 0), (2, 3), (3, 2)]
    middle = [(1, 2), (2, 1)]
    outward = [(1, 0), (2, 3)]
    in_middle = (dec_at == 1) | (dec_at == 2)

    def over_cores(*values):
        return [lax.ppermute(value, "mdl", over_core) for value in values]

    def pick(middle_got, outer_got):
        return jnp.where(in_middle, middle_got, outer_got)

    where = jnp.stack(mates(dec_at)).astype(jnp.int32)
    cosines, sines = angles(lengths[pre_at], rows)
    cosines, sines = cosines[:, :, 0], sines[:, :, 0]
    cosines = jnp.concatenate([cosines, cosines], axis=-1)
    sines = jnp.concatenate([-sines, sines], axis=-1)
    sinks = jnp.pad(
        lax.dynamic_index_in_dim(sink_cache, groups[pre_at, dec_at], 0, keepdims=False),
        ((0, 16 - SINKS), (0, 0)),
    )
    prior = lengths[pre_at, dec_at].reshape(1)

    edges = lax.optimization_barrier
    half = sent_a.shape[0] // 4 * 3
    mate = lax.ppermute(own, "dec", pairs)
    inner = lax.ppermute(own, "dec", middle)
    y_own = lax.ppermute(own, "mdl", over_y)
    o_far = lax.ppermute(w_out, "pre", swap)
    mate, inner, y_own, o_far, first_w, early_a = edges(
        (mate, inner, y_own, o_far, turned[:, :split], sent_a[:half])
    )
    first_w = lax.all_to_all(first_w, "dec", 0, 0, tiled=True)
    inner_mate = lax.ppermute(mate, "dec", middle)
    outer = lax.ppermute(inner, "dec", outward)
    y_mate = lax.ppermute(mate, "mdl", over_y)
    far_a0 = lax.ppermute(early_a, "pre", swap)
    core_own = over_cores(own, y_own)
    first_w, inner_mate, outer, y_mate, far_a0, second_w, late_o, *tables = edges(
        (first_w, inner_mate, outer, y_mate, far_a0, turned[:, split:], w_out, where, prior, cosines, sines, sinks)
    )
    where, prior, cosines, sines, sinks = tables
    second_w = lax.all_to_all(second_w, "dec", 0, 0, tiled=True)
    third = pick(inner, outer)
    outer_mate = lax.ppermute(inner_mate, "dec", outward)
    y_third = lax.ppermute(third, "mdl", over_y)
    far_first = lax.ppermute(first_w, "pre", swap)
    core_mate = over_cores(mate, y_mate)
    second_w, outer_mate, y_third, far_first, late_o = edges(
        (second_w, outer_mate, y_third, far_first, late_o)
    )
    far_second = lax.ppermute(second_w, "pre", swap)
    fourth = pick(inner_mate, outer_mate)
    y_fourth = lax.ppermute(fourth, "mdl", over_y)
    *core_third, late_o = edges((*over_cores(third, y_third), late_o))
    o_mate = lax.ppermute(late_o, "dec", pairs)
    o_inner = lax.ppermute(late_o, "dec", middle)
    near = list(zip(core_own, core_mate, core_third))
    pieces = norm(3, [own, mate, third, y_own, y_mate, y_third, *near[0], *near[1]], gain)
    quarter = sent_b.shape[0] // 4
    late_ab = jnp.concatenate([sent_a[half:], sent_b[:quarter]], axis=0)
    pieces = [*pieces, fourth, y_fourth, *over_cores(fourth, y_fourth)]
    far_second, late_ab, late_b, *pieces = edges((far_second, late_ab, sent_b[quarter:], *pieces))
    far_ab = lax.ppermute(late_ab, "pre", swap)
    o_outer = lax.ppermute(o_inner, "dec", outward)
    o_inner_mate = lax.ppermute(o_mate, "dec", middle)
    weights = [first_w, far_first, second_w, far_second]

    found = project(where, pieces, weights, gain, cosines, sines)
    found, far_ab, o_outer, o_inner_mate, late_b = edges(
        (found, far_ab, o_outer, o_inner_mate, late_b)
    )
    parts = lax.all_to_all(found, "dec", 0, 0, tiled=True)
    far_b1 = lax.ppermute(late_b, "pre", swap)
    parts, far_b1 = edges((parts, far_b1))
    o_third = pick(o_inner, o_outer)
    o_far_third = lax.ppermute(o_third, "pre", swap)
    o_outer_mate = lax.ppermute(o_inner_mate, "dec", outward)
    attended, decode_a = attend(prior, parts, cache_a[:, 0], (far_a0, far_ab), sinks)
    attended, o_far_third, o_outer_mate, o_far = edges((attended, o_far_third, o_outer_mate, o_far))
    o_fourth = pick(o_inner_mate, o_outer_mate)
    o_far_fourth = lax.ppermute(o_fourth, "pre", swap)
    o_far_mate = lax.ppermute(o_far, "dec", pairs)
    second = lax.ppermute(attended, "mdl", over_y)
    shares = [
        attended,
        second,
        lax.ppermute(attended, "mdl", over_core),
        lax.ppermute(second, "mdl", over_core),
    ]
    attn_out = finish(
        shares,
        [w_out, o_mate, o_third, o_fourth],
        [o_far, o_far_mate, o_far_third, o_far_fourth],
    )
    decode_b = join(cache_b[:, 0], far_ab, far_b1)
    return (attn_out[None, None], decode_a[None, None], decode_b[None, None])


def body(sizes, tokens, norm_gain, w_qkv, w_out, sink_cache, cache_a, cache_b, lengths, groups):
    heads_dev = cache_a.shape[-1] // (2 * HD)
    shapes = (sizes["pre"], sizes["mdl"], sizes["dec"], heads_dev)
    split = shapes == (2, 4, 4, 8) and tokens.shape[0] == 1 and tokens.shape[1] == 1
    args = (tokens, norm_gain, w_qkv, w_out, sink_cache, cache_a, cache_b, lengths, groups)
    return split_body(sizes, *args) if split else general_body(*args)


def solution(mesh):
    placed = (
        P("pre", "dec", None, "mdl"),
        P(),
        P(("pre", "dec"), None, "mdl"),
        P(("pre", "dec"), "mdl"),
        P(None, None, "mdl"),
        P(None, "dec", "pre", "mdl"),
        P(None, "dec", "pre", "mdl"),
        P(),
        P(),
    )
    return jax.shard_map(
        functools.partial(body, dict(mesh.shape)),
        mesh=mesh,
        in_specs=placed,
        out_specs=(
            P("pre", "dec", None, "mdl"),
            P("pre", "dec", None, "mdl"),
            P("pre", "dec", None, "mdl"),
        ),
        check_vma=False,
    )
```

```python
import functools

import jax
import jax.numpy as jnp
from jax import lax
from jax.experimental import pallas as pl
from jax.experimental.pallas import tpu as pltpu
from jax.sharding import PartitionSpec as P

HD = 96
WINDOW = 1024
SINKS = 4


MASKED_SCORE = -1e30


def rotate(vector, cosines, sines):
    halfway = vector.shape[-1] // 2
    first_half = vector[..., :halfway]
    second_half = vector[..., halfway:]
    return jnp.concatenate(
        [first_half * cosines - second_half * sines, second_half * cosines + first_half * sines],
        axis=-1,
    )


def angles(offsets, count):
    halfway = HD // 2
    frequency = 10000.0 ** (-(jnp.arange(halfway).astype(jnp.float32) * 2.0) / HD)
    places = offsets.astype(jnp.float32)[:, None] + jnp.arange(count).astype(jnp.float32)[None, :]
    phases = places[:, :, None] * frequency[None, None, :]
    return (jnp.cos(phases)[:, :, None, :], jnp.sin(phases)[:, :, None, :])


def window_mask(slot_count, fresh_len, prior):
    slot_pos = jnp.arange(slot_count)[None, None, :]
    query_pos = jnp.arange(fresh_len)[None, :, None]
    return (slot_pos >= query_pos + 1) & (slot_pos >= SINKS + WINDOW - prior[:, None, None])


def masked_scores(query, all_keys, key_mask):
    scores = jnp.einsum(
        "rqhd,rkhd->rhqk", query, all_keys, preferred_element_type=jnp.float32
    ) * HD ** (-0.5)
    return jnp.where(key_mask[:, None], scores, MASKED_SCORE)


def partial_terms(scores, key_mask, all_values, row_top):
    probability = jnp.where(key_mask[:, None], jnp.exp(scores - row_top[..., None]), 0.0)
    denominator = jnp.sum(probability, axis=-1)
    numerator = jnp.einsum(
        "rhqk,rkhd->rqhd",
        probability.astype(jnp.bfloat16),
        all_values,
        preferred_element_type=jnp.float32,
    )
    return (numerator, denominator)


def general_body(tokens, norm_gain, w_qkv, w_out, sink_cache, cache_a, cache_b, lengths, groups):
    req_count = tokens.shape[0]
    fresh_len = tokens.shape[2]
    col_width = cache_a.shape[-1] // 2
    heads_dev = col_width // HD
    row_count = req_count * fresh_len
    pre_at = lax.axis_index("pre") * req_count
    dec_at = lax.axis_index("dec")
    gathered = lax.all_gather(tokens, "mdl", axis=3, tiled=True)
    as_float = gathered.reshape(row_count, -1).astype(jnp.float32)
    normed = (
        as_float
        * lax.rsqrt(jnp.mean(as_float * as_float, axis=-1, keepdims=True) + 1e-05)
        * norm_gain.astype(jnp.float32)
    ).astype(jnp.bfloat16)
    shard_rows = lax.all_gather(w_qkv, ("pre", "dec"), axis=0, tiled=True)
    columns = normed
    projected = jnp.dot(
        columns, shard_rows.reshape(shard_rows.shape[0], -1), preferred_element_type=jnp.float32
    )
    projected = projected.reshape(req_count, fresh_len, 3, heads_dev, HD)
    my_len = lax.dynamic_slice(lengths, (pre_at, dec_at), (req_count, 1))[:, 0]
    my_group = lax.dynamic_slice(groups, (pre_at, dec_at), (req_count, 1))[:, 0]
    cosines, sines = angles(my_len, fresh_len)
    query = rotate(projected[:, :, 0], cosines, sines).astype(jnp.bfloat16)
    key_new = rotate(projected[:, :, 1], cosines, sines).astype(jnp.bfloat16)
    value_new = projected[:, :, 2].astype(jnp.bfloat16)
    onehot = (my_group[:, None] == jnp.arange(sink_cache.shape[0])[None, :]).astype(jnp.float32)
    sink_rows = jnp.einsum("rg,gsc->rsc", onehot, sink_cache.astype(jnp.float32)).astype(
        jnp.bfloat16
    )
    sink_rows = sink_rows.reshape(req_count, SINKS, heads_dev, 2, HD)
    sink_keys = sink_rows[:, :, :, 0]
    sink_values = sink_rows[:, :, :, 1]
    sink_ok = jnp.ones((req_count, fresh_len, SINKS), dtype=bool)
    recent_ok = jnp.arange(fresh_len)[None, None, :] <= jnp.arange(fresh_len)[None, :, None]
    moved_a, moved_b = (
        lax.all_to_all(cache_a, "pre", split_axis=0, concat_axis=2, tiled=True),
        lax.all_to_all(cache_b, "pre", split_axis=0, concat_axis=2, tiled=True),
    )
    full_window = moved_a[:, 0].reshape(req_count, -1, heads_dev, 2, HD)
    window_keys = full_window[:, :, :, 0]
    window_values = full_window[:, :, :, 1]
    all_keys = jnp.concatenate([sink_keys, window_keys, key_new], axis=1)
    all_values = jnp.concatenate([sink_values, window_values, value_new], axis=1)
    far_mask = window_mask(WINDOW, fresh_len, my_len)
    key_mask = jnp.concatenate([sink_ok, far_mask, recent_ok], axis=2)
    scores = masked_scores(query, all_keys, key_mask)
    row_top = jnp.max(scores, axis=-1)
    numerator, denominator = partial_terms(scores, key_mask, all_values, row_top)
    attended = (
        (numerator / jnp.transpose(denominator, (0, 2, 1))[..., None])
        .astype(jnp.bfloat16)
        .reshape(row_count, col_width)
    )
    every_head = lax.all_gather(attended, "mdl", axis=1, tiled=True)
    columns = every_head
    output_rows = jnp.dot(
        columns,
        lax.all_gather(w_out, ("pre", "dec"), axis=0, tiled=True),
        preferred_element_type=jnp.float32,
    )
    attn_out = output_rows.astype(jnp.bfloat16).reshape(req_count, 1, fresh_len, -1)
    fresh_kv = jnp.stack([key_new, value_new], axis=3).reshape(req_count, fresh_len, 2 * col_width)[
        :, None
    ]
    decode_a = jnp.concatenate([moved_a[:, :, fresh_len:], fresh_kv], axis=2)
    return (attn_out, decode_a, moved_b)


VMEM_BYTES = 56 * 1024 * 1024
NT = (((1,), (1,)), ((), ()))


def mates(at):
    return [at, at + 1 - 2 * lax.rem(at, 2), 2 - at // 2, 3 - 3 * (at // 2)]


def near_half():
    return jnp.where(lax.axis_index("mdl") // 2 == lax.axis_index("pre"), 0, 1)


def feature_place(which):
    row, core = lax.axis_index("mdl") // 2, lax.axis_index("mdl") % 2
    row = row if which in (0, 2) else 1 - row
    core = core if which < 2 else 1 - core
    return row * 2 + core, core


def normed_parts(parts, gain):
    parts = [part.astype(jnp.float32) for part in parts]
    squares = sum(jnp.sum(part * part, axis=1, keepdims=True) for part in parts)
    scale = lax.rsqrt(squares / (4 * parts[0].shape[1]) + 1e-05)
    return [
        (part * scale * gain[feature_place(which)[0]]).astype(jnp.bfloat16)
        for which, part in enumerate(parts)
    ]


def norm_kernel(count, *refs):
    pieces, (gain, *outs) = refs[:-5], refs[-5:]
    rows = pieces[0].shape[0]
    for slot in range(count):
        parts = normed_parts([pieces[which * count + slot][...] for which in range(4)], gain)
        for which, part in enumerate(parts):
            outs[which][slot * rows : (slot + 1) * rows] = part


def norm(count, pieces, gain):
    rows, depth = pieces[0].shape
    space = pl.BlockSpec(memory_space=pltpu.VMEM)
    return pl.pallas_call(
        functools.partial(norm_kernel, count),
        out_shape=[jax.ShapeDtypeStruct((count * rows, depth), jnp.bfloat16)] * 4,
        in_specs=[space] * (len(pieces) + 1),
        out_specs=[space] * 4,
        compiler_params=pltpu.CompilerParams(vmem_limit_bytes=VMEM_BYTES),
        cost_estimate=pl.CostEstimate(
            flops=24 * count * rows * depth, bytes_accessed=16 * count * rows * depth, transcendentals=0
        ),
        name="norm",
    )(*pieces, gain)


def project_kernel(*refs):
    where, weights, gain = refs[0], refs[9:13], refs[13]
    cosines, sines, out, held_qk, held_v, sems = refs[14:]
    early, depth = weights[0].shape[1:]
    late = held_qk.shape[2] - early
    copies = []
    for which, source in enumerate(weights):
        row = near_half() if which % 2 == 0 else 1 - near_half()
        for place in range(4):
            block = pl.ds(place % 2 * depth, depth)
            if which < 2:
                moves = [(source.at[place], held_qk.at[row, place // 2, pl.ds(0, early), block])]
            else:
                moves = [
                    (source.at[place, pl.ds(0, late)], held_qk.at[row, place // 2, pl.ds(early, late), block]),
                    (source.at[place, pl.ds(late, early - late)], held_v.at[row, place // 2, :, block]),
                ]
            for one, two in moves:
                copies.append(pltpu.make_async_copy(one, two, sems.at[len(copies)]))
    for copy in copies:
        copy.start()
    rows, columns = refs[5].shape[0], held_qk.shape[2]
    width = columns // 2
    lane = lax.broadcasted_iota(jnp.int32, (1, columns), 1)
    in_first = lane % HD < HD // 2
    first = 0
    groups = (
        [piece[...] for piece in refs[1:5]],
        normed_parts([piece[...] for piece in refs[5:9]], gain),
    )
    for copy in copies:
        copy.wait()
    for pieces in groups:
        count = pieces[0].shape[0] // rows
        turning, values = (
            sum(
                lax.dot_general(
                    piece,
                    held[which % 2, feature_place(which)[1]],
                    NT,
                    preferred_element_type=jnp.float32,
                )
                for which, piece in enumerate(pieces)
            )
            for held in (held_qk, held_v)
        )
        for slot in range(count):
            at = where[first + slot]
            turned = turning[slot * rows : (slot + 1) * rows]
            ahead = pltpu.roll(turned, columns - HD // 2, 1)
            behind = pltpu.roll(turned, HD // 2, 1)
            cosine, sine = (
                jnp.concatenate([table[at]] * (columns // HD), axis=1) for table in (cosines, sines)
            )
            turned = turned * cosine + jnp.where(in_first, ahead, behind) * sine
            out[at, :rows] = turned.astype(jnp.bfloat16)
            value = values[slot * rows : (slot + 1) * rows].astype(jnp.bfloat16)
            for row in range(2):
                out[at, rows:, row * width : (row + 1) * width] = value[
                    row * rows // 2 : (row + 1) * rows // 2
                ]
        first += count


def project(where, pieces, weights, gain, cosines, sines):
    rows, depth = cosines.shape[1], weights[0].shape[2]
    columns = 4 * weights[0].shape[1] // 3
    width = columns // 2
    return pl.pallas_call(
        project_kernel,
        out_shape=jax.ShapeDtypeStruct((4, rows + rows // 2, columns), jnp.bfloat16),
        in_specs=[pl.BlockSpec(memory_space=pltpu.SMEM)]
        + [pl.BlockSpec(memory_space=pltpu.VMEM)] * 8
        + [pl.BlockSpec(memory_space=pl.ANY)] * 4
        + [pl.BlockSpec(memory_space=pltpu.VMEM)] * 3,
        out_specs=pl.BlockSpec(memory_space=pltpu.VMEM),
        scratch_shapes=[
            pltpu.VMEM((2, 2, columns, 2 * depth), jnp.bfloat16),
            pltpu.VMEM((2, 2, width, 2 * depth), jnp.bfloat16),
            pltpu.SemaphoreType.DMA((24,)),
        ],
        compiler_params=pltpu.CompilerParams(vmem_limit_bytes=VMEM_BYTES),
        cost_estimate=pl.CostEstimate(
            flops=8 * rows * 8 * depth * (columns + width),
            bytes_accessed=16_000_000,
            transcendentals=0,
        ),
        name="project",
    )(where, *pieces, *weights, gain, cosines, sines)


def attend_kernel(
    prior, held, cache, far0, far1, far2, sinks, attended, decode, window, bias, sems, out_sems
):
    pre_at = lax.axis_index("pre")
    rows, half = attended.shape[0], cache.shape[1]
    fresh, last = 2 * half, 2 * half + rows
    loads = [
        pltpu.make_async_copy(cache.at[pre_at], window.at[pl.ds(0, half)], sems.at[0]),
    ]
    start = half
    for far in (far0, far1, far2):
        count = min(far.shape[0], 2 * half - start)
        loads.append(
            pltpu.make_async_copy(
                far.at[pl.ds(0, count)], window.at[pl.ds(start, count)], sems.at[len(loads)]
            )
        )
        start += count
    for load in loads:
        load.start()
    span = 2 * HD
    heads = cache.shape[2] // span
    local = heads // 4
    for head in range(heads):
        block, at = head // local, head % local
        left = head * span
        start = (local + at) * HD
        window[fresh:last, left : left + HD] = held[block, :rows, start : start + HD]
        for row in range(2):
            start = row * local * HD + at * HD
            window[
                fresh + row * rows // 2 : fresh + (row + 1) * rows // 2, left + HD : left + span
            ] = held[block, rows:, start : start + HD]
    window[last:] = jnp.zeros((window.shape[0] - last, window.shape[1]), window.dtype)
    window[last : last + sinks.shape[0]] = sinks[...]
    tail = pltpu.make_async_copy(
        window.at[pl.ds(fresh, rows)], decode.at[pl.ds(2 * half - rows, rows)], out_sems.at[0]
    )
    tail.start()
    token = lax.broadcasted_iota(jnp.int32, (rows, 1), 0)
    lowest = jnp.maximum(token + 1, SINKS + 2 * half - prior[0])
    slot = lax.broadcasted_iota(jnp.int32, (1, half), 1)
    new = lax.broadcasted_iota(jnp.int32, (1, rows), 1)
    sink = lax.broadcasted_iota(jnp.int32, (1, window.shape[0] - last), 1)

    def shown(ok):
        return jnp.where(ok, 0.0, MASKED_SCORE)

    bias[:, :half] = shown(slot >= lowest - pre_at * half)
    bias[:, half:fresh] = shown(slot >= lowest - (1 - pre_at) * half)
    bias[:, fresh:last] = shown(new <= token)
    bias[:, last:] = jnp.broadcast_to(shown(sink < SINKS), (rows, window.shape[0] - last))
    for load in loads:
        load.wait()

    def keep(early, late):
        first = pltpu.make_async_copy(
            window.at[pl.ds(early + rows, half - rows)],
            decode.at[pl.ds(0, half - rows)],
            out_sems.at[1],
        )
        second = pltpu.make_async_copy(
            window.at[pl.ds(late, half)], decode.at[pl.ds(half - rows, half)], out_sems.at[2]
        )
        return first, second

    @pl.when(pre_at == 0)
    def _():
        for copy in keep(0, half):
            copy.start()

    @pl.when(pre_at != 0)
    def _():
        for copy in keep(half, 0):
            copy.start()

    scale = HD ** (-0.5)

    def score(head):
        block, at = head // local, head % local * HD
        left = head * span
        return lax.dot_general(
            held[block, :rows, at : at + HD],
            window[:, left : left + HD],
            NT,
            preferred_element_type=jnp.float32,
        )

    ahead = score(0)
    for head in range(heads):
        scores = ahead * scale + bias[...]
        if head + 1 < heads:
            ahead = score(head + 1)
        top = jnp.max(scores, axis=1, keepdims=True)
        probability = jnp.exp(scores - top)
        below = jnp.sum(probability, axis=1, keepdims=True)
        mixed = jnp.dot(
            probability.astype(jnp.bfloat16),
            window[:, head * span + HD : (head + 1) * span],
            preferred_element_type=jnp.float32,
        )
        attended[:, head * HD : (head + 1) * HD] = (mixed / below).astype(jnp.bfloat16)
    tail.wait()

    @pl.when(pre_at == 0)
    def _():
        for copy in keep(0, half):
            copy.wait()

    @pl.when(pre_at != 0)
    def _():
        for copy in keep(half, 0):
            copy.wait()


def attend(prior, parts, cache, fars, sinks):
    rows = 2 * parts.shape[1] // 3
    half, width = cache.shape[1:]
    keys = 2 * half + rows + 128
    return pl.pallas_call(
        attend_kernel,
        out_shape=[
            jax.ShapeDtypeStruct((rows, width // 2), jnp.bfloat16),
            jax.ShapeDtypeStruct((2 * half, width), jnp.bfloat16),
        ],
        in_specs=[
            pl.BlockSpec(memory_space=pltpu.SMEM),
            pl.BlockSpec(memory_space=pltpu.VMEM),
            pl.BlockSpec(memory_space=pl.ANY),
            pl.BlockSpec(memory_space=pl.ANY),
            pl.BlockSpec(memory_space=pl.ANY),
            pl.BlockSpec(memory_space=pl.ANY),
            pl.BlockSpec(memory_space=pltpu.VMEM),
        ],
        out_specs=[
            pl.BlockSpec(memory_space=pltpu.VMEM),
            pl.BlockSpec(memory_space=pl.ANY),
        ],
        scratch_shapes=[
            pltpu.VMEM((keys, width), jnp.bfloat16),
            pltpu.VMEM((rows, keys), jnp.float32),
            pltpu.SemaphoreType.DMA((4,)),
            pltpu.SemaphoreType.DMA((3,)),
        ],
        compiler_params=pltpu.CompilerParams(vmem_limit_bytes=VMEM_BYTES),
        cost_estimate=pl.CostEstimate(
            flops=2 * rows * keys * width,
            bytes_accessed=10_000_000,
            transcendentals=rows * keys * width // (2 * HD),
        ),
        name="attend",
    )(prior, parts, cache, *fars, sinks)


def finish_kernel(*refs):
    pieces, own, far, out = refs[:4], refs[4:8], refs[8:12], refs[12]
    core_at, match = lax.axis_index("mdl") % 2, near_half() == 0
    depth = own[0].shape[0]
    total = None
    for step, place in enumerate(mates(lax.axis_index("dec"))):
        columns = pl.ds(pl.multiple_of(lax.rem(place, 2) * depth, depth), depth)
        same = place // 2 == core_at
        own_row, far_row = (
            jnp.where(same, pieces[which][:, columns], pieces[which + 2][:, columns])
            for which in range(2)
        )
        for heads, weights in (
            (jnp.where(match, own_row, far_row), own[step]),
            (jnp.where(match, far_row, own_row), far[step]),
        ):
            term = jnp.dot(heads, weights[...], preferred_element_type=jnp.float32)
            total = term if total is None else total + term
    out[...] = total.astype(jnp.bfloat16)


def finish(pieces, own, far):
    rows, depth = pieces[0].shape
    columns = own[0].shape[1]
    return pl.pallas_call(
        finish_kernel,
        out_shape=jax.ShapeDtypeStruct((rows, columns), jnp.bfloat16),
        in_specs=[pl.BlockSpec(memory_space=pltpu.VMEM)] * 12,
        out_specs=pl.BlockSpec(memory_space=pltpu.VMEM),
        compiler_params=pltpu.CompilerParams(vmem_limit_bytes=VMEM_BYTES),
        cost_estimate=pl.CostEstimate(
            flops=8 * rows * depth * columns, bytes_accessed=7_000_000, transcendentals=0
        ),
        name="finish",
    )(*pieces, *own, *far)


def join_kernel(cache, far0, far1, out, held, sems):
    half = held.shape[1]
    part = half - far1.shape[0]
    pre_at = lax.axis_index("pre")
    loads = [
        pltpu.make_async_copy(cache.at[pre_at], held.at[0], sems.at[0]),
        pltpu.make_async_copy(
            far0.at[pl.ds(far0.shape[0] - part, part)], held.at[1, pl.ds(0, part)], sems.at[1]
        ),
        pltpu.make_async_copy(far1, held.at[1, pl.ds(part, half - part)], sems.at[4]),
    ]
    stores = [
        pltpu.make_async_copy(
            held.at[which], out.at[pl.ds(pl.multiple_of(at * half, half), half)], sems.at[2 + which]
        )
        for which, at in enumerate((pre_at, 1 - pre_at))
    ]
    for load in loads:
        load.start()
    loads[0].wait()
    stores[0].start()
    loads[1].wait()
    loads[2].wait()
    stores[1].start()
    for store in stores:
        store.wait()


def join(cache, far0, far1):
    half, width = cache.shape[1:]
    return pl.pallas_call(
        join_kernel,
        out_shape=jax.ShapeDtypeStruct((2 * half, width), jnp.bfloat16),
        in_specs=[pl.BlockSpec(memory_space=pl.ANY)] * 3,
        out_specs=pl.BlockSpec(memory_space=pl.ANY),
        scratch_shapes=[pltpu.VMEM((2, half, width), jnp.bfloat16), pltpu.SemaphoreType.DMA((5,))],
        compiler_params=pltpu.CompilerParams(vmem_limit_bytes=VMEM_BYTES),
        cost_estimate=pl.CostEstimate(
            flops=0, bytes_accessed=8 * half * width, transcendentals=0
        ),
        name="join",
    )(cache, far0, far1)


def split_body(sizes, tokens, norm_gain, w_qkv, w_out, sink_cache, cache_a, cache_b, lengths, groups):
    dec = sizes["dec"]
    rows = tokens.shape[2]
    pre_at, dec_at, mdl_at = (lax.axis_index(name) for name in ("pre", "dec", "mdl"))
    swap = [(0, 1), (1, 0)]
    over_y = [(0, 2), (1, 3), (2, 0), (3, 1)]
    over_core = [(0, 1), (1, 0), (2, 3), (3, 2)]

    def along(step):
        return [(at, (at + step) % dec) for at in range(dec)]

    sent_a, sent_b = (
        lax.dynamic_index_in_dim(cache[:, 0], 1 - pre_at, 0, keepdims=False)
        for cache in (cache_a, cache_b)
    )
    own = tokens.reshape(rows, -1)
    gain = norm_gain.astype(jnp.float32).reshape(sizes["mdl"], 1, -1)

    turned = jnp.transpose(w_qkv, (1, 2, 0)).reshape(3, dec, -1, w_qkv.shape[0])
    turned = jnp.transpose(turned, (1, 0, 2, 3)).reshape(dec, -1, w_qkv.shape[0])
    split = turned.shape[1] // 2
    pairs = [(0, 1), (1, 0), (2, 3), (3, 2)]
    middle = [(1, 2), (2, 1)]
    outward = [(1, 0), (2, 3)]
    in_middle = (dec_at == 1) | (dec_at == 2)

    def over_cores(*values):
        return [lax.ppermute(value, "mdl", over_core) for value in values]

    def pick(middle_got, outer_got):
        return jnp.where(in_middle, middle_got, outer_got)

    where = jnp.stack(mates(dec_at)).astype(jnp.int32)
    cosines, sines = angles(lengths[pre_at], rows)
    cosines, sines = cosines[:, :, 0], sines[:, :, 0]
    cosines = jnp.concatenate([cosines, cosines], axis=-1)
    sines = jnp.concatenate([-sines, sines], axis=-1)
    sinks = jnp.pad(
        lax.dynamic_index_in_dim(sink_cache, groups[pre_at, dec_at], 0, keepdims=False),
        ((0, 16 - SINKS), (0, 0)),
    )
    prior = lengths[pre_at, dec_at].reshape(1)

    edges = lax.optimization_barrier
    half, most = sent_a.shape[0] // 16 * 11, sent_a.shape[0] // 4 * 3
    mate = lax.ppermute(own, "dec", pairs)
    inner = lax.ppermute(own, "dec", middle)
    y_own = lax.ppermute(own, "mdl", over_y)
    o_far = lax.ppermute(w_out, "pre", swap)
    mate, inner, y_own, first_w, early_a = edges((mate, inner, y_own, turned[:, :split], sent_a[:half]))
    o_far, early_a = edges((o_far, early_a))
    first_w = lax.all_to_all(first_w, "dec", 0, 0, tiled=True)
    inner_mate = lax.ppermute(mate, "dec", middle)
    outer = lax.ppermute(inner, "dec", outward)
    y_mate = lax.ppermute(mate, "mdl", over_y)
    far_a0 = lax.ppermute(early_a, "pre", swap)
    core_own = over_cores(own, y_own)
    first_w, inner_mate, outer, y_mate, far_a0, early_a, second_w, late_o, *tables = edges(
        (first_w, inner_mate, outer, y_mate, far_a0, sent_a[half:most], turned[:, split:], w_out, where, prior, cosines, sines, sinks)
    )
    where, prior, cosines, sines, sinks = tables
    second_w = lax.all_to_all(second_w, "dec", 0, 0, tiled=True)
    third = pick(inner, outer)
    outer_mate = lax.ppermute(inner_mate, "dec", outward)
    y_third = lax.ppermute(third, "mdl", over_y)
    far_first = lax.ppermute(first_w, "pre", swap)
    far_a1 = lax.ppermute(early_a, "pre", swap)
    core_mate = over_cores(mate, y_mate)
    second_w, outer_mate, y_third, far_first, far_a1, late_o = edges(
        (second_w, outer_mate, y_third, far_first, far_a1, late_o)
    )
    far_second = lax.ppermute(second_w, "pre", swap)
    fourth = pick(inner_mate, outer_mate)
    y_fourth = lax.ppermute(fourth, "mdl", over_y)
    *core_third, late_o = edges((*over_cores(third, y_third), late_o))
    o_mate = lax.ppermute(late_o, "dec", pairs)
    o_inner = lax.ppermute(late_o, "dec", middle)
    near = list(zip(core_own, core_mate, core_third))
    pieces = norm(3, [own, mate, third, y_own, y_mate, y_third, *near[0], *near[1]], gain)
    quarter = sent_b.shape[0] // 4
    late_ab = jnp.concatenate([sent_a[most:], sent_b[:quarter]], axis=0)
    pieces = [*pieces, fourth, y_fourth, *over_cores(fourth, y_fourth)]
    far_second, late_ab, late_b, *pieces = edges((far_second, late_ab, sent_b[quarter:], *pieces))
    far_ab = lax.ppermute(late_ab, "pre", swap)
    o_outer = lax.ppermute(o_inner, "dec", outward)
    o_inner_mate = lax.ppermute(o_mate, "dec", middle)
    weights = [first_w, far_first, second_w, far_second]

    found = project(where, pieces, weights, gain, cosines, sines)
    found, far_ab, o_outer, o_inner_mate, late_b = edges(
        (found, far_ab, o_outer, o_inner_mate, late_b)
    )
    parts = lax.all_to_all(found, "dec", 0, 0, tiled=True)
    far_b1 = lax.ppermute(late_b, "pre", swap)
    parts, far_b1 = edges((parts, far_b1))
    o_third = pick(o_inner, o_outer)
    o_far_third = lax.ppermute(o_third, "pre", swap)
    o_outer_mate = lax.ppermute(o_inner_mate, "dec", outward)
    attended, decode_a = attend(prior, parts, cache_a[:, 0], (far_a0, far_a1, far_ab), sinks)
    attended, o_far_third, o_outer_mate, o_far = edges((attended, o_far_third, o_outer_mate, o_far))
    o_fourth = pick(o_inner_mate, o_outer_mate)
    o_far_fourth = lax.ppermute(o_fourth, "pre", swap)
    o_far_mate = lax.ppermute(o_far, "dec", pairs)
    second = lax.ppermute(attended, "mdl", over_y)
    shares = [
        attended,
        second,
        lax.ppermute(attended, "mdl", over_core),
        lax.ppermute(second, "mdl", over_core),
    ]
    attn_out = finish(
        shares,
        [w_out, o_mate, o_third, o_fourth],
        [o_far, o_far_mate, o_far_third, o_far_fourth],
    )
    decode_b = join(cache_b[:, 0], far_ab, far_b1)
    return (attn_out[None, None], decode_a[None, None], decode_b[None, None])


def body(sizes, tokens, norm_gain, w_qkv, w_out, sink_cache, cache_a, cache_b, lengths, groups):
    heads_dev = cache_a.shape[-1] // (2 * HD)
    shapes = (sizes["pre"], sizes["mdl"], sizes["dec"], heads_dev)
    split = shapes == (2, 4, 4, 8) and tokens.shape[0] == 1 and tokens.shape[1] == 1
    args = (tokens, norm_gain, w_qkv, w_out, sink_cache, cache_a, cache_b, lengths, groups)
    return split_body(sizes, *args) if split else general_body(*args)


def solution(mesh):
    placed = (
        P("pre", "dec", None, "mdl"),
        P(),
        P(("pre", "dec"), None, "mdl"),
        P(("pre", "dec"), "mdl"),
        P(None, None, "mdl"),
        P(None, "dec", "pre", "mdl"),
        P(None, "dec", "pre", "mdl"),
        P(),
        P(),
    )
    return jax.shard_map(
        functools.partial(body, dict(mesh.shape)),
        mesh=mesh,
        in_specs=placed,
        out_specs=(
            P("pre", "dec", None, "mdl"),
            P("pre", "dec", None, "mdl"),
            P("pre", "dec", None, "mdl"),
        ),
        check_vma=False,
    )
```
